32 devices in a mesh: rep: 4 (over y, x), inner: 8 (over z, core).
Axes of the slice: x: 2, y: 2, z: 4, core: 2. Of those that a mesh axis runs over, the one named last changes fastest.
Arguments:
- tokens: bfloat16 [4096, 1024], P(('rep', 'inner')), may hold values from -6 to 6
- cotangent: bfloat16 [4096, 1024], P(('rep', 'inner')), may hold values from -6 to 6
- qkv_weight: bfloat16 [1024, 3072], P('inner'), may hold values from -0.1875 to 0.1875
- out_weight: bfloat16 [1024, 1024], P('inner'), may hold values from -3.5 to 3.5
- in_weight: bfloat16 [1024, 5248], P('inner'), may hold values from -0.1875 to 0.1875
- down_weight: bfloat16 [2624, 1024], P('inner'), may hold values from -0.125 to 0.125
- gain_one: bfloat16 [1024], P('inner'), may hold values from 0.5 to 1.5
- gain_two: bfloat16 [1024], P('inner'), may hold values from 0.5 to 1.5
Outputs:
- layer_out: bfloat16 [4096, 1024], P(('rep', 'inner'))
- input_grad: bfloat16 [4096, 1024], P(('rep', 'inner'))
- qkv_grad: float32 [1024, 3072], P('inner')
- out_grad: float32 [1024, 1024], P('inner')
- in_grad: float32 [1024, 5248], P('inner')
- down_grad: float32 [2624, 1024], P('inner')
- gain_one_grad: float32 [1024], P('inner')
- gain_two_grad: float32 [1024], P('inner')
The draws below stay inside these ranges and needn't reach their ends.
All inputs are finite; a program needn't handle non-finite values.
Results may differ from the reference program's by a relative error of at most 0.023.
Values may be sent and summed in bfloat16 or wider, within the bound.
No kernel may reach another device: no remote copies, remote signals or barrier semaphores. Data moves between devices by JAX's collectives and lax.ppermute only.
A program may use at most 256 MiB of HBM per device.

```python
import jax
import jax.numpy as jnp
from jax import lax

D = 1024
HEAD_DIM = 64
FF = 2624
SEQ_LEN = 1024
TOKENS = 4096
N_REP = 4


def steps_of(rng, extent, split, low, high):
    level, own = 1.0, jax.random.fold_in(rng, 6)
    for dim, parts in split:
        draws = jnp.exp(jax.random.uniform(jax.random.fold_in(own, dim), (parts,), jnp.float32, low / len(split), high / len(split)))
        level = level * jnp.repeat(draws, extent[dim] // parts).reshape([-1 if axis == dim else 1 for axis in range(len(extent))])
    return level


def normal_values(key, dims, deviation, bound, split=(), kind=jnp.bfloat16):
    factor_of = steps_of(key, dims, split, -0.22, 0.18) if split else 1.0
    values = jax.random.normal(key, dims, jnp.float32) * deviation * factor_of
    return jnp.minimum(jnp.maximum(values, -bound), bound).astype(kind)


def setup_inputs(seed: int = 0) -> dict:
    arg_keys = jax.random.split(jax.random.key(seed), 9)
    return {
        "tokens": normal_values(arg_keys[0], (TOKENS, D), 1.0, 6.0, ((0, 32),)),
        "cotangent": normal_values(arg_keys[1], (TOKENS, D), 1.0, 6.0, ((0, 32),)),
        "qkv_weight": normal_values(arg_keys[2], (D, 3 * D), D ** -0.5, 0.1875, ((0, 8),)),
        "out_weight": normal_values(arg_keys[3], (D, D), (max(1, 3 * D // SEQ_LEN)) ** -0.5, 3.5, ((0, 8),)),
        "in_weight": normal_values(arg_keys[4], (D, 2 * FF), D ** -0.5, 0.1875, ((0, 8),)),
        "down_weight": normal_values(arg_keys[5], (FF, D), FF ** -0.5, 0.125, ((0, 8),)),
        "gain_one": jnp.clip(1.0 + 0.1 * jax.random.normal(arg_keys[6], (D,), jnp.float32), 0.5, 1.5).astype(jnp.bfloat16),
        "gain_two": jnp.clip(1.0 + 0.1 * jax.random.normal(arg_keys[7], (D,), jnp.float32), 0.5, 1.5).astype(jnp.bfloat16),
    }


@jax.custom_vjp
def low(v):
    return lax.optimization_barrier(v.astype(jnp.bfloat16)).astype(jnp.float32)

@jax.custom_vjp
def low_back(v):
    return v

def low_keep(v):
    return (low(v), None)

def low_pass(kept, grad):
    return (grad,)

def back_keep(v):
    return (v, None)

def back_low(kept, grad):
    return (low(grad),)
low.defvjp(low_keep, low_pass)
low_back.defvjp(back_keep, back_low)
EPSILON = 1e-05
THETA = 160000.0
HIGH = lax.Precision.HIGHEST

def norm_rows(values, gain_row):
    centred = values - lax.optimization_barrier(jnp.mean(values, axis=-1, keepdims=True))
    inv_scale = lax.rsqrt(lax.optimization_barrier(jnp.mean(centred * centred, axis=-1, keepdims=True)) + EPSILON)
    return centred * inv_scale * gain_row

def rotate(values, cos_table, sine_table):
    half_width = values.shape[-1] // 2
    first_half = values[..., :half_width]
    second_half = values[..., half_width:]
    return jnp.concatenate([first_half * cos_table - second_half * sine_table, second_half * cos_table + first_half * sine_table], axis=-1)

def attend_block(query_block, all_keys, all_values, score_scale):
    scores = jnp.einsum('qhd,khd->hqk', query_block, all_keys, precision=HIGH) * score_scale
    scores = low_back(scores)
    weights = low(jax.nn.softmax(scores, axis=-1))
    return jnp.einsum('hqk,khd->qhd', weights, all_values, precision=HIGH)

def layer(inputs, w_qkv, w_out, w_in, w_down, gain_one, gain_two, cos_table, sine_table):
    seq_count = inputs.shape[0]
    model_width = inputs.shape[1]
    head_count = model_width // HEAD_DIM
    score_scale = HEAD_DIM ** (-0.5)
    normed_one = low(norm_rows(inputs, gain_one))
    projected = low_back(jnp.dot(normed_one, w_qkv, precision=HIGH))
    query_heads = low(rotate(projected[:, :model_width].reshape(seq_count, head_count, HEAD_DIM), cos_table, sine_table))
    key_heads = low(rotate(projected[:, model_width:2 * model_width].reshape(seq_count, head_count, HEAD_DIM), cos_table, sine_table))
    value_heads = low(projected[:, 2 * model_width:].reshape(seq_count, head_count, HEAD_DIM))
    block_count = max(1, seq_count // 512)
    block_rows = seq_count // block_count
    query_blocks = query_heads.reshape(block_count, block_rows, head_count, HEAD_DIM)
    attend = jax.checkpoint(lambda query_block: attend_block(query_block, key_heads, value_heads, score_scale))
    attended = lax.map(attend, query_blocks).reshape(seq_count, model_width)
    attended = low(low_back(attended))
    middle = inputs + low_back(jnp.dot(attended, w_out, precision=HIGH))
    normed_two = low(norm_rows(middle, gain_two))
    hidden = low_back(jnp.dot(normed_two, w_in, precision=HIGH))
    half_width = hidden.shape[1] // 2
    gated = low(jax.nn.gelu(hidden[:, :half_width], approximate=False) * hidden[:, half_width:])
    return middle + jnp.dot(gated, w_down, precision=HIGH)

def reference(tokens, cotangent, qkv_weight, out_weight, in_weight, down_weight, gain_one, gain_two):
    seq_count = SEQ_LEN
    tok_place = jnp.arange(seq_count, dtype=jnp.int32).astype(jnp.float32)
    inv_freq = 1.0 / THETA ** (jnp.arange(HEAD_DIM // 2, dtype=jnp.float32) * (2.0 / HEAD_DIM))
    tok_angle = tok_place[:, None] * inv_freq[None, :]
    cos_table = jnp.cos(tok_angle)[:, None, :]
    sine_table = jnp.sin(tok_angle)[:, None, :]

    def forward(inputs, w_qkv, w_out, w_in, w_down, first_gain, second_gain):
        sequences = inputs.reshape(N_REP, seq_count, inputs.shape[1])
        one_seq = jax.checkpoint(lambda seq_rows: layer(seq_rows, w_qkv, w_out, w_in, w_down, first_gain, second_gain, cos_table, sine_table))
        return lax.map(one_seq, sequences).reshape(inputs.shape)
    layer_out, pull_back = jax.vjp(forward, tokens.astype(jnp.float32), qkv_weight.astype(jnp.float32), out_weight.astype(jnp.float32), in_weight.astype(jnp.float32), down_weight.astype(jnp.float32), gain_one.astype(jnp.float32), gain_two.astype(jnp.float32))
    grads = pull_back(cotangent.astype(jnp.float32))
    return (layer_out.astype(jnp.bfloat16), grads[0].astype(jnp.bfloat16), grads[1], grads[2], grads[3], grads[4], grads[5], grads[6])
```

```python
import functools

import jax
import jax.numpy as jnp
from jax import lax
from jax.experimental import pallas as pl
from jax.experimental.pallas import tpu as pltpu
from jax.sharding import PartitionSpec as P

HEAD_DIM = 64
EPSILON = 1e-05
THETA = 160000.0
F32 = jnp.float32
BF16 = jnp.bfloat16
NT = (((1,), (1,)), ((), ()))
TN = (((0,), (0,)), ((), ()))
VMEM_LIMIT = 56 * 1024 * 1024


def dot(a, b):
    return jnp.dot(a, b, preferred_element_type=F32)


def dot_nt(a, b):
    return lax.dot_general(a, b, NT, preferred_element_type=F32)


def dot_tn(a, b):
    return lax.dot_general(a, b, TN, preferred_element_type=F32)


def call(body, outs, args, scratch=(), n_smem=0):
    in_specs = [pl.BlockSpec(memory_space=pltpu.SMEM)] * n_smem + [
        pl.BlockSpec(memory_space=pltpu.VMEM)
    ] * (len(args) - n_smem)
    return pl.pallas_call(
        body,
        out_shape=[jax.ShapeDtypeStruct(s, d) for s, d in outs],
        in_specs=in_specs,
        out_specs=[pl.BlockSpec(memory_space=pltpu.VMEM)] * len(outs),
        scratch_shapes=[pltpu.VMEM(s, d) for s, d in scratch],
        compiler_params=pltpu.CompilerParams(vmem_limit_bytes=VMEM_LIMIT),
    )(*args)


def hat_of(values):
    centred = values - jnp.mean(values, axis=-1, keepdims=True)
    inv = lax.rsqrt(jnp.mean(centred * centred, axis=-1, keepdims=True) + EPSILON)
    return centred * inv, inv


def partner(x):
    width = x.shape[-1]
    half = HEAD_DIM // 2
    lane = lax.broadcasted_iota(jnp.int32, x.shape, x.ndim - 1)
    ahead = pltpu.roll(x, width - half, 1)
    behind = pltpu.roll(x, half, 1)
    return jnp.where(lane % HEAD_DIM < half, ahead, behind)


def tile_lanes(table, width):
    return jnp.concatenate([table] * (width // table.shape[-1]), axis=-1)


def head_mask(h, width):
    lane = lax.broadcasted_iota(jnp.int32, (1, width), 1)
    return ((lane >= h * HEAD_DIM) & (lane < (h + 1) * HEAD_DIM)).astype(BF16)


def qkv_kernel(n_rep, refs_x, w_ref, g_ref, cos_ref, sin_ref, q_ref, kv_ref, a_ref):
    rows = refs_x[0].shape[0]
    for m in range(n_rep):
        hat, _ = hat_of(refs_x[m][...].astype(F32))
        a_ref[m * rows : (m + 1) * rows, :] = (hat * g_ref[...]).astype(BF16)
    width = q_ref.shape[1]
    step = 2 * rows if n_rep % 2 == 0 else rows
    for r0 in range(0, n_rep * rows, step):
        sl = slice(r0, r0 + step)
        proj = dot(a_ref[sl, :], w_ref[...])
        cos = tile_lanes(cos_ref[sl, :], width)
        sin = tile_lanes(sin_ref[sl, :], width)
        query = proj[:, :width]
        key = proj[:, width : 2 * width]
        q_ref[sl, :] = ((query * cos + partner(query) * sin).astype(BF16).astype(F32) * HEAD_DIM**-0.5).astype(BF16)
        kv_ref[sl, :width] = (key * cos + partner(key) * sin).astype(BF16)
        kv_ref[sl, width:] = proj[:, 2 * width :].astype(BF16)


def attend_kernel(n_part, q_ref, refs_kv, o_ref, lse_ref, k_scr, vt_scr):
    rows, width = q_ref.shape
    keys = refs_kv[0].shape[0]
    for l in range(n_part):
        k_scr[l * keys : (l + 1) * keys, :] = refs_kv[l][:, :width]
        vt_scr[:, l * keys : (l + 1) * keys] = refs_kv[l][:, width:].astype(F32).T.astype(BF16)
    heads = width // HEAD_DIM
    step = min(256, rows)

    def body(c, carry):
        r0 = pl.multiple_of(c * step, step)
        for h in range(heads):
            pair = h // 2 * 128
            q = q_ref[pl.ds(r0, step), pair : pair + 128] * head_mask(h % 2, 128)
            s = dot_nt(k_scr[:, pair : pair + 128], q)
            top = jnp.max(s, axis=0, keepdims=True)
            e = jnp.exp(s - top)
            mass = jnp.sum(e, axis=0, keepdims=True)
            lse_ref[h : h + 1, pl.ds(r0, step)] = top + jnp.log(mass)
            ot = dot(vt_scr[h * HEAD_DIM : (h + 1) * HEAD_DIM, :], e.astype(BF16)) / mass
            ot_list.append(ot)
            if h % 2 == 1:
                both = jnp.concatenate(ot_list, axis=0)
                o_ref[pl.ds(r0, step), pair : pair + 128] = both.T.astype(BF16)
                ot_list.clear()
        return carry

    ot_list = []
    lax.fori_loop(0, rows // step, body, 0)


def ff_kernel(
    n_rep, sub_j, refs_x, refs_o, wout_ref, win_ref, wdown_ref, refs_c, g_ref,
    r_ref, a_ref, m_ref, du_ref, c_ref, o_ref, da_ref, gain_ref, hat_scr, u_scr, dm_scr,
):
    rows = refs_x[0].shape[0]
    total = n_rep * rows
    quarter = refs_o[0].shape[1]
    j = sub_j[0]
    for m in range(n_rep):
        hat_scr[m * rows : (m + 1) * rows, :] = refs_x[m][...].astype(F32)
        c_ref[m * rows : (m + 1) * rows, :] = refs_c[m][...]
    for m in range(n_rep):
        start = pl.multiple_of((j ^ m) * quarter, quarter)
        for k in range(n_rep):
            at = (k ^ m) * rows
            o_ref[k * rows : (k + 1) * rows, pl.ds(start, quarter)] = refs_o[m][at : at + rows, :]
    hat_scr[...] += dot(o_ref[...], wout_ref[...])
    r_ref[...] = hat_scr[:rows, :]

    def norm_step(c, carry):
        r0 = pl.multiple_of(c * 64, 64)
        hat, _ = hat_of(hat_scr[pl.ds(r0, 64), :])
        hat_scr[pl.ds(r0, 64), :] = hat
        a_ref[pl.ds(r0, 64), :] = (hat * g_ref[...]).astype(BF16)
        return carry

    lax.fori_loop(0, total // 64, norm_step, 0)
    u_scr[...] = dot(a_ref[...], win_ref[...])
    dm_scr[...] = dot_nt(c_ref[...], wdown_ref[...])
    width = m_ref.shape[1]

    def gate_step(c, carry):
        r0 = pl.multiple_of(c * 32, 32)
        sl = pl.ds(r0, 32)
        pre = u_scr[sl, :width]
        gate = u_scr[sl, width:]
        dm = dm_scr[sl, :]
        cdf = 0.5 * (1.0 + lax.erf(pre * (0.5**0.5)))
        pdf = jnp.exp(-0.5 * pre * pre) * 0.3989422804014327
        act = pre * cdf
        m_ref[sl, :] = (act * gate).astype(BF16)
        du_ref[sl, :width] = (dm * gate * (cdf + pre * pdf)).astype(BF16)
        du_ref[sl, width:] = (dm * act).astype(BF16)
        return carry

    lax.fori_loop(0, total // 32, gate_step, 0)
    da = dot_nt(du_ref[...], win_ref[...])
    da_ref[...] = da.astype(BF16)
    gain_ref[...] = jnp.sum(da * hat_scr[...], axis=0, keepdims=True)


def ff_grads_kernel(m_ref, wdown_ref, c_ref, a_ref, du_ref, lo_ref, din_ref, ddown_ref):
    lo_ref[...] = dot(m_ref[...], wdown_ref[...]).astype(BF16)
    din_ref[...] = dot_tn(a_ref[...], du_ref[...]).astype(BF16)
    ddown_ref[...] = dot_tn(m_ref[...], c_ref[...]).astype(BF16)


def norm_back(values, gain, grad):
    hat, inv = hat_of(values)
    dhat = grad * gain
    return inv * (
        dhat
        - jnp.mean(dhat, axis=-1, keepdims=True)
        - hat * jnp.mean(dhat * hat, axis=-1, keepdims=True)
    )


def middle_kernel(n_rep, refs_da, r_ref, c_ref, g_ref, dr_ref, dz_ref):
    rows = r_ref.shape[0]
    grad = refs_da[0][:rows, :].astype(F32)
    for m in range(1, n_rep):
        grad = grad + refs_da[m][...].astype(F32)
    dr = c_ref[...].astype(F32) + norm_back(r_ref[...], g_ref[...], grad)
    dr_ref[...] = dr
    dz_ref[...] = dr.astype(BF16)


def attend_back_kernel(
    n_rep, n_part, sub_j, refs_dz, wout_ref, o_ref, q_ref, refs_kv, lse_ref, cos_ref, sin_ref,
    dq_ref, dkv_ref, refs_send, dz_ref, do_scr, k_scr, v_scr, kt_scr, delta_scr, dk_scr, dv_scr,
):
    rows, width = q_ref.shape
    keys = refs_kv[0].shape[0]
    part = refs_dz[0].shape[0]
    j = sub_j[0]
    for m in range(n_rep):
        dz_ref[m * part : (m + 1) * part, :] = refs_dz[m][...]
    start = pl.multiple_of(j * width, width)
    dout = dot_nt(dz_ref[...], wout_ref[pl.ds(start, width), :]).astype(BF16)
    do_scr[...] = dout
    prod_t = (dout.astype(F32) * o_ref[...].astype(F32)).T
    heads = width // HEAD_DIM
    for h in range(heads):
        delta_scr[h : h + 1, :] = jnp.sum(
            prod_t[h * HEAD_DIM : (h + 1) * HEAD_DIM, :], axis=0, keepdims=True
        )
    for l in range(n_part):
        sl = slice(l * keys, (l + 1) * keys)
        k_scr[sl, :] = refs_kv[l][:, :width]
        v_scr[sl, :] = refs_kv[l][:, width:]
        kt_scr[:, sl] = refs_kv[l][:, :width].astype(F32).T.astype(BF16)
    dk_scr[...] = jnp.zeros_like(dk_scr)
    dv_scr[...] = jnp.zeros_like(dv_scr)
    step = min(256, rows)

    def body(c, carry):
        r0 = pl.multiple_of(c * step, step)
        for h in range(heads):
            pair = h // 2 * 128
            lanes = slice(pair, pair + 128)
            mask = head_mask(h % 2, 128)
            q = q_ref[pl.ds(r0, step), lanes] * mask
            do = do_scr[pl.ds(r0, step), lanes] * mask
            p = jnp.exp(dot_nt(k_scr[:, lanes], q) - lse_ref[h : h + 1, pl.ds(r0, step)])
            dp = dot_nt(v_scr[:, lanes], do)
            ds = (p * (dp - delta_scr[h : h + 1, pl.ds(r0, step)])).astype(BF16)
            dv_scr[:, lanes] += dot(p.astype(BF16), do)
            dk_scr[:, lanes] += dot(ds, q)
            dq_list.append(dot(kt_scr[h * HEAD_DIM : (h + 1) * HEAD_DIM, :], ds))
            if h % 2 == 1:
                dq = jnp.concatenate(dq_list, axis=0).T * HEAD_DIM**-0.5
                dq_list.clear()
                cos = cos_ref[pl.ds(r0, step), :]
                sin = sin_ref[pl.ds(r0, step), :]
                dq_ref[pl.ds(r0, step), lanes] = (dq * cos - partner(dq) * sin).astype(BF16)
        return carry

    dq_list = []
    lax.fori_loop(0, rows // step, body, 0)
    dkv_ref[:, :width] = dk_scr[:keys, :]
    dkv_ref[:, width:] = dv_scr[:keys, :]
    for l in range(1, n_part):
        sl = slice(l * keys, (l + 1) * keys)
        refs_send[l - 1][:, :width] = dk_scr[sl, :].astype(BF16)
        refs_send[l - 1][:, width:] = dv_scr[sl, :].astype(BF16)


def out_grad_kernel(sub_j, o_ref, dz_ref, dout_ref):
    quarter = dout_ref.shape[1]
    cols = dz_ref[:, pl.ds(pl.multiple_of(sub_j[0] * quarter, quarter), quarter)]
    dout_ref[...] = dot_tn(o_ref[...], cols).astype(BF16)


def qkv_back_kernel(
    n_rep, n_part, dq_ref, dkv_ref, refs_got, cos_ref, sin_ref, a_ref, w_ref, refs_x,
    dqkv_ref, da_ref, gain_ref, dp_scr,
):
    width = dq_ref.shape[1]
    part = refs_x[0].shape[0]
    dkv = dkv_ref[...]
    for l in range(n_part - 1):
        dkv = dkv + refs_got[l][...].astype(F32)
    dk = dkv[:, :width]
    cos = tile_lanes(cos_ref[...], width)
    sin = tile_lanes(sin_ref[...], width)
    dp_scr[:, :width] = dq_ref[...]
    dp_scr[:, width : 2 * width] = (dk * cos - partner(dk) * sin).astype(BF16)
    dp_scr[:, 2 * width :] = dkv[:, width:].astype(BF16)
    dqkv_ref[...] = dot_tn(a_ref[...], dp_scr[...]).astype(BF16)
    gain = jnp.zeros(gain_ref.shape, F32)
    da = dot_nt(dp_scr[...], w_ref[...])
    da_ref[...] = da.astype(BF16)
    for m in range(n_rep):
        hat, _ = hat_of(refs_x[m][...].astype(F32))
        gain = gain + jnp.sum(da[m * part : (m + 1) * part, :] * hat, axis=0, keepdims=True)
    gain_ref[...] = gain


def last_kernel(n_rep, refs_da, x_ref, dr_ref, g_ref, out_ref):
    rows = x_ref.shape[0]
    grad = refs_da[0][:rows, :].astype(F32)
    for m in range(1, n_rep):
        grad = grad + refs_da[m][...].astype(F32)
    out_ref[...] = (dr_ref[...] + norm_back(x_ref[...].astype(F32), g_ref[...], grad)).astype(BF16)


def split_refs(counts, refs):
    out, at = [], 0
    for n in counts:
        if n is None:
            out.append(refs[at])
            at += 1
        else:
            out.append(list(refs[at : at + n]))
            at += n
    return out


def grouped(kernel, static, counts):
    def body(*refs):
        kernel(*static, *split_refs(counts, refs))

    return body


def on_device(
    n_rep, n_inner,
    tokens, cotangent, qkv_weight, out_weight, in_weight, down_weight, gain_one, gain_two,
):
    part = n_inner // n_rep
    rows, dim = tokens.shape
    sub = rows // n_rep
    w_rows = qkv_weight.shape[0]
    width = dim // n_rep
    ff_shard = down_weight.shape[0]
    unit = -(-ff_shard // n_rep)
    pitch = -(-unit // 16) * 16
    ff = pitch * n_inner
    total = n_rep * rows
    j = lax.axis_index("rep")
    i = lax.axis_index("inner")
    s = i // part
    t = i % part
    j_arr = jnp.reshape(j, (1,)).astype(jnp.int32)

    def rep_swap(x, m):
        return lax.ppermute(x, "rep", [(a, a ^ m) for a in range(n_rep)])

    def plane_swap(x, m):
        pairs = [(a * part + b, (a ^ m) * part + b) for a in range(n_rep) for b in range(part)]
        return lax.ppermute(x, "inner", pairs)

    def part_swap(x, l):
        pairs = [(a * part + b, a * part + (b ^ l)) for a in range(n_rep) for b in range(part)]
        return lax.ppermute(x, "inner", pairs)

    def rep_gather(x):
        return [x] + [rep_swap(x, m) for m in range(1, n_rep)]

    def block(x, index, size):
        return lax.dynamic_slice_in_dim(x, index * size, size, 0)

    def to_plane(x):
        got = [block(x, j, sub)] + [rep_swap(block(x, j ^ m, sub), m) for m in range(1, n_rep)]
        stack = jnp.concatenate(got, axis=0)
        pieces = [block(stack, s ^ j, sub)]
        for m in range(1, n_rep):
            pieces.append(plane_swap(block(stack, s ^ m ^ j, sub), m))
        return jnp.concatenate(pieces, axis=0)

    def from_plane(x):
        got = []
        for k in range(n_rep):
            pairs = []
            for a in range(n_rep):
                for z in range(n_rep):
                    for b in range(part):
                        pairs.append((a * n_inner + z * part + b, z * n_inner + (a ^ k) * part + b))
            got.append(lax.ppermute(block(x, s ^ j ^ k, sub), ("rep", "inner"), pairs))
        stack = jnp.concatenate(got, axis=0)
        return jnp.concatenate([block(stack, s ^ a, sub) for a in range(n_rep)], axis=0)

    w_qkv_own = jnp.concatenate(
        [lax.dynamic_slice_in_dim(qkv_weight, p * dim + j * width, width, 1) for p in range(3)], axis=1
    )
    halves = jnp.pad(in_weight.reshape(w_rows, 2 * n_inner, ff_shard), ((0, 0), (0, 0), (0, unit * n_rep - ff_shard)))
    w_in_own = lax.dynamic_slice_in_dim(halves, j * unit, unit, 2)
    w_in_own = jnp.pad(w_in_own, ((0, 0), (0, 0), (0, pitch - unit))).reshape(w_rows, 2 * ff)
    w_down_own = lax.dynamic_slice_in_dim(jnp.pad(down_weight, ((0, unit * n_rep - ff_shard), (0, 0))), j * unit, unit, 0)
    w_down_own = jnp.pad(w_down_own, ((0, pitch - unit), (0, 0)))
    w_qkv = lax.all_gather(w_qkv_own, "inner", axis=0, tiled=True)
    w_out = lax.all_gather(out_weight, "inner", axis=0, tiled=True)
    w_down = lax.all_gather(w_down_own, "inner", axis=0, tiled=True)
    w_in = lax.all_gather(w_in_own, "inner", axis=0, tiled=True)
    gains = lax.all_gather(jnp.concatenate([gain_one, gain_two])[None], "inner", axis=0, tiled=True)
    first_gain = gains[:, :w_rows].reshape(1, dim).astype(F32)
    second_gain = gains[:, w_rows:].reshape(1, dim).astype(F32)

    order = jnp.arange(total, dtype=jnp.int32)
    place = (
        ((s ^ (order // sub % n_rep)) * part + t) * rows + (j ^ (order // rows)) * sub + order % sub
    ).astype(F32)
    inv_freq = 1.0 / THETA ** (jnp.arange(HEAD_DIM // 2, dtype=F32) * (2.0 / HEAD_DIM))
    angle = place[:, None] * inv_freq[None, :]
    cos_half, sin_half = jnp.cos(angle), jnp.sin(angle)
    cos = jnp.concatenate([cos_half] * 4, axis=1)
    sin = jnp.concatenate([-sin_half, sin_half] * 2, axis=1)

    xs = rep_gather(to_plane(tokens))
    q, kv, a_one = call(
        grouped(qkv_kernel, (n_rep,), (n_rep,) + (None,) * 7),
        [((total, width), BF16), ((total, 2 * width), BF16), ((total, dim), BF16)],
        [*xs, w_qkv, first_gain, cos, sin],
    )
    kvs = [kv] + [part_swap(kv, l) for l in range(1, part)]
    heads = width // HEAD_DIM
    stat_rows = -(-heads // 8) * 8
    o, lse = call(
        grouped(attend_kernel, (part,), (None, part) + (None,) * 4),
        [((total, width), BF16), ((stat_rows, total), F32)],
        [q, *kvs],
        [((total * part, width), BF16), ((width, total * part), BF16)],
    )
    os_ = rep_gather(o)
    c_own = to_plane(cotangent)
    cs = rep_gather(c_own)
    r_own, a_two, gated, d_hidden, c_all, o_all, da_two, gain_two_part = call(
        grouped(ff_kernel, (n_rep,), (None, n_rep, n_rep, None, None, None, n_rep) + (None,) * 12),
        [
            ((rows, dim), F32), ((total, dim), BF16), ((total, ff), BF16), ((total, 2 * ff), BF16),
            ((total, dim), BF16), ((total, dim), BF16), ((total, dim), BF16), ((1, dim), F32),
        ],
        [j_arr, *xs, *os_, w_out, w_in, w_down, *cs, second_gain],
        [((total, dim), F32), ((total, 2 * ff), F32), ((total, ff), F32)],
        n_smem=1,
    )
    das = [da_two] + [rep_swap(da_two[m * rows : (m + 1) * rows], m) for m in range(1, n_rep)]
    lo, d_in, d_down = call(
        ff_grads_kernel,
        [((total, dim), BF16), ((dim, 2 * ff), BF16), ((ff, dim), BF16)],
        [gated, w_down, c_all, a_two, d_hidden],
    )
    d_in = lax.psum_scatter(d_in, "inner", scatter_dimension=0, tiled=True)
    d_down = lax.psum_scatter(d_down, "inner", scatter_dimension=0, tiled=True)
    dr, dz = call(
        grouped(middle_kernel, (n_rep,), (n_rep,) + (None,) * 5),
        [((rows, dim), F32), ((rows, dim), BF16)],
        [*das, r_own, c_own, second_gain],
    )
    dzs = rep_gather(dz)
    los = [lo[:rows]] + [rep_swap(lo[m * rows : (m + 1) * rows], m) for m in range(1, n_rep)]
    layer_own = r_own
    for piece in los:
        layer_own = layer_own + piece.astype(F32)
    layer_out = from_plane(layer_own.astype(BF16))

    back = call(
        grouped(
            attend_back_kernel,
            (n_rep, part),
            (None, n_rep, None, None, None, part, None, None, None, None, None, part - 1, None) + (None,) * 7,
        ),
        [((total, width), BF16), ((total, 2 * width), F32)]
        + [((total, 2 * width), BF16)] * (part - 1)
        + [((total, dim), BF16)],
        [j_arr, *dzs, w_out, o, q, *kvs, lse, cos, sin],
        [
            ((total, width), BF16), ((total * part, width), BF16), ((total * part, width), BF16),
            ((width, total * part), BF16), ((stat_rows, total), F32),
            ((total * part, width), F32), ((total * part, width), F32),
        ],
        n_smem=1,
    )
    dq, dkv, sends, dz_all = back[0], back[1], back[2:-1], back[-1]
    gots = [part_swap(x, l + 1) for l, x in enumerate(sends)]
    (d_out,) = call(
        out_grad_kernel,
        [((dim, width), BF16)],
        [j_arr, o_all, dz_all],
        n_smem=1,
    )
    d_out = lax.psum_scatter(d_out, "inner", scatter_dimension=0, tiled=True)
    d_qkv, da_one, gain_one_part = call(
        grouped(qkv_back_kernel, (n_rep, part), (None, None, part - 1, None, None, None, None, n_rep) + (None,) * 4),
        [((dim, 3 * width), BF16), ((total, dim), BF16), ((1, dim), F32)],
        [dq, dkv, *gots, cos, sin, a_one, w_qkv, *xs],
        [((total, 3 * width), BF16)],
    )
    d_qkv = lax.psum_scatter(d_qkv, "inner", scatter_dimension=0, tiled=True)
    das = [da_one] + [rep_swap(da_one[m * rows : (m + 1) * rows], m) for m in range(1, n_rep)]
    (grad_own,) = call(
        grouped(last_kernel, (n_rep,), (n_rep,) + (None,) * 4),
        [((rows, dim), BF16)],
        [*das, xs[0], dr, first_gain],
    )
    input_grad = from_plane(grad_own)

    def all_quarters(x):
        got = jnp.stack(rep_gather(x))
        return jnp.stack([lax.dynamic_index_in_dim(got, j ^ a, 0, keepdims=False) for a in range(n_rep)]).astype(F32)

    g_qkv = all_quarters(d_qkv).reshape(n_rep, w_rows, 3, width).transpose(1, 2, 0, 3).reshape(w_rows, 3 * dim)
    g_out = all_quarters(d_out).transpose(1, 0, 2).reshape(w_rows, dim)
    g_in = all_quarters(d_in).reshape(n_rep, w_rows, 2 * n_inner, pitch)[..., :unit]
    g_in = g_in.transpose(1, 2, 0, 3).reshape(w_rows, 2 * n_inner, n_rep * unit)[..., :ff_shard].reshape(w_rows, -1)
    g_down = all_quarters(d_down)[:, :unit].reshape(n_rep * unit, dim)[:ff_shard]
    gain_sum = lax.psum(jnp.concatenate([gain_one_part, gain_two_part]), ("rep", "inner"))
    gain_own = lax.dynamic_slice_in_dim(gain_sum, i * w_rows, w_rows, 1)
    return (layer_out, input_grad, g_qkv, g_out, g_in, g_down, gain_own[0], gain_own[1])


def solution(mesh):
    rows = P(("rep", "inner"), None)
    weight = P("inner", None)
    return jax.shard_map(
        functools.partial(on_device, mesh.shape["rep"], mesh.shape["inner"]),
        mesh=mesh,
        in_specs=(rows, rows, weight, weight, weight, weight, P("inner"), P("inner")),
        out_specs=(rows, rows, weight, weight, weight, weight, P("inner"), P("inner")),
        check_vma=False,
    )
```

```python
import functools

import jax
import jax.numpy as jnp
from jax import lax
from jax.experimental import pallas as pl
from jax.experimental.pallas import tpu as pltpu
from jax.sharding import PartitionSpec as P

HEAD_DIM = 64
EPSILON = 1e-05
THETA = 160000.0
F32 = jnp.float32
BF16 = jnp.bfloat16
NT = (((1,), (1,)), ((), ()))
TN = (((0,), (0,)), ((), ()))
VMEM_LIMIT = 56 * 1024 * 1024


def dot(a, b):
    return jnp.dot(a, b, preferred_element_type=F32)


def dot_nt(a, b):
    return lax.dot_general(a, b, NT, preferred_element_type=F32)


def dot_tn(a, b):
    return lax.dot_general(a, b, TN, preferred_element_type=F32)


def call(body, outs, args, scratch=(), n_smem=0, n_any=0, micros=1):
    n_vmem = len(args) - n_smem - n_any
    in_specs = (
        [pl.BlockSpec(memory_space=pltpu.SMEM)] * n_smem
        + [pl.BlockSpec(memory_space=pltpu.VMEM)] * n_vmem
        + [pl.BlockSpec(memory_space=pl.ANY)] * n_any
    )

    def without_waited(*refs):
        body(*refs[: n_smem + n_vmem], *refs[len(args) :])

    return pl.pallas_call(
        without_waited,
        out_shape=[jax.ShapeDtypeStruct(s, d) for s, d in outs],
        in_specs=in_specs,
        out_specs=[pl.BlockSpec(memory_space=pltpu.VMEM)] * len(outs),
        scratch_shapes=[pltpu.VMEM(s, d) for s, d in scratch],
        compiler_params=pltpu.CompilerParams(vmem_limit_bytes=VMEM_LIMIT),
        cost_estimate=pl.CostEstimate(
            flops=int(micros * 1e9), transcendentals=0, bytes_accessed=int(micros * 1e6)
        ),
    )(*args)


def after(value, *others):
    return lax.optimization_barrier((value, *others))[0]


def hat_of(values):
    centred = values - jnp.mean(values, axis=-1, keepdims=True)
    inv = lax.rsqrt(jnp.mean(centred * centred, axis=-1, keepdims=True) + EPSILON)
    return centred * inv, inv


def partner(x):
    width = x.shape[-1]
    half = HEAD_DIM // 2
    lane = lax.broadcasted_iota(jnp.int32, x.shape, x.ndim - 1)
    ahead = pltpu.roll(x, width - half, 1)
    behind = pltpu.roll(x, half, 1)
    return jnp.where(lane % HEAD_DIM < half, ahead, behind)


def tile_lanes(table, width):
    return jnp.concatenate([table] * (width // table.shape[-1]), axis=-1)


def head_mask(h, width):
    lane = lax.broadcasted_iota(jnp.int32, (1, width), 1)
    return ((lane >= h * HEAD_DIM) & (lane < (h + 1) * HEAD_DIM)).astype(BF16)


def pick_kernel(n_rep, at_ref, x_ref, outs):
    sub = x_ref.shape[0] // n_rep
    for m in range(n_rep):
        outs[m][...] = x_ref[pl.ds(pl.multiple_of((at_ref[0] ^ m) * sub, sub), sub), :]


def pick_plane_kernel(n_rep, at_ref, pieces, outs, scr):
    sub = pieces[0].shape[0]
    for m in range(n_rep):
        scr[m * sub : (m + 1) * sub, :] = pieces[m][...]
    for m in range(n_rep):
        block = at_ref[0] ^ at_ref[1] ^ m
        outs[m][...] = scr[pl.ds(pl.multiple_of(block * sub, sub), sub), :]


def place_kernel(n_rep, at_ref, pieces, out_ref):
    sub = pieces[0].shape[0]
    for k in range(n_rep):
        out_ref[pl.ds(pl.multiple_of((at_ref[1] ^ k) * sub, sub), sub), :] = pieces[k][...]


def send_back(n_rep, at_ref, scr, outs):
    sub = outs[0].shape[0]
    for k in range(n_rep):
        block = at_ref[0] ^ at_ref[1] ^ k
        outs[k][...] = scr[pl.ds(pl.multiple_of(block * sub, sub), sub), :].astype(BF16)


def weight_kernel(at_ref, qkv_ref, out_ref, gain_ref, pack_ref):
    rows, dim = out_ref.shape
    width = pack_ref.shape[1] // 4
    for p in range(3):
        start = pl.multiple_of(p * dim + at_ref[0] * width, width)
        pack_ref[:rows, p * width : (p + 1) * width] = qkv_ref[:, pl.ds(start, width)]
    start = pl.multiple_of(at_ref[0] * width, width)
    pack_ref[:rows, 3 * width :] = out_ref[:, pl.ds(start, width)]
    pack_ref[rows:, :] = gain_ref[...]


def packed_rows(pitch, dim, lanes):
    extra = pitch * dim // lanes
    spots = [(0, 0, 0, 0, extra, min(dim, lanes))]
    left = lanes - dim
    if left:
        rest = pitch - extra
        for c in range(dim // left):
            spots.append((c * rest, dim, extra, c * left, rest, left))
    return extra, spots


def ff_weight_kernel(n_rep, unit, pitch, at_ref, in_ref, down_ref, pack_ref, down_scr):
    rows = in_ref.shape[0]
    shard, dim = down_ref.shape
    lanes = pack_ref.shape[1]
    for jj in range(n_rep):
        size = min(unit, shard - jj * unit)

        @pl.when(at_ref[0] == jj)
        def _(jj=jj, size=size):
            pieces = []
            for p in range(in_ref.shape[1] // shard):
                first = p * shard + jj * unit
                pieces.append(in_ref[:, first : first + size])
                pieces.append(jnp.zeros((rows, pitch - size), BF16))
            pack_ref[:rows, :] = jnp.concatenate(pieces, axis=1)
            down_scr[:size, :] = down_ref[jj * unit : jj * unit + size, :]
            down_scr[size:, :] = jnp.zeros((pitch - size, dim), BF16)

    _, spots = packed_rows(pitch, dim, lanes)
    for row, lane, row_in, col_in, n, w in spots:
        pack_ref[rows + row : rows + row + n, lane : lane + w] = down_scr[row_in : row_in + n, col_in : col_in + w]


def qkv_kernel(
    n_rep, n_part, at_ref, refs_x, refs_own, refs_other, cos_ref, sin_ref,
    q_ref, kv_ref, a_ref, w_ref, gains_ref,
):
    rows = refs_x[0].shape[0]
    width = q_ref.shape[1]
    dim = a_ref.shape[1]
    lanes = 4 * width
    high = refs_own[0].shape[0]
    w_rows = high - 8
    gains = jnp.zeros((8, lanes), F32)
    for l in range(n_part):
        for m in range(n_rep):
            ref, base = (refs_own[m], 0) if l == 0 else (refs_other[l - 1], m * high)
            shard = (at_ref[1] ^ m) * n_part + (at_ref[2] ^ l)
            start = pl.multiple_of(shard * w_rows, w_rows)
            w_ref[pl.ds(start, w_rows), :] = ref[base : base + w_rows, : 3 * width]
            gains = gains + ref[base + w_rows : base + high, :].astype(F32)
    per = dim // lanes
    for g in range(2):
        gains_ref[g : g + 1, :] = jnp.concatenate(
            [gains[g * per + k : g * per + k + 1, :] for k in range(per)], axis=1
        )
    for m in range(n_rep):
        hat, _ = hat_of(refs_x[m][...].astype(F32))
        a_ref[m * rows : (m + 1) * rows, :] = (hat * gains_ref[0:1, :]).astype(BF16)
    step = 2 * rows if n_rep % 2 == 0 else rows
    for r0 in range(0, n_rep * rows, step):
        sl = slice(r0, r0 + step)
        proj = dot(a_ref[sl, :], w_ref[...])
        cos = tile_lanes(cos_ref[sl, :], width)
        sin = tile_lanes(sin_ref[sl, :], width)
        query = proj[:, :width]
        key = proj[:, width : 2 * width]
        query = (query * cos + partner(query) * sin).astype(BF16).astype(F32)
        q_ref[sl, :] = (query * HEAD_DIM**-0.5).astype(BF16)
        kv_ref[sl, :width] = (key * cos + partner(key) * sin).astype(BF16)
        kv_ref[sl, width:] = proj[:, 2 * width :].astype(BF16)


def attend_kernel(n_part, q_ref, refs_kv, o_ref, lse_ref, k_scr, vt_scr):
    rows, width = q_ref.shape
    keys = refs_kv[0].shape[0]
    for l in range(n_part):
        k_scr[l * keys : (l + 1) * keys, :] = refs_kv[l][:, :width]
        vt_scr[:, l * keys : (l + 1) * keys] = refs_kv[l][:, width:].astype(F32).T.astype(BF16)
    heads = width // HEAD_DIM
    step = min(256, rows)

    def body(c, carry):
        r0 = pl.multiple_of(c * step, step)
        for h in range(heads):
            pair = h // 2 * 128
            q = q_ref[pl.ds(r0, step), pair : pair + 128] * head_mask(h % 2, 128)
            s = dot_nt(k_scr[:, pair : pair + 128], q)
            top = jnp.max(s, axis=0, keepdims=True)
            e = jnp.exp(s - top)
            mass = jnp.sum(e, axis=0, keepdims=True)
            lse_ref[h : h + 1, pl.ds(r0, step)] = top + jnp.log(mass)
            ot = dot(vt_scr[h * HEAD_DIM : (h + 1) * HEAD_DIM, :], e.astype(BF16)) / mass
            ot_list.append(ot)
            if h % 2 == 1:
                both = jnp.concatenate(ot_list, axis=0)
                o_ref[pl.ds(r0, step), pair : pair + 128] = both.T.astype(BF16)
                ot_list.clear()
        return carry

    ot_list = []
    lax.fori_loop(0, rows // step, body, 0)


def ff_kernel(
    n_rep, n_part, pitch, at_ref, refs_x, refs_o, refs_wo, refs_wo_other, ffw_ref, refs_c, gains_ref,
    r_ref, refs_da, a_ref, m_ref, du_ref, c_ref, o_ref, wout_ref, wdown_ref, gain_ref,
    hat_scr, u_scr, dm_scr, win_scr,
):
    rows, dim = refs_x[0].shape
    total = n_rep * rows
    quarter = refs_o[0].shape[1]
    j = at_ref[0]
    n_inner = n_rep * n_part
    w_rows = dim // n_inner
    lanes = win_scr.shape[1]
    extra, spots = packed_rows(pitch, dim, lanes)
    for k in range(n_rep):
        col = pl.multiple_of((j ^ k) * quarter, quarter)
        for l in range(n_part):
            for m in range(n_rep):
                shard = (at_ref[1] ^ m) * n_part + (at_ref[2] ^ l)
                row = pl.multiple_of(shard * w_rows, w_rows)
                if l == 0:
                    piece = refs_wo[k][m * w_rows : (m + 1) * w_rows, :]
                else:
                    at = (k * n_rep + m) * w_rows
                    piece = refs_wo_other[l - 1][at : at + w_rows, :]
                wout_ref[pl.ds(row, w_rows), pl.ds(col, quarter)] = piece
    for m in range(n_rep):
        hat_scr[m * rows : (m + 1) * rows, :] = refs_x[m][...].astype(F32)
        c_ref[m * rows : (m + 1) * rows, :] = refs_c[m][...]
        col = pl.multiple_of((j ^ m) * quarter, quarter)
        for k in range(n_rep):
            at = (k ^ m) * rows
            o_ref[k * rows : (k + 1) * rows, pl.ds(col, quarter)] = refs_o[m][at : at + rows, :]
    for p in range(n_inner):
        base = p * (w_rows + extra)
        win_scr[p * w_rows : (p + 1) * w_rows, :] = ffw_ref[base : base + w_rows, :]
        for row, lane, row_in, col_in, n, w in spots:
            top = base + w_rows + row
            wdown_ref[p * pitch + row_in : p * pitch + row_in + n, col_in : col_in + w] = ffw_ref[
                top : top + n, lane : lane + w
            ]
    hat_scr[...] += dot(o_ref[...], wout_ref[...])
    r_ref[...] = hat_scr[:rows, :]
    gain = gains_ref[1:2, :]

    def norm_step(c, carry):
        r0 = pl.multiple_of(c * 64, 64)
        hat, _ = hat_of(hat_scr[pl.ds(r0, 64), :])
        hat_scr[pl.ds(r0, 64), :] = hat
        a_ref[pl.ds(r0, 64), :] = (hat * gain).astype(BF16)
        return carry

    lax.fori_loop(0, total // 64, norm_step, 0)
    u_scr[...] = dot(a_ref[...], win_scr[...])
    dm_scr[...] = dot_nt(c_ref[...], wdown_ref[...])
    width = m_ref.shape[1]

    def gate_step(c, carry):
        sl = pl.ds(pl.multiple_of(c * 32, 32), 32)
        pre = u_scr[sl, :width]
        gate = u_scr[sl, width:]
        dm = dm_scr[sl, :]
        cdf = 0.5 * (1.0 + lax.erf(pre * (0.5**0.5)))
        pdf = jnp.exp(-0.5 * pre * pre) * 0.3989422804014327
        act = pre * cdf
        m_ref[sl, :] = (act * gate).astype(BF16)
        du_ref[sl, :width] = (dm * gate * (cdf + pre * pdf)).astype(BF16)
        du_ref[sl, width:] = (dm * act).astype(BF16)
        return carry

    lax.fori_loop(0, total // 32, gate_step, 0)
    total_gain = jnp.zeros((1, dim), F32)
    for m in range(n_rep):
        sl = slice(m * rows, (m + 1) * rows)
        da = dot_nt(du_ref[sl, :], win_scr[...])
        refs_da[m][...] = da.astype(BF16)
        total_gain = total_gain + jnp.sum(da * hat_scr[sl, :], axis=0, keepdims=True)
    gain_ref[...] = total_gain


def ff_grads_kernel(n_rep, n_inner, pitch, m_ref, wdown_ref, c_ref, a_ref, du_ref, refs_lo, grad_ref, down_scr):
    rows, dim = refs_lo[0].shape
    w_rows = dim // n_inner
    lanes = du_ref.shape[1]
    extra, spots = packed_rows(pitch, dim, lanes)
    high = w_rows + extra
    down_scr[...] = dot_tn(m_ref[...], c_ref[...]).astype(BF16)
    din = dot_tn(a_ref[...], du_ref[...]).astype(BF16)
    for p in range(n_inner):
        grad_ref[p * high : p * high + w_rows, :] = din[p * w_rows : (p + 1) * w_rows, :]
        for row, lane, row_in, col_in, n, w in spots:
            top = p * high + w_rows + row
            grad_ref[top : top + n, lane : lane + w] = down_scr[
                p * pitch + row_in : p * pitch + row_in + n, col_in : col_in + w
            ]
    for m in range(n_rep):
        refs_lo[m][...] = dot(m_ref[m * rows : (m + 1) * rows, :], wdown_ref[...]).astype(BF16)


def norm_back(values, gain, grad):
    hat, inv = hat_of(values)
    dhat = grad * gain
    return inv * (
        dhat
        - jnp.mean(dhat, axis=-1, keepdims=True)
        - hat * jnp.mean(dhat * hat, axis=-1, keepdims=True)
    )


def sum_of(refs):
    total = refs[0][...].astype(F32)
    for ref in refs[1:]:
        total = total + ref[...].astype(F32)
    return total


def middle_kernel(n_rep, refs_da, r_ref, c_ref, gains_ref, dr_ref, dz_ref):
    dr = c_ref[...].astype(F32) + norm_back(r_ref[...], gains_ref[1:2, :], sum_of(refs_da))
    dr_ref[...] = dr
    dz_ref[...] = dr.astype(BF16)


def layer_out_kernel(n_rep, at_ref, refs_lo, r_ref, outs, scr):
    scr[...] = r_ref[...] + sum_of(refs_lo)
    send_back(n_rep, at_ref, scr, outs)


def last_kernel(n_rep, at_ref, refs_da, x_ref, dr_ref, gains_ref, outs, scr):
    back = norm_back(x_ref[...].astype(F32), gains_ref[0:1, :], sum_of(refs_da))
    scr[...] = dr_ref[...] + back
    send_back(n_rep, at_ref, scr, outs)


def attend_back_kernel(
    n_rep, n_part, sub_j, refs_dz, wout_ref, o_ref, q_ref, refs_kv, lse_ref, cos_ref, sin_ref,
    dq_ref, dkv_ref, refs_send, dz_ref, do_scr, k_scr, v_scr, kt_scr, delta_scr, dk_scr, dv_scr,
):
    rows, width = q_ref.shape
    keys = refs_kv[0].shape[0]
    part = refs_dz[0].shape[0]
    j = sub_j[0]
    for m in range(n_rep):
        dz_ref[m * part : (m + 1) * part, :] = refs_dz[m][...]
    start = pl.multiple_of(j * width, width)
    dout = dot_nt(dz_ref[...], wout_ref[pl.ds(start, width), :]).astype(BF16)
    do_scr[...] = dout
    prod_t = (dout.astype(F32) * o_ref[...].astype(F32)).T
    heads = width // HEAD_DIM
    for h in range(heads):
        delta_scr[h : h + 1, :] = jnp.sum(
            prod_t[h * HEAD_DIM : (h + 1) * HEAD_DIM, :], axis=0, keepdims=True
        )
    for l in range(n_part):
        sl = slice(l * keys, (l + 1) * keys)
        k_scr[sl, :] = refs_kv[l][:, :width]
        v_scr[sl, :] = refs_kv[l][:, width:]
        kt_scr[:, sl] = refs_kv[l][:, :width].astype(F32).T.astype(BF16)
    dk_scr[...] = jnp.zeros_like(dk_scr)
    dv_scr[...] = jnp.zeros_like(dv_scr)
    step = min(256, rows)

    def body(c, carry):
        r0 = pl.multiple_of(c * step, step)
        for h in range(heads):
            pair = h // 2 * 128
            lanes = slice(pair, pair + 128)
            mask = head_mask(h % 2, 128)
            q = q_ref[pl.ds(r0, step), lanes] * mask
            do = do_scr[pl.ds(r0, step), lanes] * mask
            p = jnp.exp(dot_nt(k_scr[:, lanes], q) - lse_ref[h : h + 1, pl.ds(r0, step)])
            dp = dot_nt(v_scr[:, lanes], do)
            ds = (p * (dp - delta_scr[h : h + 1, pl.ds(r0, step)])).astype(BF16)
            dv_scr[:, lanes] += dot(p.astype(BF16), do)
            dk_scr[:, lanes] += dot(ds, q)
            dq_list.append(dot(kt_scr[h * HEAD_DIM : (h + 1) * HEAD_DIM, :], ds))
            if h % 2 == 1:
                dq = jnp.concatenate(dq_list, axis=0).T * HEAD_DIM**-0.5
                dq_list.clear()
                cos = cos_ref[pl.ds(r0, step), :]
                sin = sin_ref[pl.ds(r0, step), :]
                dq_ref[pl.ds(r0, step), lanes] = (dq * cos - partner(dq) * sin).astype(BF16)
        return carry

    dq_list = []
    lax.fori_loop(0, rows // step, body, 0)
    dkv_ref[:, :width] = dk_scr[:keys, :]
    dkv_ref[:, width:] = dv_scr[:keys, :]
    for l in range(1, n_part):
        sl = slice(l * keys, (l + 1) * keys)
        refs_send[l - 1][:, :width] = dk_scr[sl, :].astype(BF16)
        refs_send[l - 1][:, width:] = dv_scr[sl, :].astype(BF16)


def out_grad_kernel(sub_j, o_ref, dz_ref, dout_ref):
    quarter = dout_ref.shape[1]
    cols = dz_ref[:, pl.ds(pl.multiple_of(sub_j[0] * quarter, quarter), quarter)]
    dout_ref[...] = dot_tn(o_ref[...], cols).astype(BF16)


def qkv_back_kernel(
    n_rep, n_part, at_ref, dq_ref, dkv_ref, refs_got, cos_ref, sin_ref, a_ref, w_ref, refs_x, dout_ref,
    gain_two_ref, keep_ref, refs_send, refs_da, dp_scr, grad_scr,
):
    width = dq_ref.shape[1]
    rows, dim = refs_x[0].shape
    lanes = 4 * width
    high = keep_ref.shape[0] // n_rep
    w_rows = high - 8
    dkv = dkv_ref[...]
    for got in refs_got:
        dkv = dkv + got[...].astype(F32)
    dk = dkv[:, :width]
    cos = tile_lanes(cos_ref[...], width)
    sin = tile_lanes(sin_ref[...], width)
    dp_scr[:, :width] = dq_ref[...]
    dp_scr[:, width : 2 * width] = (dk * cos - partner(dk) * sin).astype(BF16)
    dp_scr[:, 2 * width :] = dkv[:, width:].astype(BF16)
    grad_scr[:, : 3 * width] = dot_tn(a_ref[...], dp_scr[...])
    grad_scr[:, 3 * width :] = dout_ref[...].astype(F32)
    gain = jnp.zeros((1, dim), F32)
    for m in range(n_rep):
        da = dot_nt(dp_scr[m * rows : (m + 1) * rows, :], w_ref[...])
        refs_da[m][...] = da.astype(BF16)
        hat, _ = hat_of(refs_x[m][...].astype(F32))
        gain = gain + jnp.sum(da * hat, axis=0, keepdims=True)
    per = dim // lanes
    strips = [g[:, k * lanes : (k + 1) * lanes] for g in (gain, gain_two_ref[...]) for k in range(per)]
    strips.append(jnp.zeros((8 - len(strips), lanes), F32))
    gains = jnp.concatenate(strips, axis=0)
    for l in range(n_part):
        for m in range(n_rep):
            shard = (at_ref[1] ^ m) * n_part + (at_ref[2] ^ l)
            block = grad_scr[pl.ds(pl.multiple_of(shard * w_rows, w_rows), w_rows), :]
            ref = keep_ref if l == 0 else refs_send[l - 1]
            ref[m * high : m * high + w_rows, :] = block.astype(ref.dtype)
            ref[m * high + w_rows : (m + 1) * high, :] = gains.astype(ref.dtype)


def part_sum_kernel(n_rep, keep_ref, refs_got, own_ref, outs):
    high = own_ref.shape[0]
    for m in range(n_rep):
        sl = slice(m * high, (m + 1) * high)
        total = keep_ref[sl, :]
        for got in refs_got:
            total = total + got[sl, :].astype(F32)
        if m == 0:
            own_ref[...] = total
        else:
            outs[m - 1][...] = total.astype(BF16)


def plane_sum_kernel(own_ref, refs_got, out_ref):
    out_ref[...] = (own_ref[...] + sum_of(refs_got)).astype(BF16)


def grads_kernel(n_rep, at_ref, pieces, qkv_ref, out_ref, gains_ref):
    width = pieces[0].shape[1] // 4
    rows, dim = out_ref.shape
    for m in range(n_rep):
        for p in range(3):
            start = pl.multiple_of(p * dim + (at_ref[0] ^ m) * width, width)
            qkv_ref[:, pl.ds(start, width)] = pieces[m][:rows, p * width : (p + 1) * width].astype(F32)
        start = pl.multiple_of((at_ref[0] ^ m) * width, width)
        out_ref[:, pl.ds(start, width)] = pieces[m][:rows, 3 * width :].astype(F32)
    gains = pieces[0][rows:, :].astype(F32)
    for m in range(1, n_rep):
        gains = gains + pieces[m][rows:, :].astype(F32)
    gains_ref[...] = gains


def ff_out_kernel(n_rep, unit, pitch, at_ref, pieces, in_ref, down_ref, scr, down_scr):
    high, lanes = pieces[0].shape
    rows = in_ref.shape[0]
    shard, dim = down_ref.shape
    for m in range(n_rep):
        scr[at_ref[0] ^ m] = pieces[m][...]
    _, spots = packed_rows(pitch, dim, lanes)
    strips = []
    for jj in range(n_rep):
        size = min(unit, shard - jj * unit)
        for row, lane, row_in, col_in, n, w in spots:
            down_scr[row_in : row_in + n, col_in : col_in + w] = scr[
                jj, rows + row : rows + row + n, lane : lane + w
            ].astype(F32)
        down_ref[jj * unit : jj * unit + size, :] = down_scr[:size, :]
    for p in range(lanes // pitch):
        strips = []
        for jj in range(n_rep):
            size = min(unit, shard - jj * unit)
            strips.append(scr[jj, :rows, p * pitch : p * pitch + size].astype(F32))
        in_ref[:, p * shard : (p + 1) * shard] = jnp.concatenate(strips, axis=1)


def split_refs(counts, refs):
    out, at = [], 0
    for n in counts:
        if n is None:
            out.append(refs[at])
            at += 1
        else:
            out.append(list(refs[at : at + n]))
            at += n
    return out


def grouped(kernel, static, counts):
    def body(*refs):
        kernel(*static, *split_refs(counts, refs))

    return body


def on_device(
    n_rep, n_inner,
    tokens, cotangent, qkv_weight, out_weight, in_weight, down_weight, gain_one, gain_two,
):
    part = n_inner // n_rep
    rows, dim = tokens.shape
    sub = rows // n_rep
    w_rows = qkv_weight.shape[0]
    width = dim // n_rep
    lanes = 4 * width
    high = w_rows + 8
    ff_shard = down_weight.shape[0]
    unit = -(-ff_shard // n_rep)
    pitch = -(-unit // 16) * 16
    ff = pitch * n_inner
    ff_high = w_rows + pitch * dim // (2 * ff)
    total = n_rep * rows
    j = lax.axis_index("rep")
    i = lax.axis_index("inner")
    s = i // part
    t = i % part
    at = jnp.stack([j, s, t]).astype(jnp.int32)

    def rep_swap(x, m):
        return lax.ppermute(x, "rep", [(a, a ^ m) for a in range(n_rep)])

    def plane_swap(x, m):
        pairs = [(a * part + b, (a ^ m) * part + b) for a in range(n_rep) for b in range(part)]
        return lax.ppermute(x, "inner", pairs)

    def part_swap(x, l):
        pairs = [(a * part + b, a * part + (b ^ l)) for a in range(n_rep) for b in range(part)]
        return lax.ppermute(x, "inner", pairs)

    def rep_gather(x):
        return [x] + [rep_swap(x, m) for m in range(1, n_rep)]

    def rep_trade(pieces):
        return [pieces[0]] + [rep_swap(pieces[m], m) for m in range(1, n_rep)]

    def plane_trade(pieces):
        return [pieces[0]] + [plane_swap(pieces[m], m) for m in range(1, n_rep)]

    def send_home(pieces):
        got = []
        for k in range(n_rep):
            pairs = []
            for a in range(n_rep):
                for z in range(n_rep):
                    for b in range(part):
                        pairs.append((a * n_inner + z * part + b, z * n_inner + (a ^ k) * part + b))
            got.append(lax.ppermute(pieces[k], ("rep", "inner"), pairs))
        return got

    small = [((sub, dim), BF16)] * n_rep

    def pick(x):
        return call(grouped(pick_kernel, (n_rep,), (None, None, n_rep)), small, [at, x], n_smem=1)

    def pick_plane(pieces):
        return call(
            grouped(pick_plane_kernel, (n_rep,), (None, n_rep, n_rep, None)),
            small, [at, *pieces], [((rows, dim), BF16)], n_smem=1,
        )

    def place(pieces):
        return call(
            grouped(place_kernel, (n_rep,), (None, n_rep, None)), [((rows, dim), BF16)], [at, *pieces], n_smem=1
        )[0]

    x_first = rep_trade(pick(tokens))
    gain_rows = jnp.zeros((2, dim), BF16)
    gain_rows = lax.dynamic_update_slice(gain_rows, jnp.stack([gain_one, gain_two]), (0, i * w_rows))
    gain_rows = gain_rows.reshape(2 * dim // lanes, lanes)
    gain_rows = jnp.pad(gain_rows, ((0, 8 - gain_rows.shape[0]), (0, 0)))
    (w_pack,) = call(weight_kernel, [((high, lanes), BF16)], [at, qkv_weight, out_weight, gain_rows], n_smem=1)
    w_own = [w_pack] + [plane_swap(w_pack, m) for m in range(1, n_rep)]
    (ff_pack,) = call(
        grouped(ff_weight_kernel, (n_rep, unit, pitch), (None,) * 5),
        [((ff_high, 2 * ff), BF16)],
        [at, in_weight, down_weight],
        [((pitch, dim), BF16)],
        n_smem=1,
    )
    x_own = jnp.concatenate(plane_trade(pick_plane(x_first)), axis=0)
    w_own = [after(w, x_own) for w in w_own]
    ff_w = lax.all_gather(after(ff_pack, *w_own), "inner", axis=0, tiled=True)
    xs = rep_gather(x_own)
    c_first = rep_trade(pick(after(cotangent, *x_first)))
    c_own = jnp.concatenate(plane_trade(pick_plane([after(c, x_own) for c in c_first])), axis=0)

    w_other = [part_swap(jnp.concatenate(w_own, axis=0), l) for l in range(1, part)]
    wo_own = rep_gather(after(jnp.concatenate([w[:w_rows, 3 * width :] for w in w_own], axis=0), xs[-1]))
    wo_other = [part_swap(jnp.concatenate(wo_own, axis=0), l) for l in range(1, part)]

    order = jnp.arange(total, dtype=jnp.int32)
    spot = ((s ^ (order // sub % n_rep)) * part + t) * rows + (j ^ (order // rows)) * sub + order % sub
    inv_freq = 1.0 / THETA ** (jnp.arange(HEAD_DIM // 2, dtype=F32) * (2.0 / HEAD_DIM))
    angle = spot.astype(F32)[:, None] * inv_freq[None, :]
    cos_half, sin_half = jnp.cos(angle), jnp.sin(angle)
    cos = jnp.concatenate([cos_half] * 4, axis=1)
    sin = jnp.concatenate([-sin_half, sin_half] * 2, axis=1)

    q, kv, a_one, w_qkv, gains = call(
        grouped(qkv_kernel, (n_rep, part), (None, n_rep, n_rep, part - 1) + (None,) * 7),
        [
            ((total, width), BF16), ((total, 2 * width), BF16), ((total, dim), BF16),
            ((dim, 3 * width), BF16), ((2, dim), F32),
        ],
        [at, *xs, *w_own, *w_other, cos, sin],
        n_smem=1, micros=4,
    )
    kvs = [kv] + [part_swap(kv, l) for l in range(1, part)]
    heads = width // HEAD_DIM
    stat_rows = -(-heads // 8) * 8
    o, lse = call(
        grouped(attend_kernel, (part,), (None, part) + (None,) * 4),
        [((total, width), BF16), ((stat_rows, total), F32)],
        [q, *kvs],
        [((total * part, width), BF16), ((width, total * part), BF16)],
        micros=8,
    )
    os_ = rep_gather(o)
    cs = rep_gather(after(c_own, xs[-1]))
    ff_out = call(
        grouped(
            ff_kernel, (n_rep, part, pitch),
            (None, n_rep, n_rep, n_rep, part - 1, None, n_rep, None, None, n_rep) + (None,) * 12,
        ),
        [((rows, dim), F32)]
        + [((rows, dim), BF16)] * n_rep
        + [
            ((total, dim), BF16), ((total, ff), BF16), ((total, 2 * ff), BF16), ((total, dim), BF16),
            ((total, dim), BF16), ((dim, dim), BF16), ((ff, dim), BF16), ((1, dim), F32),
        ],
        [at, *xs, *os_, *wo_own, *wo_other, ff_w, *cs, gains],
        [((total, dim), F32), ((total, 2 * ff), F32), ((total, ff), F32), ((dim, 2 * ff), BF16)],
        n_smem=1, micros=14,
    )
    r_own, da_two = ff_out[0], ff_out[1 : 1 + n_rep]
    a_two, gated, d_hidden, c_all, o_all, w_out, w_down, gain_two_part = ff_out[1 + n_rep :]
    das = rep_trade(da_two)
    ff_back = call(
        grouped(ff_grads_kernel, (n_rep, n_inner, pitch), (None,) * 5 + (n_rep, None, None)),
        [((rows, dim), BF16)] * n_rep + [((n_inner * ff_high, 2 * ff), BF16)],
        [gated, w_down, c_all, a_two, d_hidden],
        [((ff, dim), BF16)],
        micros=7,
    )
    lo, ff_grad = ff_back[:-1], ff_back[-1]
    dr, dz = call(
        grouped(middle_kernel, (n_rep,), (n_rep,) + (None,) * 5),
        [((rows, dim), F32), ((rows, dim), BF16)],
        [*das, r_own, c_own, gains, ff_grad],
        n_any=1, micros=2,
    )
    ff_grad = lax.psum_scatter(ff_grad, "inner", scatter_dimension=0, tiled=True)
    dzs = rep_gather(dz)

    back = call(
        grouped(
            attend_back_kernel,
            (n_rep, part),
            (None, n_rep, None, None, None, part, None, None, None, None, None, part - 1, None) + (None,) * 7,
        ),
        [((total, width), BF16), ((total, 2 * width), F32)]
        + [((total, 2 * width), BF16)] * (part - 1)
        + [((total, dim), BF16)],
        [at, *dzs, w_out, o, q, *kvs, lse, cos, sin],
        [
            ((total, width), BF16), ((total * part, width), BF16), ((total * part, width), BF16),
            ((width, total * part), BF16), ((stat_rows, total), F32),
            ((total * part, width), F32), ((total * part, width), F32),
        ],
        n_smem=1, micros=10,
    )
    dq, dkv, sends, dz_all = back[0], back[1], back[2:-1], back[-1]
    gots = [part_swap(x, l + 1) for l, x in enumerate(sends)]
    (d_out,) = call(
        out_grad_kernel, [((dim, width), BF16)], [at, o_all, dz_all], n_smem=1, micros=2,
    )
    los = rep_trade([after(x, dzs[-1]) for x in lo])
    parts = call(
        grouped(layer_out_kernel, (n_rep,), (None, n_rep, None, n_rep, None)),
        small, [at, *los, r_own, dq], [((rows, dim), F32)], n_smem=1, n_any=1,
    )
    layer_out = place(send_home(parts))

    qkv_out = call(
        grouped(
            qkv_back_kernel, (n_rep, part),
            (None, None, None, part - 1, None, None, None, None, n_rep, None, None, None, part - 1, n_rep, None, None),
        ),
        [((n_rep * high, lanes), F32)]
        + [((n_rep * high, lanes), BF16)] * (part - 1)
        + [((rows, dim), BF16)] * n_rep,
        [at, dq, dkv, *gots, cos, sin, a_one, w_qkv, *xs, d_out, gain_two_part],
        [((total, 3 * width), BF16), ((dim, lanes), F32)],
        n_smem=1, micros=6,
    )
    keep, sends, da_one = qkv_out[0], qkv_out[1:part], qkv_out[part:]
    gots = [part_swap(x, l + 1) for l, x in enumerate(sends)]
    summed = call(
        grouped(part_sum_kernel, (n_rep,), (None, part - 1, None, n_rep - 1)),
        [((high, lanes), F32)] + [((high, lanes), BF16)] * (n_rep - 1),
        [keep, *gots],
    )
    gots = [plane_swap(x, m + 1) for m, x in enumerate(summed[1:])]
    das = rep_trade(da_one)
    parts = call(
        grouped(last_kernel, (n_rep,), (None, n_rep, None, None, None, n_rep, None)),
        small, [at, *das, xs[0], dr, gains], [((rows, dim), F32)], n_smem=1, micros=2,
    )
    input_grad = place(send_home(parts))
    (quarter,) = call(
        grouped(plane_sum_kernel, (), (None, n_rep - 1, None)), [((high, lanes), BF16)], [summed[0], *gots]
    )
    g_qkv, g_out, g_gains = call(
        grouped(grads_kernel, (n_rep,), (None, n_rep, None, None, None)),
        [((w_rows, 3 * dim), F32), ((w_rows, dim), F32), ((8, lanes), F32)],
        [at, *rep_gather(quarter)],
        n_smem=1, micros=2,
    )
    g_in, g_down = call(
        grouped(ff_out_kernel, (n_rep, unit, pitch), (None, n_rep, None, None, None, None)),
        [((w_rows, 2 * n_inner * ff_shard), F32), ((ff_shard, dim), F32)],
        [at, *rep_gather(ff_grad)],
        [((n_rep, ff_high, 2 * ff), BF16), ((pitch, dim), F32)],
        n_smem=1, micros=4,
    )
    gain_grads = g_gains[: 2 * dim // lanes].reshape(2, dim)
    gain_grads = lax.dynamic_slice_in_dim(gain_grads, i * w_rows, w_rows, 1)
    return (layer_out, input_grad, g_qkv, g_out, g_in, g_down, gain_grads[0], gain_grads[1])


def solution(mesh):
    rows = P(("rep", "inner"), None)
    weight = P("inner", None)
    return jax.shard_map(
        functools.partial(on_device, mesh.shape["rep"], mesh.shape["inner"]),
        mesh=mesh,
        in_specs=(rows, rows, weight, weight, weight, weight, P("inner"), P("inner")),
        out_specs=(rows, rows, weight, weight, weight, weight, P("inner"), P("inner")),
        check_vma=False,
    )
```

```python
import functools

import jax
import jax.numpy as jnp
from jax import lax
from jax.experimental import pallas as pl
from jax.experimental.pallas import tpu as pltpu
from jax.sharding import PartitionSpec as P

HEAD_DIM = 64
EPSILON = 1e-05
THETA = 160000.0
F32 = jnp.float32
BF16 = jnp.bfloat16
NT = (((1,), (1,)), ((), ()))
TN = (((0,), (0,)), ((), ()))
VMEM_LIMIT = 56 * 1024 * 1024


def dot(a, b):
    return jnp.dot(a, b, preferred_element_type=F32)


def dot_nt(a, b):
    return lax.dot_general(a, b, NT, preferred_element_type=F32)


def dot_tn(a, b):
    return lax.dot_general(a, b, TN, preferred_element_type=F32)


def call(body, outs, args, scratch=(), n_smem=0, n_any=0, micros=1):
    n_vmem = len(args) - n_smem - n_any
    in_specs = (
        [pl.BlockSpec(memory_space=pltpu.SMEM)] * n_smem
        + [pl.BlockSpec(memory_space=pltpu.VMEM)] * n_vmem
        + [pl.BlockSpec(memory_space=pl.ANY)] * n_any
    )

    def without_waited(*refs):
        body(*refs[: n_smem + n_vmem], *refs[len(args) :])

    return pl.pallas_call(
        without_waited,
        out_shape=[jax.ShapeDtypeStruct(s, d) for s, d in outs],
        in_specs=in_specs,
        out_specs=[pl.BlockSpec(memory_space=pltpu.VMEM)] * len(outs),
        scratch_shapes=[pltpu.VMEM(s, d) for s, d in scratch],
        compiler_params=pltpu.CompilerParams(vmem_limit_bytes=VMEM_LIMIT),
        cost_estimate=pl.CostEstimate(
            flops=int(micros * 1e9), transcendentals=0, bytes_accessed=int(micros * 1e6)
        ),
    )(*args)


def after(value, *others):
    return lax.optimization_barrier((value, *others))[0]


def hat_of(values):
    centred = values - jnp.mean(values, axis=-1, keepdims=True)
    inv = lax.rsqrt(jnp.mean(centred * centred, axis=-1, keepdims=True) + EPSILON)
    return centred * inv, inv


def partner(x):
    width = x.shape[-1]
    half = HEAD_DIM // 2
    lane = lax.broadcasted_iota(jnp.int32, x.shape, x.ndim - 1)
    ahead = pltpu.roll(x, width - half, 1)
    behind = pltpu.roll(x, half, 1)
    return jnp.where(lane % HEAD_DIM < half, ahead, behind)


def tile_lanes(table, width):
    return jnp.concatenate([table] * (width // table.shape[-1]), axis=-1)


def head_mask(h, width):
    lane = lax.broadcasted_iota(jnp.int32, (1, width), 1)
    return ((lane >= h * HEAD_DIM) & (lane < (h + 1) * HEAD_DIM)).astype(BF16)


def place_kernel(n_rep, at_ref, pieces, first_ref, second_ref):
    sub = pieces[0].shape[0] // 2
    for k in range(n_rep):
        spot = pl.ds(pl.multiple_of((at_ref[1] ^ k) * sub, sub), sub)
        first_ref[spot, :] = pieces[k][:sub, :]
        second_ref[spot, :] = pieces[k][sub:, :]


def send_back(n_rep, at_ref, scr, outs, first):
    sub = outs[0].shape[0] // 2
    for k in range(n_rep):
        block = at_ref[0] ^ k
        outs[k][first : first + sub, :] = scr[pl.ds(pl.multiple_of(block * sub, sub), sub), :].astype(BF16)


def weight_kernel(n_inner, n_part, at_ref, qkv_ref, out_ref, gains_ref, pack_ref):
    rows, dim = out_ref.shape
    lanes = pack_ref.shape[1]
    width = lanes // 4
    for p in range(3):
        start = pl.multiple_of(p * dim + at_ref[0] * width, width)
        pack_ref[:rows, p * width : (p + 1) * width] = qkv_ref[:, pl.ds(start, width)]
    start = pl.multiple_of(at_ref[0] * width, width)
    pack_ref[:rows, 3 * width :] = out_ref[:, pl.ds(start, width)]
    shard = lax.broadcasted_iota(jnp.int32, (2, dim), 1) // rows
    own = jnp.concatenate([gains_ref[...].astype(F32)] * n_inner, axis=1)
    own = jnp.where(shard == at_ref[1] * n_part + at_ref[2], own, 0.0)
    strips = [own[g : g + 1, k * lanes : (k + 1) * lanes] for g in range(2) for k in range(dim // lanes)]
    strips.append(jnp.zeros((8 - len(strips), lanes), F32))
    pack_ref[rows:, :] = jnp.concatenate(strips, axis=0).astype(BF16)


def packed_rows(pitch, dim, lanes):
    extra = pitch * dim // lanes
    spots = [(0, 0, 0, 0, extra, min(dim, lanes))]
    left = lanes - dim
    if left:
        rest = pitch - extra
        for c in range(dim // left):
            spots.append((c * rest, dim, extra, c * left, rest, left))
    return extra, spots


def ff_weight_kernel(n_rep, unit, pitch, at_ref, in_ref, down_ref, pack_ref, down_scr):
    rows = in_ref.shape[0]
    shard, dim = down_ref.shape
    lanes = pack_ref.shape[1]
    for jj in range(n_rep):
        size = min(unit, shard - jj * unit)

        @pl.when(at_ref[0] == jj)
        def _(jj=jj, size=size):
            pieces = []
            for p in range(in_ref.shape[1] // shard):
                first = p * shard + jj * unit
                pieces.append(in_ref[:, first : first + size])
                pieces.append(jnp.zeros((rows, pitch - size), BF16))
            pack_ref[:rows, :] = jnp.concatenate(pieces, axis=1)
            down_scr[:size, :] = down_ref[jj * unit : jj * unit + size, :]
            down_scr[size:, :] = jnp.zeros((pitch - size, dim), BF16)

    _, spots = packed_rows(pitch, dim, lanes)
    for row, lane, row_in, col_in, n, w in spots:
        pack_ref[rows + row : rows + row + n, lane : lane + w] = down_scr[row_in : row_in + n, col_in : col_in + w]


def qkv_kernel(
    n_rep, n_part, refs_x, pack_ref, cos_ref, sin_ref,
    q_ref, kv_ref, a_ref, w_ref, gains_ref,
):
    rows = refs_x[0].shape[0]
    width = q_ref.shape[1]
    dim = a_ref.shape[1]
    lanes = 4 * width
    n_inner = n_rep * n_part
    high = pack_ref.shape[0] // n_inner
    w_rows = high - 8
    gains = jnp.zeros((8, lanes), F32)
    for p in range(n_inner):
        base = p * high
        w_ref[p * w_rows : (p + 1) * w_rows, :] = pack_ref[base : base + w_rows, : 3 * width]
        gains = gains + pack_ref[base + w_rows : base + high, :].astype(F32)
    per = dim // lanes
    for g in range(2):
        gains_ref[g : g + 1, :] = jnp.concatenate(
            [gains[g * per + k : g * per + k + 1, :] for k in range(per)], axis=1
        )
    for m in range(n_rep):
        hat, _ = hat_of(refs_x[m][...].astype(F32))
        a_ref[m * rows : (m + 1) * rows, :] = (hat * gains_ref[0:1, :]).astype(BF16)
    step = 2 * rows if n_rep % 2 == 0 else rows
    for r0 in range(0, n_rep * rows, step):
        sl = slice(r0, r0 + step)
        proj = dot(a_ref[sl, :], w_ref[...])
        cos = tile_lanes(cos_ref[sl, :], width)
        sin = tile_lanes(sin_ref[sl, :], width)
        query = proj[:, :width]
        key = proj[:, width : 2 * width]
        query = (query * cos + partner(query) * sin).astype(BF16).astype(F32)
        q_ref[sl, :] = (query * HEAD_DIM**-0.5).astype(BF16)
        kv_ref[sl, :width] = (key * cos + partner(key) * sin).astype(BF16)
        kv_ref[sl, width:] = proj[:, 2 * width :].astype(BF16)


def attend_kernel(n_part, q_ref, refs_kv, o_ref, lse_ref, k_scr, vt_scr):
    rows, width = q_ref.shape
    keys = refs_kv[0].shape[0]
    for l in range(n_part):
        k_scr[l * keys : (l + 1) * keys, :] = refs_kv[l][:, :width]
        vt_scr[:, l * keys : (l + 1) * keys] = refs_kv[l][:, width:].astype(F32).T.astype(BF16)
    heads = width // HEAD_DIM
    step = min(256, rows)

    def body(c, carry):
        r0 = pl.multiple_of(c * step, step)
        for h in range(heads):
            pair = h // 2 * 128
            q = q_ref[pl.ds(r0, step), pair : pair + 128] * head_mask(h % 2, 128)
            s = dot_nt(k_scr[:, pair : pair + 128], q)
            top = jnp.max(s, axis=0, keepdims=True)
            e = jnp.exp(s - top)
            mass = jnp.sum(e, axis=0, keepdims=True)
            lse_ref[h : h + 1, pl.ds(r0, step)] = top + jnp.log(mass)
            ot = dot(vt_scr[h * HEAD_DIM : (h + 1) * HEAD_DIM, :], e.astype(BF16)) / mass
            ot_list.append(ot)
            if h % 2 == 1:
                both = jnp.concatenate(ot_list, axis=0)
                o_ref[pl.ds(r0, step), pair : pair + 128] = both.T.astype(BF16)
                ot_list.clear()
        return carry

    ot_list = []
    lax.fori_loop(0, rows // step, body, 0)


def ff_kernel(
    n_rep, n_part, pitch, at_ref, refs_x, refs_o, refs_wo, refs_wo_other, ffw_ref, refs_c, gains_ref,
    r_ref, refs_da, a_ref, m_ref, du_ref, c_ref, o_ref, wout_ref, wdown_ref, gain_ref,
    hat_scr, u_scr, dm_scr, win_scr,
):
    rows, dim = refs_x[0].shape
    total = n_rep * rows
    quarter = refs_o[0].shape[1]
    j = at_ref[0]
    n_inner = n_rep * n_part
    w_rows = dim // n_inner
    lanes = win_scr.shape[1]
    extra, spots = packed_rows(pitch, dim, lanes)
    for k in range(n_rep):
        col = pl.multiple_of((j ^ k) * quarter, quarter)
        for l in range(n_part):
            for m in range(n_rep):
                row = pl.multiple_of((m * n_part + (at_ref[2] ^ l)) * w_rows, w_rows)
                if l == 0:
                    piece = refs_wo[k][m * w_rows : (m + 1) * w_rows, :]
                else:
                    at = (k * n_rep + m) * w_rows
                    piece = refs_wo_other[l - 1][at : at + w_rows, :]
                wout_ref[pl.ds(row, w_rows), pl.ds(col, quarter)] = piece
    for m in range(n_rep):
        hat_scr[m * rows : (m + 1) * rows, :] = refs_x[m][...].astype(F32)
        c_ref[m * rows : (m + 1) * rows, :] = refs_c[m][...]
        col = pl.multiple_of((j ^ m) * quarter, quarter)
        for k in range(n_rep):
            at = (k ^ m) * rows
            o_ref[k * rows : (k + 1) * rows, pl.ds(col, quarter)] = refs_o[m][at : at + rows, :]
    for p in range(n_inner):
        base = p * (w_rows + extra)
        win_scr[p * w_rows : (p + 1) * w_rows, :] = ffw_ref[base : base + w_rows, :]
        for row, lane, row_in, col_in, n, w in spots:
            top = base + w_rows + row
            wdown_ref[p * pitch + row_in : p * pitch + row_in + n, col_in : col_in + w] = ffw_ref[
                top : top + n, lane : lane + w
            ]
    hat_scr[...] += dot(o_ref[...], wout_ref[...])
    r_ref[...] = hat_scr[:rows, :]
    gain = gains_ref[1:2, :]

    def norm_step(c, carry):
        r0 = pl.multiple_of(c * 64, 64)
        hat, _ = hat_of(hat_scr[pl.ds(r0, 64), :])
        hat_scr[pl.ds(r0, 64), :] = hat
        a_ref[pl.ds(r0, 64), :] = (hat * gain).astype(BF16)
        return carry

    lax.fori_loop(0, total // 64, norm_step, 0)
    u_scr[...] = dot(a_ref[...], win_scr[...])
    dm_scr[...] = dot_nt(c_ref[...], wdown_ref[...])
    width = m_ref.shape[1]

    def gate_step(c, carry):
        sl = pl.ds(pl.multiple_of(c * 32, 32), 32)
        pre = u_scr[sl, :width]
        gate = u_scr[sl, width:]
        dm = dm_scr[sl, :]
        cdf = 0.5 * (1.0 + lax.erf(pre * (0.5**0.5)))
        pdf = jnp.exp(-0.5 * pre * pre) * 0.3989422804014327
        act = pre * cdf
        m_ref[sl, :] = (act * gate).astype(BF16)
        du_ref[sl, :width] = (dm * gate * (cdf + pre * pdf)).astype(BF16)
        du_ref[sl, width:] = (dm * act).astype(BF16)
        return carry

    lax.fori_loop(0, total // 32, gate_step, 0)
    total_gain = jnp.zeros((1, dim), F32)
    for m in range(n_rep):
        sl = slice(m * rows, (m + 1) * rows)
        da = dot_nt(du_ref[sl, :], win_scr[...])
        refs_da[m][...] = da.astype(BF16)
        total_gain = total_gain + jnp.sum(da * hat_scr[sl, :], axis=0, keepdims=True)
    gain_ref[...] = total_gain


def ff_grads_kernel(n_rep, n_inner, pitch, m_ref, wdown_ref, c_ref, a_ref, du_ref, refs_lo, grad_ref, down_scr):
    rows, dim = refs_lo[0].shape
    w_rows = dim // n_inner
    lanes = du_ref.shape[1]
    extra, spots = packed_rows(pitch, dim, lanes)
    high = w_rows + extra
    down_scr[...] = dot_tn(m_ref[...], c_ref[...]).astype(BF16)
    din = dot_tn(a_ref[...], du_ref[...]).astype(BF16)
    for p in range(n_inner):
        grad_ref[p * high : p * high + w_rows, :] = din[p * w_rows : (p + 1) * w_rows, :]
        for row, lane, row_in, col_in, n, w in spots:
            top = p * high + w_rows + row
            grad_ref[top : top + n, lane : lane + w] = down_scr[
                p * pitch + row_in : p * pitch + row_in + n, col_in : col_in + w
            ]
    for m in range(n_rep):
        refs_lo[m][...] = dot(m_ref[m * rows : (m + 1) * rows, :], wdown_ref[...]).astype(BF16)


def norm_back(values, gain, grad):
    hat, inv = hat_of(values)
    dhat = grad * gain
    return inv * (
        dhat
        - jnp.mean(dhat, axis=-1, keepdims=True)
        - hat * jnp.mean(dhat * hat, axis=-1, keepdims=True)
    )


def sum_of(refs):
    total = refs[0][...].astype(F32)
    for ref in refs[1:]:
        total = total + ref[...].astype(F32)
    return total


def middle_kernel(n_rep, refs_da, r_ref, c_ref, gains_ref, dr_ref, dz_ref):
    dr = c_ref[...].astype(F32) + norm_back(r_ref[...], gains_ref[1:2, :], sum_of(refs_da))
    dr_ref[...] = dr
    dz_ref[...] = dr.astype(BF16)


def last_kernel(n_rep, at_ref, refs_da, refs_lo, x_ref, dr_ref, r_ref, gains_ref, outs, scr):
    rows = x_ref.shape[0]
    sub = rows // n_rep
    scr[...] = r_ref[...] + sum_of(refs_lo)
    send_back(n_rep, at_ref, scr, outs, sub)
    back = norm_back(x_ref[...].astype(F32), gains_ref[0:1, :], sum_of(refs_da))
    scr[...] = dr_ref[...] + back
    send_back(n_rep, at_ref, scr, outs, 0)


def attend_back_kernel(
    n_rep, n_part, sub_j, refs_dz, wout_ref, o_ref, q_ref, refs_kv, lse_ref, cos_ref, sin_ref,
    dq_ref, dkv_ref, refs_send, dz_ref, do_scr, k_scr, v_scr, kt_scr, delta_scr, dk_scr, dv_scr,
):
    rows, width = q_ref.shape
    keys = refs_kv[0].shape[0]
    part = refs_dz[0].shape[0]
    j = sub_j[0]
    for m in range(n_rep):
        dz_ref[m * part : (m + 1) * part, :] = refs_dz[m][...]
    start = pl.multiple_of(j * width, width)
    dout = dot_nt(dz_ref[...], wout_ref[pl.ds(start, width), :]).astype(BF16)
    do_scr[...] = dout
    prod_t = (dout.astype(F32) * o_ref[...].astype(F32)).T
    heads = width // HEAD_DIM
    for h in range(heads):
        delta_scr[h : h + 1, :] = jnp.sum(
            prod_t[h * HEAD_DIM : (h + 1) * HEAD_DIM, :], axis=0, keepdims=True
        )
    for l in range(n_part):
        sl = slice(l * keys, (l + 1) * keys)
        k_scr[sl, :] = refs_kv[l][:, :width]
        v_scr[sl, :] = refs_kv[l][:, width:]
        kt_scr[:, sl] = refs_kv[l][:, :width].astype(F32).T.astype(BF16)
    dk_scr[...] = jnp.zeros_like(dk_scr)
    dv_scr[...] = jnp.zeros_like(dv_scr)
    step = min(256, rows)

    def body(c, carry):
        r0 = pl.multiple_of(c * step, step)
        for h in range(heads):
            pair = h // 2 * 128
            lanes = slice(pair, pair + 128)
            mask = head_mask(h % 2, 128)
            q = q_ref[pl.ds(r0, step), lanes] * mask
            do = do_scr[pl.ds(r0, step), lanes] * mask
            p = jnp.exp(dot_nt(k_scr[:, lanes], q) - lse_ref[h : h + 1, pl.ds(r0, step)])
            dp = dot_nt(v_scr[:, lanes], do)
            ds = (p * (dp - delta_scr[h : h + 1, pl.ds(r0, step)])).astype(BF16)
            dv_scr[:, lanes] += dot(p.astype(BF16), do)
            dk_scr[:, lanes] += dot(ds, q)
            dq_list.append(dot(kt_scr[h * HEAD_DIM : (h + 1) * HEAD_DIM, :], ds))
            if h % 2 == 1:
                dq = jnp.concatenate(dq_list, axis=0).T * HEAD_DIM**-0.5
                dq_list.clear()
                cos = cos_ref[pl.ds(r0, step), :]
                sin = sin_ref[pl.ds(r0, step), :]
                dq_ref[pl.ds(r0, step), lanes] = (dq * cos - partner(dq) * sin).astype(BF16)
        return carry

    dq_list = []
    lax.fori_loop(0, rows // step, body, 0)
    dkv_ref[:, :width] = dk_scr[:keys, :]
    dkv_ref[:, width:] = dv_scr[:keys, :]
    for l in range(1, n_part):
        sl = slice(l * keys, (l + 1) * keys)
        refs_send[l - 1][:, :width] = dk_scr[sl, :].astype(BF16)
        refs_send[l - 1][:, width:] = dv_scr[sl, :].astype(BF16)


def out_grad_kernel(sub_j, o_ref, dz_ref, dout_ref):
    quarter = dout_ref.shape[1]
    cols = dz_ref[:, pl.ds(pl.multiple_of(sub_j[0] * quarter, quarter), quarter)]
    dout_ref[...] = dot_tn(o_ref[...], cols).astype(BF16)


def qkv_back_kernel(
    n_rep, n_inner, dq_ref, dkv_ref, refs_got, cos_ref, sin_ref, a_ref, w_ref, refs_x, dout_ref,
    gain_two_ref, grad_ref, refs_da, dp_scr,
):
    width = dq_ref.shape[1]
    rows, dim = refs_x[0].shape
    lanes = 4 * width
    high = grad_ref.shape[0] // n_inner
    w_rows = high - 8
    dkv = dkv_ref[...]
    for got in refs_got:
        dkv = dkv + got[...].astype(F32)
    dk = dkv[:, :width]
    cos = tile_lanes(cos_ref[...], width)
    sin = tile_lanes(sin_ref[...], width)
    dp_scr[:, :width] = dq_ref[...]
    dp_scr[:, width : 2 * width] = (dk * cos - partner(dk) * sin).astype(BF16)
    dp_scr[:, 2 * width :] = dkv[:, width:].astype(BF16)
    grad = dot_tn(a_ref[...], dp_scr[...]).astype(BF16)
    gain = jnp.zeros((1, dim), F32)
    for m in range(n_rep):
        da = dot_nt(dp_scr[m * rows : (m + 1) * rows, :], w_ref[...])
        refs_da[m][...] = da.astype(BF16)
        hat, _ = hat_of(refs_x[m][...].astype(F32))
        gain = gain + jnp.sum(da * hat, axis=0, keepdims=True)
    per = dim // lanes
    strips = [g[:, k * lanes : (k + 1) * lanes] for g in (gain, gain_two_ref[...]) for k in range(per)]
    strips.append(jnp.zeros((8 - len(strips), lanes), F32))
    gains = jnp.concatenate(strips, axis=0).astype(BF16)
    for p in range(n_inner):
        sl = slice(p * w_rows, (p + 1) * w_rows)
        grad_ref[p * high : p * high + w_rows, : 3 * width] = grad[sl, :]
        grad_ref[p * high : p * high + w_rows, 3 * width :] = dout_ref[sl, :]
        grad_ref[p * high + w_rows : (p + 1) * high, :] = gains


def grads_kernel(n_rep, at_ref, pieces, qkv_ref, out_ref, gains_ref):
    width = pieces[0].shape[1] // 4
    rows, dim = out_ref.shape
    for m in range(n_rep):
        for p in range(3):
            start = pl.multiple_of(p * dim + (at_ref[0] ^ m) * width, width)
            qkv_ref[:, pl.ds(start, width)] = pieces[m][:rows, p * width : (p + 1) * width].astype(F32)
        start = pl.multiple_of((at_ref[0] ^ m) * width, width)
        out_ref[:, pl.ds(start, width)] = pieces[m][:rows, 3 * width :].astype(F32)
    gains = pieces[0][rows:, :].astype(F32)
    for m in range(1, n_rep):
        gains = gains + pieces[m][rows:, :].astype(F32)
    gains_ref[...] = gains


def ff_out_kernel(n_rep, unit, pitch, scr, in_ref, down_ref, down_scr):
    _, high, lanes = scr.shape
    rows = in_ref.shape[0]
    shard, dim = down_ref.shape
    _, spots = packed_rows(pitch, dim, lanes)
    strips = []
    for jj in range(n_rep):
        size = min(unit, shard - jj * unit)
        for row, lane, row_in, col_in, n, w in spots:
            down_scr[row_in : row_in + n, col_in : col_in + w] = scr[
                jj, rows + row : rows + row + n, lane : lane + w
            ].astype(F32)
        down_ref[jj * unit : jj * unit + size, :] = down_scr[:size, :]
    for p in range(lanes // pitch):
        strips = []
        for jj in range(n_rep):
            size = min(unit, shard - jj * unit)
            strips.append(scr[jj, :rows, p * pitch : p * pitch + size].astype(F32))
        in_ref[:, p * shard : (p + 1) * shard] = jnp.concatenate(strips, axis=1)


def split_refs(counts, refs):
    out, at = [], 0
    for n in counts:
        if n is None:
            out.append(refs[at])
            at += 1
        else:
            out.append(list(refs[at : at + n]))
            at += n
    return out


def grouped(kernel, static, counts):
    def body(*refs):
        kernel(*static, *split_refs(counts, refs))

    return body


def on_device(
    n_rep, n_inner,
    tokens, cotangent, qkv_weight, out_weight, in_weight, down_weight, gain_one, gain_two,
):
    part = n_inner // n_rep
    rows, dim = tokens.shape
    sub = rows // n_rep
    w_rows = qkv_weight.shape[0]
    width = dim // n_rep
    lanes = 4 * width
    high = w_rows + 8
    ff_shard = down_weight.shape[0]
    unit = -(-ff_shard // n_rep)
    pitch = -(-unit // 16) * 16
    ff = pitch * n_inner
    ff_high = w_rows + pitch * dim // (2 * ff)
    total = n_rep * rows
    j = lax.axis_index("rep")
    i = lax.axis_index("inner")
    s = i // part
    t = i % part
    at = jnp.stack([j, s, t]).astype(jnp.int32)

    def rep_swap(x, m):
        return lax.ppermute(x, "rep", [(a, a ^ m) for a in range(n_rep)])

    def plane_swap(x, m):
        pairs = [(a * part + b, (a ^ m) * part + b) for a in range(n_rep) for b in range(part)]
        return lax.ppermute(x, "inner", pairs)

    def part_swap(x, l):
        pairs = [(a * part + b, a * part + (b ^ l)) for a in range(n_rep) for b in range(part)]
        return lax.ppermute(x, "inner", pairs)

    def rep_gather(x):
        return [x] + [rep_swap(x, m) for m in range(1, n_rep)]

    def rep_trade(pieces):
        return [pieces[0]] + [rep_swap(pieces[m], m) for m in range(1, n_rep)]

    def plane_trade(pieces):
        return [pieces[0]] + [plane_swap(pieces[m], m) for m in range(1, n_rep)]

    def send_home(pieces):
        got = []
        for k in range(n_rep):
            pairs = []
            for a in range(n_rep):
                for z in range(n_rep):
                    for b in range(part):
                        pairs.append((a * n_inner + z * part + b, z * n_inner + (a ^ k) * part + b))
            got.append(lax.ppermute(pieces[k], ("rep", "inner"), pairs))
        return got

    home = [((2 * sub, dim), BF16)] * n_rep
    planes = [[z * part + b for z in range(n_rep)] for b in range(part)]

    (w_pack,) = call(
        functools.partial(weight_kernel, n_inner, part), [((high, lanes), BF16)],
        [at, qkv_weight, out_weight, jnp.stack([gain_one, gain_two])], n_smem=1,
    )
    w_all = lax.all_gather(w_pack, "inner", axis=0, tiled=True)
    x_first = lax.all_to_all(after(tokens, w_pack), "rep", 0, 0, tiled=True)
    in_late = after(in_weight, x_first)
    x_own = lax.all_to_all(x_first, "inner", 0, 0, axis_index_groups=planes, tiled=True)
    c_first = lax.all_to_all(after(cotangent, x_first), "rep", 0, 0, tiled=True)
    x_own = after(x_own, c_first)
    c_own = lax.all_to_all(after(c_first, x_own), "inner", 0, 0, axis_index_groups=planes, tiled=True)
    xs = rep_gather(x_own)
    (ff_pack,) = call(
        grouped(ff_weight_kernel, (n_rep, unit, pitch), (None,) * 5),
        [((ff_high, 2 * ff), BF16)],
        [at, in_late, down_weight, w_pack],
        [((pitch, dim), BF16)],
        n_smem=1, n_any=1,
    )
    ff_w = lax.all_gather(ff_pack, "inner", axis=0, tiled=True)

    own = w_all.reshape(n_rep, part, high, lanes)
    own = lax.dynamic_slice_in_dim(own, t, 1, 1)[:, 0, :w_rows, 3 * width :].reshape(n_rep * w_rows, width)
    wo_own = rep_gather(after(own, xs[-1]))
    wo_other = [part_swap(jnp.concatenate(wo_own, axis=0), l) for l in range(1, part)]

    order = jnp.arange(total, dtype=jnp.int32)
    spot = ((order // sub % n_rep) * part + t) * rows + (j ^ (order // rows)) * sub + order % sub
    inv_freq = 1.0 / THETA ** (jnp.arange(HEAD_DIM // 2, dtype=F32) * (2.0 / HEAD_DIM))
    angle = spot.astype(F32)[:, None] * inv_freq[None, :]
    cos_half, sin_half = jnp.cos(angle), jnp.sin(angle)
    cos = jnp.concatenate([cos_half] * 4, axis=1)
    sin = jnp.concatenate([-sin_half, sin_half] * 2, axis=1)

    q, kv, a_one, w_qkv, gains = call(
        grouped(qkv_kernel, (n_rep, part), (n_rep,) + (None,) * 8),
        [
            ((total, width), BF16), ((total, 2 * width), BF16), ((total, dim), BF16),
            ((dim, 3 * width), BF16), ((2, dim), F32),
        ],
        [*xs, w_all, cos, sin, c_own],
        n_any=1, micros=4,
    )
    kvs = [kv] + [part_swap(kv, l) for l in range(1, part)]
    heads = width // HEAD_DIM
    stat_rows = -(-heads // 8) * 8
    o, lse = call(
        grouped(attend_kernel, (part,), (None, part) + (None,) * 4),
        [((total, width), BF16), ((stat_rows, total), F32)],
        [q, *kvs],
        [((total * part, width), BF16), ((width, total * part), BF16)],
        micros=8,
    )
    os_ = rep_gather(o)
    cs = rep_gather(after(c_own, xs[-1]))
    ff_out = call(
        grouped(
            ff_kernel, (n_rep, part, pitch),
            (None, n_rep, n_rep, n_rep, part - 1, None, n_rep, None, None, n_rep) + (None,) * 12,
        ),
        [((rows, dim), F32)]
        + [((rows, dim), BF16)] * n_rep
        + [
            ((total, dim), BF16), ((total, ff), BF16), ((total, 2 * ff), BF16), ((total, dim), BF16),
            ((total, dim), BF16), ((dim, dim), BF16), ((ff, dim), BF16), ((1, dim), F32),
        ],
        [at, *xs, *os_, *wo_own, *wo_other, ff_w, *cs, gains],
        [((total, dim), F32), ((total, 2 * ff), F32), ((total, ff), F32), ((dim, 2 * ff), BF16)],
        n_smem=1, micros=14,
    )
    r_own, da_two = ff_out[0], ff_out[1 : 1 + n_rep]
    a_two, gated, d_hidden, c_all, o_all, w_out, w_down, gain_two_part = ff_out[1 + n_rep :]
    das = rep_trade(da_two)
    ff_back = call(
        grouped(ff_grads_kernel, (n_rep, n_inner, pitch), (None,) * 5 + (n_rep, None, None)),
        [((rows, dim), BF16)] * n_rep + [((n_inner * ff_high, 2 * ff), BF16)],
        [gated, w_down, c_all, a_two, d_hidden],
        [((ff, dim), BF16)],
        micros=30,
    )
    lo, ff_grad = ff_back[:-1], ff_back[-1]
    dr, dz = call(
        grouped(middle_kernel, (n_rep,), (n_rep,) + (None,) * 5),
        [((rows, dim), F32), ((rows, dim), BF16)],
        [*das, r_own, c_own, gains, ff_grad],
        n_any=1, micros=2,
    )
    ff_grad = lax.psum_scatter(after(ff_grad, *das[1:]), "inner", scatter_dimension=0, tiled=True)
    dzs = rep_gather(dz)

    back = call(
        grouped(
            attend_back_kernel,
            (n_rep, part),
            (None, n_rep, None, None, None, part, None, None, None, None, None, part - 1, None) + (None,) * 7,
        ),
        [((total, width), BF16), ((total, 2 * width), F32)]
        + [((total, 2 * width), BF16)] * (part - 1)
        + [((total, dim), BF16)],
        [at, *dzs, w_out, o, q, *kvs, lse, cos, sin],
        [
            ((total, width), BF16), ((total * part, width), BF16), ((total * part, width), BF16),
            ((width, total * part), BF16), ((stat_rows, total), F32),
            ((total * part, width), F32), ((total * part, width), F32),
        ],
        n_smem=1, micros=10,
    )
    dq, dkv, sends, dz_all = back[0], back[1], back[2:-1], back[-1]
    los = rep_trade([after(x, dzs[-1]) for x in lo])
    gots = [part_swap(after(x, *los[1:]), l + 1) for l, x in enumerate(sends)]
    (d_out,) = call(
        out_grad_kernel, [((dim, width), BF16)], [at, o_all, dz_all], n_smem=1, micros=2,
    )
    qkv_out = call(
        grouped(qkv_back_kernel, (n_rep, n_inner), (None, None, part - 1) + (None,) * 4 + (n_rep,) + (None,) * 3 + (n_rep, None)),
        [((n_inner * high, lanes), BF16)] + [((rows, dim), BF16)] * n_rep,
        [dq, dkv, *gots, cos, sin, a_one, w_qkv, *xs, d_out, gain_two_part],
        [((total, 3 * width), BF16)],
        micros=6,
    )
    das = rep_trade(qkv_out[1:])
    ff_grad = after(ff_grad, *das[1:])
    d_pack = lax.psum_scatter(after(qkv_out[0], ff_grad), "inner", scatter_dimension=0, tiled=True)
    parts = call(
        grouped(last_kernel, (n_rep,), (None, n_rep, n_rep, None, None, None, None, n_rep, None)),
        home, [at, *das, *los, xs[0], dr, r_own, gains], [((rows, dim), F32)], n_smem=1, micros=2,
    )
    ff_grads = jnp.concatenate([after(ff_grad, *das[1:])] * n_rep, axis=0)
    ff_grads = lax.all_to_all(ff_grads, "rep", 0, 0, tiled=True).reshape(n_rep, ff_high, 2 * ff)
    back_home = send_home(parts)
    quarter = after(d_pack, *back_home)
    input_grad, layer_out = call(
        grouped(place_kernel, (n_rep,), (None, n_rep, None, None)),
        [((rows, dim), BF16)] * 2, [at, *back_home, d_pack], n_smem=1, n_any=1,
    )
    g_qkv, g_out, g_gains = call(
        grouped(grads_kernel, (n_rep,), (None, n_rep, None, None, None)),
        [((w_rows, 3 * dim), F32), ((w_rows, dim), F32), ((8, lanes), F32)],
        [at, *rep_gather(quarter)],
        n_smem=1, micros=2,
    )
    g_in, g_down = call(
        grouped(ff_out_kernel, (n_rep, unit, pitch), (None,) * 4),
        [((w_rows, 2 * n_inner * ff_shard), F32), ((ff_shard, dim), F32)],
        [ff_grads, d_pack],
        [((pitch, dim), F32)],
        n_any=1, micros=4,
    )
    gain_grads = g_gains[: 2 * dim // lanes].reshape(2, dim)
    gain_grads = lax.dynamic_slice_in_dim(gain_grads, i * w_rows, w_rows, 1)
    return (layer_out, input_grad, g_qkv, g_out, g_in, g_down, gain_grads[0], gain_grads[1])


def solution(mesh):
    rows = P(("rep", "inner"), None)
    weight = P("inner", None)
    return jax.shard_map(
        functools.partial(on_device, mesh.shape["rep"], mesh.shape["inner"]),
        mesh=mesh,
        in_specs=(rows, rows, weight, weight, weight, weight, P("inner"), P("inner")),
        out_specs=(rows, rows, weight, weight, weight, weight, P("inner"), P("inner")),
        check_vma=False,
    )
```

```python
import functools
import math

import jax
import jax.numpy as jnp
from jax import lax
from jax.experimental import pallas as pl
from jax.experimental.pallas import tpu as pltpu
from jax.sharding import PartitionSpec as P

HEAD_DIM = 64
EPSILON = 1e-05
THETA = 160000.0
F32 = jnp.float32
BF16 = jnp.bfloat16
NT = (((1,), (1,)), ((), ()))
TN = (((0,), (0,)), ((), ()))
VMEM_SPARE = 8 * 1024 * 1024
VMEM_WHOLE = 60 * 1024 * 1024


def dot(a, b):
    return jnp.dot(a, b, preferred_element_type=F32)


def dot_nt(a, b):
    return lax.dot_general(a, b, NT, preferred_element_type=F32)


def dot_tn(a, b):
    return lax.dot_general(a, b, TN, preferred_element_type=F32)


def call(body, outs, args, scratch=(), n_smem=0, n_any=0, far=(), far_outs=(), n_sems=0, whole=False, micros=1):
    n_passed = len(args) - n_any
    spaces = [pltpu.SMEM] * n_smem + [pltpu.VMEM] * (n_passed - n_smem) + [pltpu.HBM] * n_any
    for k in far:
        spaces[k] = pltpu.HBM
    held = sum(math.prod(s) * jnp.dtype(d).itemsize for s, d in scratch)

    def without_waited(*refs):
        body(*refs[:n_passed], *refs[len(args) :])

    return pl.pallas_call(
        without_waited,
        out_shape=[jax.ShapeDtypeStruct(s, d) for s, d in outs],
        in_specs=[pl.BlockSpec(memory_space=space) for space in spaces],
        out_specs=[pl.BlockSpec(memory_space=pltpu.HBM if k in far_outs else pltpu.VMEM) for k in range(len(outs))],
        scratch_shapes=[pltpu.VMEM(s, d) for s, d in scratch]
        + ([pltpu.SemaphoreType.DMA((n_sems,))] if n_sems else []),
        compiler_params=pltpu.CompilerParams(vmem_limit_bytes=VMEM_WHOLE if whole else held + VMEM_SPARE),
        cost_estimate=pl.CostEstimate(
            flops=int(micros * 1e9), transcendentals=0, bytes_accessed=int(micros * 1e6)
        ),
    )(*args)


class Copies:
    def __init__(self, sems):
        self.sems = sems
        self.used = 0

    def start(self, source, target):
        copy = pltpu.make_async_copy(source, target, self.sems.at[self.used])
        self.used += 1
        copy.start()
        return copy


def wait_all(copies):
    for copy in copies:
        copy.wait()


def after(value, *others):
    return lax.optimization_barrier((value, *others))[0]


def hat_of(values):
    centred = values - jnp.mean(values, axis=-1, keepdims=True)
    inv = lax.rsqrt(jnp.mean(centred * centred, axis=-1, keepdims=True) + EPSILON)
    return centred * inv, inv


def spot(block, size):
    return pl.ds(pl.multiple_of(block * size, size), size)


def partner(x):
    width = x.shape[-1]
    half = HEAD_DIM // 2
    lane = lax.broadcasted_iota(jnp.int32, x.shape, x.ndim - 1)
    ahead = pltpu.roll(x, width - half, 1)
    behind = pltpu.roll(x, half, 1)
    return jnp.where(lane % HEAD_DIM < half, ahead, behind)


def tile_lanes(table, width):
    return jnp.concatenate([table] * (width // table.shape[-1]), axis=-1)


def head_mask(h, width):
    lane = lax.broadcasted_iota(jnp.int32, (1, width), 1)
    return ((lane >= h * HEAD_DIM) & (lane < (h + 1) * HEAD_DIM)).astype(BF16)


def place_kernel(n_rep, at_ref, pieces, first_ref, second_ref):
    sub = pieces[0].shape[0] // 2
    for k in range(n_rep):
        spot = pl.ds(pl.multiple_of((at_ref[1] ^ k) * sub, sub), sub)
        first_ref[spot, :] = pieces[k][:sub, :]
        second_ref[spot, :] = pieces[k][sub:, :]


def send_back(n_rep, at_ref, scr, outs, first):
    sub = outs[0].shape[0] // 2
    for k in range(n_rep):
        block = at_ref[0] ^ k
        outs[k][first : first + sub, :] = scr[pl.ds(pl.multiple_of(block * sub, sub), sub), :].astype(BF16)


def weight_kernel(n_inner, n_part, at_ref, qkv_ref, out_ref, gains_ref, pack_ref):
    rows, dim = out_ref.shape
    lanes = pack_ref.shape[1]
    width = lanes // 4
    for p in range(3):
        start = pl.multiple_of(p * dim + at_ref[0] * width, width)
        pack_ref[:rows, p * width : (p + 1) * width] = qkv_ref[:, pl.ds(start, width)]
    start = pl.multiple_of(at_ref[0] * width, width)
    pack_ref[:rows, 3 * width :] = out_ref[:, pl.ds(start, width)]
    shard = lax.broadcasted_iota(jnp.int32, (2, dim), 1) // rows
    own = jnp.concatenate([gains_ref[...].astype(F32)] * n_inner, axis=1)
    own = jnp.where(shard == at_ref[1] * n_part + at_ref[2], own, 0.0)
    strips = [own[g : g + 1, k * lanes : (k + 1) * lanes] for g in range(2) for k in range(dim // lanes)]
    strips.append(jnp.zeros((8 - len(strips), lanes), F32))
    pack_ref[rows:, :] = jnp.concatenate(strips, axis=0).astype(BF16)


def packed_rows(pitch, dim, lanes):
    extra = pitch * dim // lanes
    spots = [(0, 0, 0, 0, extra, min(dim, lanes))]
    left = lanes - dim
    if left:
        rest = pitch - extra
        for c in range(dim // left):
            spots.append((c * rest, dim, extra, c * left, rest, left))
    return extra, spots


def ff_weight_kernel(n_rep, unit, pitch, at_ref, in_ref, down_ref, pack_ref, down_scr):
    rows = in_ref.shape[0]
    shard, dim = down_ref.shape
    lanes = pack_ref.shape[1]
    for jj in range(n_rep):
        size = min(unit, shard - jj * unit)

        @pl.when(at_ref[0] == jj)
        def _(jj=jj, size=size):
            pieces = []
            for p in range(in_ref.shape[1] // shard):
                first = p * shard + jj * unit
                pieces.append(in_ref[:, first : first + size])
                pieces.append(jnp.zeros((rows, pitch - size), BF16))
            pack_ref[:rows, :] = jnp.concatenate(pieces, axis=1)
            down_scr[:size, :] = down_ref[jj * unit : jj * unit + size, :]
            down_scr[size:, :] = jnp.zeros((pitch - size, dim), BF16)

    _, spots = packed_rows(pitch, dim, lanes)
    for row, lane, row_in, col_in, n, w in spots:
        pack_ref[rows + row : rows + row + n, lane : lane + w] = down_scr[row_in : row_in + n, col_in : col_in + w]


def qkv_kernel(
    n_rep, at_ref, refs_x, pack_ref, cos_ref, sin_ref, q_ref, kv_ref, a_out, w_out, gains_ref,
    a_ref, w_ref, rows_scr, sems,
):
    rows = refs_x[0].shape[0]
    width = q_ref.shape[1]
    dim = a_ref.shape[1]
    lanes = 4 * width
    n_inner, high, _ = pack_ref.shape
    w_rows = high - 8
    copies = Copies(sems)
    gains_in = copies.start(pack_ref.at[:, w_rows:, :], rows_scr)
    weights_in = copies.start(pack_ref.at[:, :w_rows, : 3 * width], w_ref)
    gains_in.wait()
    gains = rows_scr[0].astype(F32)
    for p in range(1, n_inner):
        gains = gains + rows_scr[p].astype(F32)
    per = dim // lanes
    for g in range(2):
        gains_ref[g : g + 1, :] = jnp.concatenate(
            [gains[g * per + k : g * per + k + 1, :] for k in range(per)], axis=1
        )
    for m in range(n_rep):
        hat, _ = hat_of(refs_x[m][...].astype(F32))
        a_ref[spot(at_ref[0] ^ m, rows), :] = (hat * gains_ref[0:1, :]).astype(BF16)
    weights_in.wait()
    done = [copies.start(a_ref, a_out), copies.start(w_ref, w_out)]
    weights = w_ref[...].reshape(dim, 3 * width)
    step = 2 * rows if n_rep % 2 == 0 else rows
    for r0 in range(0, n_rep * rows, step):
        sl = slice(r0, r0 + step)
        proj = dot(a_ref[sl, :], weights)
        cos = tile_lanes(cos_ref[sl, :], width)
        sin = tile_lanes(sin_ref[sl, :], width)
        query = proj[:, :width]
        key = proj[:, width : 2 * width]
        query = (query * cos + partner(query) * sin).astype(BF16).astype(F32)
        q_ref[sl, :] = (query * HEAD_DIM**-0.5).astype(BF16)
        kv_ref[sl, :width] = (key * cos + partner(key) * sin).astype(BF16)
        kv_ref[sl, width:] = proj[:, 2 * width :].astype(BF16)
    wait_all(done)


def attend_kernel(n_part, q_ref, refs_kv, o_ref, lse_ref, k_scr, vt_scr):
    rows, width = q_ref.shape
    keys = refs_kv[0].shape[0]
    for l in range(n_part):
        k_scr[l * keys : (l + 1) * keys, :] = refs_kv[l][:, :width]
        vt_scr[:, l * keys : (l + 1) * keys] = refs_kv[l][:, width:].astype(F32).T.astype(BF16)
    heads = width // HEAD_DIM
    step = min(256, rows)

    def body(c, carry):
        r0 = pl.multiple_of(c * step, step)
        for h in range(heads):
            pair = h // 2 * 128
            q = q_ref[pl.ds(r0, step), pair : pair + 128] * head_mask(h % 2, 128)
            s = dot_nt(k_scr[:, pair : pair + 128], q)
            top = jnp.max(s, axis=0, keepdims=True)
            e = jnp.exp(s - top)
            mass = jnp.sum(e, axis=0, keepdims=True)
            lse_ref[h : h + 1, pl.ds(r0, step)] = top + jnp.log(mass)
            ot = dot(vt_scr[h * HEAD_DIM : (h + 1) * HEAD_DIM, :], e.astype(BF16)) / mass
            ot_list.append(ot)
            if h % 2 == 1:
                both = jnp.concatenate(ot_list, axis=0)
                o_ref[pl.ds(r0, step), pair : pair + 128] = both.T.astype(BF16)
                ot_list.clear()
        return carry

    ot_list = []
    lax.fori_loop(0, rows // step, body, 0)


def ff_kernel(
    n_rep, n_part, at_ref, refs_x, refs_o, refs_wo, refs_wo_other, ffw_ref, refs_c, gains_ref,
    r_ref, refs_da, a_ref, m_ref, du_ref, o_out, wout_out, gain_ref,
    hat_scr, u_scr, dm_scr, win_scr, wdown_scr, x_scr, c_scr, o_scr, wout_scr, sems,
):
    rows, dim = refs_x[0].shape
    total = n_rep * rows
    quarter = refs_o[0].shape[1]
    j, t = at_ref[0], at_ref[2]
    _, w_rows, lanes = win_scr.shape
    copies = Copies(sems)
    first = []
    for m in range(n_rep):
        cols = spot(j ^ m, quarter)
        first.append(copies.start(refs_wo[m], wout_scr.at[:, t, :, cols]))
        for l in range(1, n_part):
            first.append(copies.start(refs_wo_other[l - 1].at[m], wout_scr.at[:, t ^ l, :, cols]))
        first.append(copies.start(refs_o[m], o_scr.at[:, cols]))
        first.append(copies.start(refs_x[m], x_scr.at[spot(j ^ m, rows), :]))
    second = copies.start(ffw_ref.at[:, :w_rows, :], win_scr)
    third = [copies.start(refs_c[m], c_scr.at[spot(j ^ m, rows), :]) for m in range(n_rep)]
    third += copy_down(copies, w_rows, ffw_ref, wdown_scr)
    wait_all(first)
    weights = wout_scr[...].reshape(dim, dim)
    last = [copies.start(o_scr, o_out)]
    hat_scr[...] = x_scr[...].astype(F32) + dot(o_scr[...], weights)
    r_ref[...] = hat_scr[spot(j, rows), :]
    per = quarter // w_rows // n_part
    for k in range(per):
        block = wout_scr.at[pl.ds(j * per + k, 1)]
        last.append(copies.start(block, wout_out.at[pl.ds(k, 1)]))
    gain = gains_ref[1:2, :]

    def norm_step(c, carry):
        r0 = pl.multiple_of(c * 64, 64)
        hat, _ = hat_of(hat_scr[pl.ds(r0, 64), :])
        hat_scr[pl.ds(r0, 64), :] = hat
        a_ref[pl.ds(r0, 64), :] = (hat * gain).astype(BF16)
        return carry

    lax.fori_loop(0, total // 64, norm_step, 0)
    second.wait()
    weights = win_scr[...].reshape(dim, lanes)
    u_scr[...] = dot(a_ref[...], weights)
    wait_all(third)
    dm_scr[...] = dot_nt(c_scr[...], wdown_scr[...].reshape(m_ref.shape[1], dim))
    width = m_ref.shape[1]

    def gate_step(c, carry):
        sl = pl.ds(pl.multiple_of(c * 32, 32), 32)
        pre = u_scr[sl, :width]
        gate = u_scr[sl, width:]
        dm = dm_scr[sl, :]
        cdf = 0.5 * (1.0 + lax.erf(pre * (0.5**0.5)))
        pdf = jnp.exp(-0.5 * pre * pre) * 0.3989422804014327
        act = pre * cdf
        m_ref[sl, :] = (act * gate).astype(BF16)
        du_ref[sl, :width] = (dm * gate * (cdf + pre * pdf)).astype(BF16)
        du_ref[sl, width:] = (dm * act).astype(BF16)
        return carry

    lax.fori_loop(0, total // 32, gate_step, 0)
    u_scr[:, :dim] = dot_nt(du_ref[...], win_scr[...].reshape(dim, lanes))
    total_gain = jnp.zeros((1, dim), F32)
    for m in range(n_rep):
        sl = spot(j ^ m, rows)
        da = u_scr[sl, :dim]
        refs_da[m][...] = da.astype(BF16)
        total_gain = total_gain + jnp.sum(da * hat_scr[sl, :], axis=0, keepdims=True)
    gain_ref[...] = total_gain
    wait_all(last)


def copy_down(copies, w_rows, ffw_ref, wdown_scr):
    _, pitch, dim = wdown_scr.shape
    _, spots = packed_rows(pitch, dim, ffw_ref.shape[2])
    started = []
    for row, lane, row_in, col_in, n, w in spots:
        source = ffw_ref.at[:, w_rows + row : w_rows + row + n, lane : lane + w]
        started.append(copies.start(source, wdown_scr.at[:, row_in : row_in + n, col_in : col_in + w]))
    return started


def ff_grads_kernel(
    n_rep, at_ref, m_ref, ffw_ref, refs_c, a_ref, du_ref, refs_lo, grad_out,
    down_scr, wdown_scr, c_scr, din_scr, sems,
):
    rows, dim = refs_lo[0].shape
    n_inner, w_rows, lanes = din_scr.shape
    pitch = down_scr.shape[1]
    j = at_ref[0]
    copies = Copies(sems)
    early = [copies.start(refs_c[m], c_scr.at[spot(j ^ m, rows), :]) for m in range(n_rep)]
    late = copy_down(copies, w_rows, ffw_ref, wdown_scr)
    din_scr[...] = dot_tn(a_ref[...], du_ref[...]).astype(BF16).reshape(n_inner, w_rows, lanes)
    sent = [copies.start(din_scr, grad_out.at[:, :w_rows, :])]
    wait_all(early)
    down_scr[...] = dot_tn(m_ref[...], c_scr[...]).astype(BF16).reshape(n_inner, pitch, dim)
    for row, lane, row_in, col_in, n, w in packed_rows(pitch, dim, lanes)[1]:
        source = down_scr.at[:, row_in : row_in + n, col_in : col_in + w]
        sent.append(copies.start(source, grad_out.at[:, w_rows + row : w_rows + row + n, lane : lane + w]))
    wait_all(late)
    down_scr_all = wdown_scr[...].reshape(n_inner * pitch, dim)
    c_scr[...] = dot(m_ref[...], down_scr_all).astype(BF16)
    for m in range(n_rep):
        refs_lo[m][...] = c_scr[spot(j ^ m, rows), :]
    wait_all(sent)


def norm_back(values, gain, grad):
    hat, inv = hat_of(values)
    dhat = grad * gain
    return inv * (
        dhat
        - jnp.mean(dhat, axis=-1, keepdims=True)
        - hat * jnp.mean(dhat * hat, axis=-1, keepdims=True)
    )


def sum_of(refs):
    total = refs[0][...].astype(F32)
    for ref in refs[1:]:
        total = total + ref[...].astype(F32)
    return total


def middle_kernel(n_rep, refs_da, r_ref, c_ref, gains_ref, dr_ref, dz_ref):
    dr = c_ref[...].astype(F32) + norm_back(r_ref[...], gains_ref[1:2, :], sum_of(refs_da))
    dr_ref[...] = dr
    dz_ref[...] = dr.astype(BF16)


def last_kernel(n_rep, at_ref, refs_da, refs_lo, x_ref, dr_ref, r_ref, gains_ref, outs, scr):
    rows = x_ref.shape[0]
    sub = rows // n_rep
    scr[...] = r_ref[...] + sum_of(refs_lo)
    send_back(n_rep, at_ref, scr, outs, sub)
    back = norm_back(x_ref[...].astype(F32), gains_ref[0:1, :], sum_of(refs_da))
    scr[...] = dr_ref[...] + back
    send_back(n_rep, at_ref, scr, outs, 0)


def attend_back_kernel(
    n_rep, n_part, sub_j, refs_dz, wout_ref, o_ref, q_ref, refs_kv, lse_ref, cos_ref, sin_ref,
    dq_ref, dkv_ref, refs_send, dz_ref, do_scr, k_scr, v_scr, kt_scr, delta_scr, dk_scr, dv_scr,
):
    rows, width = q_ref.shape
    keys = refs_kv[0].shape[0]
    part = refs_dz[0].shape[0]
    for m in range(n_rep):
        dz_ref[spot(sub_j[0] ^ m, part), :] = refs_dz[m][...]
    dout = dot_nt(dz_ref[...], wout_ref[...].reshape(width, dz_ref.shape[1])).astype(BF16)
    do_scr[...] = dout
    prod_t = (dout.astype(F32) * o_ref[...].astype(F32)).T
    heads = width // HEAD_DIM
    for h in range(heads):
        delta_scr[h : h + 1, :] = jnp.sum(
            prod_t[h * HEAD_DIM : (h + 1) * HEAD_DIM, :], axis=0, keepdims=True
        )
    for l in range(n_part):
        sl = slice(l * keys, (l + 1) * keys)
        k_scr[sl, :] = refs_kv[l][:, :width]
        v_scr[sl, :] = refs_kv[l][:, width:]
        kt_scr[:, sl] = refs_kv[l][:, :width].astype(F32).T.astype(BF16)
    dk_scr[...] = jnp.zeros_like(dk_scr)
    dv_scr[...] = jnp.zeros_like(dv_scr)
    step = min(256, rows)

    def body(c, carry):
        r0 = pl.multiple_of(c * step, step)
        for h in range(heads):
            pair = h // 2 * 128
            lanes = slice(pair, pair + 128)
            mask = head_mask(h % 2, 128)
            q = q_ref[pl.ds(r0, step), lanes] * mask
            do = do_scr[pl.ds(r0, step), lanes] * mask
            p = jnp.exp(dot_nt(k_scr[:, lanes], q) - lse_ref[h : h + 1, pl.ds(r0, step)])
            dp = dot_nt(v_scr[:, lanes], do)
            ds = (p * (dp - delta_scr[h : h + 1, pl.ds(r0, step)])).astype(BF16)
            dv_scr[:, lanes] += dot(p.astype(BF16), do)
            dk_scr[:, lanes] += dot(ds, q)
            dq_list.append(dot(kt_scr[h * HEAD_DIM : (h + 1) * HEAD_DIM, :], ds))
            if h % 2 == 1:
                dq = jnp.concatenate(dq_list, axis=0).T * HEAD_DIM**-0.5
                dq_list.clear()
                cos = cos_ref[pl.ds(r0, step), :]
                sin = sin_ref[pl.ds(r0, step), :]
                dq_ref[pl.ds(r0, step), lanes] = (dq * cos - partner(dq) * sin).astype(BF16)
        return carry

    dq_list = []
    lax.fori_loop(0, rows // step, body, 0)
    dkv_ref[:, :width] = dk_scr[:keys, :]
    dkv_ref[:, width:] = dv_scr[:keys, :]
    for l in range(1, n_part):
        sl = slice(l * keys, (l + 1) * keys)
        refs_send[l - 1][:, :width] = dk_scr[sl, :].astype(BF16)
        refs_send[l - 1][:, width:] = dv_scr[sl, :].astype(BF16)


def out_grad_kernel(sub_j, o_ref, dz_ref, dout_ref):
    quarter = dout_ref.shape[1]
    cols = dz_ref[:, pl.ds(pl.multiple_of(sub_j[0] * quarter, quarter), quarter)]
    dout_ref[...] = dot_tn(o_ref[...], cols).astype(BF16)


def qkv_back_kernel(
    n_rep, n_part, at_ref, dq_ref, dkv_ref, refs_got, cos_ref, sin_ref, a_ref, w_ref, refs_x, dout_ref,
    gain_two_ref, keep_ref, refs_send, refs_da, dp_scr, da_scr, grad_scr,
):
    width = dq_ref.shape[1]
    rows, dim = refs_x[0].shape
    lanes = 4 * width
    high = keep_ref.shape[0] // n_rep
    w_rows = high - 8
    dkv = dkv_ref[...]
    for got in refs_got:
        dkv = dkv + got[...].astype(F32)
    dk = dkv[:, :width]
    cos = tile_lanes(cos_ref[...], width)
    sin = tile_lanes(sin_ref[...], width)
    dp_scr[:, :width] = dq_ref[...]
    dp_scr[:, width : 2 * width] = (dk * cos - partner(dk) * sin).astype(BF16)
    dp_scr[:, 2 * width :] = dkv[:, width:].astype(BF16)
    grad_scr[:, : 3 * width] = dot_tn(a_ref[...], dp_scr[...]).astype(BF16)
    grad_scr[:, 3 * width :] = dout_ref[...]
    da_scr[...] = dot_nt(dp_scr[...], w_ref[...].reshape(dim, 3 * width))
    gain = jnp.zeros((1, dim), F32)
    for m in range(n_rep):
        da = da_scr[spot(at_ref[0] ^ m, rows), :]
        refs_da[m][...] = da.astype(BF16)
        hat, _ = hat_of(refs_x[m][...].astype(F32))
        gain = gain + jnp.sum(da * hat, axis=0, keepdims=True)
    per = dim // lanes
    strips = [g[:, k * lanes : (k + 1) * lanes] for g in (gain, gain_two_ref[...]) for k in range(per)]
    strips.append(jnp.zeros((8 - len(strips), lanes), F32))
    gains = jnp.concatenate(strips, axis=0).astype(BF16)
    for l in range(n_part):
        ref = keep_ref if l == 0 else refs_send[l - 1]
        for m in range(n_rep):
            shard = m * n_part + (at_ref[2] ^ l)
            ref[m * high : m * high + w_rows, :] = grad_scr[spot(shard, w_rows), :]
            ref[m * high + w_rows : (m + 1) * high, :] = gains


def part_sum_kernel(keep_ref, refs_got, out_ref):
    total = keep_ref[...].astype(F32)
    for got in refs_got:
        total = total + got[...].astype(F32)
    out_ref[...] = total.astype(BF16)


def grads_kernel(n_rep, at_ref, pieces, qkv_ref, out_ref, gains_ref):
    width = pieces[0].shape[1] // 4
    rows, dim = out_ref.shape
    for m in range(n_rep):
        for p in range(3):
            start = pl.multiple_of(p * dim + (at_ref[0] ^ m) * width, width)
            qkv_ref[:, pl.ds(start, width)] = pieces[m][:rows, p * width : (p + 1) * width].astype(F32)
        start = pl.multiple_of((at_ref[0] ^ m) * width, width)
        out_ref[:, pl.ds(start, width)] = pieces[m][:rows, 3 * width :].astype(F32)
    gains = pieces[0][rows:, :].astype(F32)
    for m in range(1, n_rep):
        gains = gains + pieces[m][rows:, :].astype(F32)
    gains_ref[...] = gains


def ff_out_kernel(n_rep, unit, pitch, scr, in_ref, down_ref, down_scr):
    _, high, lanes = scr.shape
    rows = in_ref.shape[0]
    shard, dim = down_ref.shape
    _, spots = packed_rows(pitch, dim, lanes)
    strips = []
    for jj in range(n_rep):
        size = min(unit, shard - jj * unit)
        for row, lane, row_in, col_in, n, w in spots:
            down_scr[row_in : row_in + n, col_in : col_in + w] = scr[
                jj, rows + row : rows + row + n, lane : lane + w
            ].astype(F32)
        down_ref[jj * unit : jj * unit + size, :] = down_scr[:size, :]
    for p in range(lanes // pitch):
        strips = []
        for jj in range(n_rep):
            size = min(unit, shard - jj * unit)
            strips.append(scr[jj, :rows, p * pitch : p * pitch + size].astype(F32))
        in_ref[:, p * shard : (p + 1) * shard] = jnp.concatenate(strips, axis=1)


def split_refs(counts, refs):
    out, at = [], 0
    for n in counts:
        if n is None:
            out.append(refs[at])
            at += 1
        else:
            out.append(list(refs[at : at + n]))
            at += n
    return out


def grouped(kernel, static, counts):
    def body(*refs):
        kernel(*static, *split_refs(counts, refs))

    return body


def on_device(
    n_rep, n_inner,
    tokens, cotangent, qkv_weight, out_weight, in_weight, down_weight, gain_one, gain_two,
):
    part = n_inner // n_rep
    rows, dim = tokens.shape
    sub = rows // n_rep
    w_rows = qkv_weight.shape[0]
    width = dim // n_rep
    lanes = 4 * width
    high = w_rows + 8
    ff_shard = down_weight.shape[0]
    unit = -(-ff_shard // n_rep)
    pitch = -(-unit // 16) * 16
    ff = pitch * n_inner
    ff_high = w_rows + pitch * dim // (2 * ff)
    total = n_rep * rows
    j = lax.axis_index("rep")
    i = lax.axis_index("inner")
    s = i // part
    t = i % part
    at = jnp.stack([j, s, t]).astype(jnp.int32)

    def rep_swap(x, m):
        return lax.ppermute(x, "rep", [(a, a ^ m) for a in range(n_rep)])

    def plane_swap(x, m):
        pairs = [(a * part + b, (a ^ m) * part + b) for a in range(n_rep) for b in range(part)]
        return lax.ppermute(x, "inner", pairs)

    def part_swap(x, l):
        pairs = [(a * part + b, a * part + (b ^ l)) for a in range(n_rep) for b in range(part)]
        return lax.ppermute(x, "inner", pairs)

    def rep_gather(x):
        return [x] + [rep_swap(x, m) for m in range(1, n_rep)]

    def rep_trade(pieces):
        return [pieces[0]] + [rep_swap(pieces[m], m) for m in range(1, n_rep)]

    def plane_trade(pieces):
        return [pieces[0]] + [plane_swap(pieces[m], m) for m in range(1, n_rep)]

    def send_home(pieces):
        got = []
        for k in range(n_rep):
            pairs = []
            for a in range(n_rep):
                for z in range(n_rep):
                    for b in range(part):
                        pairs.append((a * n_inner + z * part + b, z * n_inner + (a ^ k) * part + b))
            got.append(lax.ppermute(pieces[k], ("rep", "inner"), pairs))
        return got

    home = [((2 * sub, dim), BF16)] * n_rep
    planes = [[z * part + b for z in range(n_rep)] for b in range(part)]

    (w_pack,) = call(
        functools.partial(weight_kernel, n_inner, part), [((high, lanes), BF16)],
        [at, qkv_weight, out_weight, jnp.stack([gain_one, gain_two])], n_smem=1,
    )
    w_all = lax.all_gather(w_pack, "inner")
    x_first = lax.all_to_all(after(tokens, w_pack), "rep", 0, 0, tiled=True)
    in_late = after(in_weight, x_first)
    x_own = lax.all_to_all(x_first, "inner", 0, 0, axis_index_groups=planes, tiled=True)
    c_first = lax.all_to_all(after(cotangent, x_first), "rep", 0, 0, tiled=True)
    x_own = after(x_own, c_first)
    c_own = lax.all_to_all(after(c_first, x_own), "inner", 0, 0, axis_index_groups=planes, tiled=True)
    xs = rep_gather(x_own)
    (ff_pack,) = call(
        grouped(ff_weight_kernel, (n_rep, unit, pitch), (None,) * 5),
        [((ff_high, 2 * ff), BF16)],
        [at, in_late, down_weight, w_pack],
        [((pitch, dim), BF16)],
        n_smem=1, n_any=1,
    )
    ff_w = lax.all_gather(ff_pack, "inner")

    own = w_all.reshape(n_rep, part, high, lanes)
    own = lax.dynamic_slice_in_dim(own, t, 1, 1)[:, 0, :w_rows, 3 * width :].reshape(n_rep * w_rows, width)
    wo_own = rep_gather(after(own.reshape(n_rep, w_rows, width), xs[-1]))
    wo_other = [part_swap(jnp.stack(wo_own), l) for l in range(1, part)]

    order = jnp.arange(total, dtype=jnp.int32)
    place = ((order // sub % n_rep) * part + t) * rows + (order // rows) * sub + order % sub
    inv_freq = 1.0 / THETA ** (jnp.arange(HEAD_DIM // 2, dtype=F32) * (2.0 / HEAD_DIM))
    angle = place.astype(F32)[:, None] * inv_freq[None, :]
    cos_half, sin_half = jnp.cos(angle), jnp.sin(angle)
    cos = jnp.concatenate([cos_half] * 4, axis=1)
    sin = jnp.concatenate([-sin_half, sin_half] * 2, axis=1)

    q, kv, a_one, w_qkv, gains = call(
        grouped(qkv_kernel, (n_rep,), (None, n_rep) + (None,) * 12),
        [
            ((total, width), BF16), ((total, 2 * width), BF16), ((total, dim), BF16),
            ((n_inner, w_rows, 3 * width), BF16), ((2, dim), F32),
        ],
        [at, *xs, w_all, cos, sin, c_own],
        [((total, dim), BF16), ((n_inner, w_rows, 3 * width), BF16), ((n_inner, 8, lanes), BF16)],
        n_smem=1, n_any=1, far=(1 + n_rep,), far_outs=(2, 3), n_sems=4, whole=True, micros=2,
    )
    kvs = [kv] + [part_swap(kv, l) for l in range(1, part)]
    heads = width // HEAD_DIM
    stat_rows = -(-heads // 8) * 8
    o, lse = call(
        grouped(attend_kernel, (part,), (None, part) + (None,) * 4),
        [((total, width), BF16), ((stat_rows, total), F32)],
        [q, *kvs, *wo_own[1:]],
        [((total * part, width), BF16), ((width, total * part), BF16)],
        n_any=n_rep - 1, micros=6,
    )
    os_ = rep_gather(o)
    cs = rep_gather(after(c_own, xs[-1]))
    n_spots = len(packed_rows(pitch, dim, 2 * ff)[1])
    per = width // (part * w_rows)
    ff_out = call(
        grouped(
            ff_kernel, (n_rep, part),
            (None, n_rep, n_rep, n_rep, part - 1, None, n_rep, None, None, n_rep) + (None,) * 16,
        ),
        [((rows, dim), F32)]
        + [((rows, dim), BF16)] * n_rep
        + [
            ((total, dim), BF16), ((total, ff), BF16), ((total, 2 * ff), BF16),
            ((total, dim), BF16), ((per, part, w_rows, dim), BF16), ((1, dim), F32),
        ],
        [at, *xs, *os_, *wo_own, *wo_other, ff_w, *cs, gains],
        [
            ((total, dim), F32), ((total, 2 * ff), F32), ((total, ff), F32), ((n_inner, w_rows, 2 * ff), BF16),
            ((n_inner, pitch, dim), BF16), ((total, dim), BF16), ((total, dim), BF16), ((total, dim), BF16),
            ((n_rep, part, w_rows, dim), BF16),
        ],
        n_smem=1, far=range(1, 1 + 4 * n_rep + part), far_outs=(4 + n_rep, 5 + n_rep),
        n_sems=n_rep * (part + 3) + 1 + n_spots + 1 + per, whole=True, micros=11,
    )
    r_own, da_two = ff_out[0], ff_out[1 : 1 + n_rep]
    a_two, gated, d_hidden, o_all, w_out, gain_two_part = ff_out[1 + n_rep :]
    das = rep_trade(da_two)
    ff_back = call(
        grouped(ff_grads_kernel, (n_rep,), (None, None, None, n_rep, None, None, n_rep) + (None,) * 6),
        [((rows, dim), BF16)] * n_rep + [((n_inner, ff_high, 2 * ff), BF16)],
        [at, gated, ff_w, *cs, a_two, d_hidden],
        [
            ((n_inner, pitch, dim), BF16), ((n_inner, pitch, dim), BF16), ((total, dim), BF16),
            ((n_inner, w_rows, 2 * ff), BF16),
        ],
        n_smem=1, far=range(2, 3 + n_rep), far_outs=(n_rep,), n_sems=n_rep + 2 * n_spots + 1, whole=True, micros=5,
    )
    lo, ff_grad = ff_back[:-1], ff_back[-1]
    dr, dz = call(
        grouped(middle_kernel, (n_rep,), (n_rep,) + (None,) * 5),
        [((rows, dim), F32), ((rows, dim), BF16)],
        [*das, r_own, c_own, gains, ff_grad],
        n_any=1, micros=2,
    )
    ff_grad = lax.psum_scatter(after(ff_grad, *das[1:]), "inner", scatter_dimension=0)
    dzs = rep_gather(dz)

    back = call(
        grouped(
            attend_back_kernel,
            (n_rep, part),
            (None, n_rep, None, None, None, part, None, None, None, None, None, part - 1, None) + (None,) * 7,
        ),
        [((total, width), BF16), ((total, 2 * width), F32)]
        + [((total, 2 * width), BF16)] * (part - 1)
        + [((total, dim), BF16)],
        [at, *dzs, w_out, o, q, *kvs, lse, cos, sin],
        [
            ((total, width), BF16), ((total * part, width), BF16), ((total * part, width), BF16),
            ((width, total * part), BF16), ((stat_rows, total), F32),
            ((total * part, width), F32), ((total * part, width), F32),
        ],
        n_smem=1, micros=10,
    )
    dq, dkv, sends, dz_all = back[0], back[1], back[2:-1], back[-1]
    los = rep_trade([after(x, dzs[-1]) for x in lo])
    gots = [part_swap(after(x, *los[1:]), l + 1) for l, x in enumerate(sends)]
    (d_out,) = call(
        out_grad_kernel, [((dim, width), BF16)], [at, o_all, dz_all], n_smem=1, micros=2,
    )
    qkv_out = call(
        grouped(
            qkv_back_kernel, (n_rep, part),
            (None, None, None, part - 1, None, None, None, None, n_rep, None, None, None, part - 1, n_rep) + (None,) * 3,
        ),
        [((n_rep * high, lanes), BF16)] * part + [((rows, dim), BF16)] * n_rep,
        [at, dq, dkv, *gots, cos, sin, a_one, w_qkv, *xs, d_out, gain_two_part],
        [((total, 3 * width), BF16), ((total, dim), F32), ((dim, lanes), BF16)],
        n_smem=1, micros=4,
    )
    keep, sends, da_one = qkv_out[0], qkv_out[1:part], qkv_out[part:]
    gots = [part_swap(x, l + 1) for l, x in enumerate(sends)]
    (summed,) = call(
        grouped(part_sum_kernel, (), (None, part - 1, None)), [((n_rep * high, lanes), BF16)], [keep, *gots]
    )
    das = rep_trade(da_one)
    ff_grad = after(ff_grad, *das[1:])
    d_pack = lax.psum_scatter(
        after(summed, ff_grad), "inner", scatter_dimension=0, axis_index_groups=planes, tiled=True
    )
    parts = call(
        grouped(last_kernel, (n_rep,), (None, n_rep, n_rep, None, None, None, None, n_rep, None)),
        home, [at, *das, *los, xs[0], dr, r_own, gains], [((rows, dim), F32)], n_smem=1, whole=True, micros=2,
    )
    ff_grads = jnp.concatenate([ff_grad] * n_rep, axis=0)
    ff_grads = lax.all_to_all(ff_grads, "rep", 0, 0, tiled=True).reshape(n_rep, ff_high, 2 * ff)
    back_home = send_home(parts)
    quarter = after(d_pack, *back_home)
    input_grad, layer_out = call(
        grouped(place_kernel, (n_rep,), (None, n_rep, None, None)),
        [((rows, dim), BF16)] * 2, [at, *back_home, d_pack], n_smem=1, n_any=1,
    )
    g_qkv, g_out, g_gains = call(
        grouped(grads_kernel, (n_rep,), (None, n_rep, None, None, None)),
        [((w_rows, 3 * dim), F32), ((w_rows, dim), F32), ((8, lanes), F32)],
        [at, *rep_gather(quarter)],
        n_smem=1, micros=2,
    )
    g_in, g_down = call(
        grouped(ff_out_kernel, (n_rep, unit, pitch), (None,) * 4),
        [((w_rows, 2 * n_inner * ff_shard), F32), ((ff_shard, dim), F32)],
        [ff_grads, d_pack],
        [((pitch, dim), F32)],
        n_any=1, micros=4,
    )
    gain_grads = g_gains[: 2 * dim // lanes].reshape(2, dim)
    gain_grads = lax.dynamic_slice_in_dim(gain_grads, i * w_rows, w_rows, 1)
    return (layer_out, input_grad, g_qkv, g_out, g_in, g_down, gain_grads[0], gain_grads[1])


def solution(mesh):
    rows = P(("rep", "inner"), None)
    weight = P("inner", None)
    return jax.shard_map(
        functools.partial(on_device, mesh.shape["rep"], mesh.shape["inner"]),
        mesh=mesh,
        in_specs=(rows, rows, weight, weight, weight, weight, P("inner"), P("inner")),
        out_specs=(rows, rows, weight, weight, weight, weight, P("inner"), P("inner")),
        check_vma=False,
    )
```

```python
import functools
import math

import jax
import jax.numpy as jnp
from jax import lax
from jax.experimental import pallas as pl
from jax.experimental.pallas import tpu as pltpu
from jax.sharding import PartitionSpec as P

HEAD_DIM = 64
EPSILON = 1e-05
THETA = 160000.0
F32 = jnp.float32
BF16 = jnp.bfloat16
NT = (((1,), (1,)), ((), ()))
TN = (((0,), (0,)), ((), ()))
VMEM_SPARE = 8 * 1024 * 1024
VMEM_WHOLE = 60 * 1024 * 1024


def dot(a, b):
    return jnp.dot(a, b, preferred_element_type=F32)


def dot_nt(a, b):
    return lax.dot_general(a, b, NT, preferred_element_type=F32)


def dot_tn(a, b):
    return lax.dot_general(a, b, TN, preferred_element_type=F32)


def call(body, outs, args, scratch=(), n_smem=0, n_any=0, far=(), far_outs=(), n_sems=0, whole=False, micros=1):
    n_passed = len(args) - n_any
    spaces = [pltpu.SMEM] * n_smem + [pltpu.VMEM] * (n_passed - n_smem) + [pltpu.HBM] * n_any
    for k in far:
        spaces[k] = pltpu.HBM
    held = sum(math.prod(s) * jnp.dtype(d).itemsize for s, d in scratch)

    def without_waited(*refs):
        body(*refs[:n_passed], *refs[len(args) :])

    return pl.pallas_call(
        without_waited,
        out_shape=[jax.ShapeDtypeStruct(s, d) for s, d in outs],
        in_specs=[pl.BlockSpec(memory_space=space) for space in spaces],
        out_specs=[pl.BlockSpec(memory_space=pltpu.HBM if k in far_outs else pltpu.VMEM) for k in range(len(outs))],
        scratch_shapes=[pltpu.VMEM(s, d) for s, d in scratch]
        + ([pltpu.SemaphoreType.DMA((n_sems,))] if n_sems else []),
        compiler_params=pltpu.CompilerParams(vmem_limit_bytes=VMEM_WHOLE if whole else held + VMEM_SPARE),
        cost_estimate=pl.CostEstimate(
            flops=int(micros * 1e9), transcendentals=0, bytes_accessed=int(micros * 1e6)
        ),
    )(*args)


class Copies:
    def __init__(self, sems):
        self.sems = sems
        self.used = 0

    def start(self, source, target):
        copy = pltpu.make_async_copy(source, target, self.sems.at[self.used])
        self.used += 1
        copy.start()
        return copy


def wait_all(copies):
    for copy in copies:
        copy.wait()


def after(value, *others):
    return lax.optimization_barrier((value, *others))[0]


def hat_of(values):
    centred = values - jnp.mean(values, axis=-1, keepdims=True)
    inv = lax.rsqrt(jnp.mean(centred * centred, axis=-1, keepdims=True) + EPSILON)
    return centred * inv, inv


def spot(block, size):
    return pl.ds(pl.multiple_of(block * size, size), size)


def partner(x):
    width = x.shape[-1]
    half = HEAD_DIM // 2
    lane = lax.broadcasted_iota(jnp.int32, x.shape, x.ndim - 1)
    ahead = pltpu.roll(x, width - half, 1)
    behind = pltpu.roll(x, half, 1)
    return jnp.where(lane % HEAD_DIM < half, ahead, behind)


def tile_lanes(table, width):
    return jnp.concatenate([table] * (width // table.shape[-1]), axis=-1)


def head_mask(h, width):
    lane = lax.broadcasted_iota(jnp.int32, (1, width), 1)
    return ((lane >= h * HEAD_DIM) & (lane < (h + 1) * HEAD_DIM)).astype(BF16)


def place_kernel(n_rep, at_ref, pieces, first_ref, second_ref):
    sub = pieces[0].shape[0] // 2
    for k in range(n_rep):
        spot = pl.ds(pl.multiple_of((at_ref[1] ^ k) * sub, sub), sub)
        first_ref[spot, :] = pieces[k][:sub, :]
        second_ref[spot, :] = pieces[k][sub:, :]


def send_back(n_rep, at_ref, scr, outs, first):
    sub = outs[0].shape[0] // 2
    for k in range(n_rep):
        block = at_ref[0] ^ k
        outs[k][first : first + sub, :] = scr[pl.ds(pl.multiple_of(block * sub, sub), sub), :].astype(BF16)


def weight_kernel(n_inner, n_part, at_ref, qkv_ref, out_ref, gains_ref, pack_ref):
    rows, dim = out_ref.shape
    lanes = pack_ref.shape[1]
    width = lanes // 4
    for p in range(3):
        start = pl.multiple_of(p * dim + at_ref[0] * width, width)
        pack_ref[:rows, p * width : (p + 1) * width] = qkv_ref[:, pl.ds(start, width)]
    start = pl.multiple_of(at_ref[0] * width, width)
    pack_ref[:rows, 3 * width :] = out_ref[:, pl.ds(start, width)]
    shard = lax.broadcasted_iota(jnp.int32, (2, dim), 1) // rows
    own = jnp.concatenate([gains_ref[...].astype(F32)] * n_inner, axis=1)
    own = jnp.where(shard == at_ref[1] * n_part + at_ref[2], own, 0.0)
    strips = [own[g : g + 1, k * lanes : (k + 1) * lanes] for g in range(2) for k in range(dim // lanes)]
    strips.append(jnp.zeros((8 - len(strips), lanes), F32))
    pack_ref[rows:, :] = jnp.concatenate(strips, axis=0).astype(BF16)


def packed_rows(pitch, dim, lanes):
    extra = pitch * dim // lanes
    spots = [(0, 0, 0, 0, extra, min(dim, lanes))]
    left = lanes - dim
    if left:
        rest = pitch - extra
        for c in range(dim // left):
            spots.append((c * rest, dim, extra, c * left, rest, left))
    return extra, spots


def ff_weight_kernel(n_rep, unit, pitch, at_ref, in_ref, down_ref, pack_ref, down_scr):
    rows = in_ref.shape[0]
    shard, dim = down_ref.shape
    lanes = pack_ref.shape[1]
    for jj in range(n_rep):
        size = min(unit, shard - jj * unit)

        @pl.when(at_ref[0] == jj)
        def _(jj=jj, size=size):
            pieces = []
            for p in range(in_ref.shape[1] // shard):
                first = p * shard + jj * unit
                pieces.append(in_ref[:, first : first + size])
                pieces.append(jnp.zeros((rows, pitch - size), BF16))
            pack_ref[:rows, :] = jnp.concatenate(pieces, axis=1)
            down_scr[:size, :] = down_ref[jj * unit : jj * unit + size, :]
            down_scr[size:, :] = jnp.zeros((pitch - size, dim), BF16)

    _, spots = packed_rows(pitch, dim, lanes)
    for row, lane, row_in, col_in, n, w in spots:
        pack_ref[rows + row : rows + row + n, lane : lane + w] = down_scr[row_in : row_in + n, col_in : col_in + w]


def qkv_kernel(
    n_rep, at_ref, refs_x, pack_ref, cos_ref, sin_ref, q_ref, kv_ref, a_out, w_out, gains_ref,
    a_ref, w_ref, rows_scr, sems,
):
    rows = refs_x[0].shape[0]
    width = q_ref.shape[1]
    dim = a_ref.shape[1]
    lanes = 4 * width
    n_inner, high, _ = pack_ref.shape
    w_rows = high - 8
    copies = Copies(sems)
    gains_in = copies.start(pack_ref.at[:, w_rows:, :], rows_scr)
    weights_in = copies.start(pack_ref.at[:, :w_rows, : 3 * width], w_ref)
    gains_in.wait()
    gains = rows_scr[0].astype(F32)
    for p in range(1, n_inner):
        gains = gains + rows_scr[p].astype(F32)
    per = dim // lanes
    for g in range(2):
        gains_ref[g : g + 1, :] = jnp.concatenate(
            [gains[g * per + k : g * per + k + 1, :] for k in range(per)], axis=1
        )
    for m in range(n_rep):
        hat, _ = hat_of(refs_x[m][...].astype(F32))
        a_ref[spot(at_ref[0] ^ m, rows), :] = (hat * gains_ref[0:1, :]).astype(BF16)
    weights_in.wait()
    done = [copies.start(a_ref, a_out), copies.start(w_ref, w_out)]
    weights = w_ref[...].reshape(dim, 3 * width)
    step = 2 * rows if n_rep % 2 == 0 else rows
    for r0 in range(0, n_rep * rows, step):
        sl = slice(r0, r0 + step)
        proj = dot(a_ref[sl, :], weights)
        cos = tile_lanes(cos_ref[sl, :], width)
        sin = tile_lanes(sin_ref[sl, :], width)
        query = proj[:, :width]
        key = proj[:, width : 2 * width]
        query = (query * cos + partner(query) * sin).astype(BF16).astype(F32)
        q_ref[sl, :] = (query * HEAD_DIM**-0.5).astype(BF16)
        kv_ref[sl, :width] = (key * cos + partner(key) * sin).astype(BF16)
        kv_ref[sl, width:] = proj[:, 2 * width :].astype(BF16)
    wait_all(done)


def attend_kernel(n_part, q_ref, refs_kv, o_ref, lse_ref, k_scr, vt_scr):
    rows, width = q_ref.shape
    keys = refs_kv[0].shape[0]
    for l in range(n_part):
        k_scr[l * keys : (l + 1) * keys, :] = refs_kv[l][:, :width]
        vt_scr[:, l * keys : (l + 1) * keys] = refs_kv[l][:, width:].astype(F32).T.astype(BF16)
    heads = width // HEAD_DIM
    step = min(256, rows)

    def body(c, carry):
        r0 = pl.multiple_of(c * step, step)
        for h in range(heads):
            pair = h // 2 * 128
            q = q_ref[pl.ds(r0, step), pair : pair + 128] * head_mask(h % 2, 128)
            s = dot_nt(k_scr[:, pair : pair + 128], q)
            top = jnp.max(s, axis=0, keepdims=True)
            e = jnp.exp(s - top)
            mass = jnp.sum(e, axis=0, keepdims=True)
            lse_ref[h : h + 1, pl.ds(r0, step)] = top + jnp.log(mass)
            ot = dot(vt_scr[h * HEAD_DIM : (h + 1) * HEAD_DIM, :], e.astype(BF16)) / mass
            ot_list.append(ot)
            if h % 2 == 1:
                both = jnp.concatenate(ot_list, axis=0)
                o_ref[pl.ds(r0, step), pair : pair + 128] = both.T.astype(BF16)
                ot_list.clear()
        return carry

    ot_list = []
    lax.fori_loop(0, rows // step, body, 0)


def ff_kernel(
    n_rep, n_part, at_ref, refs_x, refs_o, refs_wo, refs_wo_other, ffw_ref, refs_c, gains_ref,
    r_ref, refs_da, a_ref, m_ref, du_ref, o_out, wout_out, gain_ref,
    hat_scr, u_scr, dm_scr, win_scr, wdown_scr, x_scr, c_scr, o_scr, wout_scr, sems,
):
    rows, dim = refs_x[0].shape
    total = n_rep * rows
    quarter = refs_o[0].shape[1]
    j, t = at_ref[0], at_ref[2]
    _, w_rows, lanes = win_scr.shape
    copies = Copies(sems)
    first = []
    for m in range(n_rep):
        cols = spot(j ^ m, quarter)
        first.append(copies.start(refs_wo[m], wout_scr.at[:, t, :, cols]))
        for l in range(1, n_part):
            first.append(copies.start(refs_wo_other[l - 1].at[m], wout_scr.at[:, t ^ l, :, cols]))
        first.append(copies.start(refs_o[m], o_scr.at[:, cols]))
        first.append(copies.start(refs_x[m], x_scr.at[spot(j ^ m, rows), :]))
    second = copies.start(ffw_ref.at[:, :w_rows, :], win_scr)
    third = [copies.start(refs_c[m], c_scr.at[spot(j ^ m, rows), :]) for m in range(n_rep)]
    third += copy_down(copies, w_rows, ffw_ref, wdown_scr)
    wait_all(first)
    weights = wout_scr[...].reshape(dim, dim)
    last = [copies.start(o_scr, o_out)]
    hat_scr[...] = x_scr[...].astype(F32) + dot(o_scr[...], weights)
    r_ref[...] = hat_scr[spot(j, rows), :]
    per = quarter // w_rows // n_part
    for k in range(per):
        block = wout_scr.at[pl.ds(j * per + k, 1)]
        last.append(copies.start(block, wout_out.at[pl.ds(k, 1)]))
    gain = gains_ref[1:2, :]

    def norm_step(c, carry):
        r0 = pl.multiple_of(c * 64, 64)
        hat, _ = hat_of(hat_scr[pl.ds(r0, 64), :])
        hat_scr[pl.ds(r0, 64), :] = hat
        a_ref[pl.ds(r0, 64), :] = (hat * gain).astype(BF16)
        return carry

    lax.fori_loop(0, total // 64, norm_step, 0)
    second.wait()
    weights = win_scr[...].reshape(dim, lanes)
    u_scr[...] = dot(a_ref[...], weights)
    wait_all(third)
    dm_scr[...] = dot_nt(c_scr[...], wdown_scr[...].reshape(m_ref.shape[1], dim))
    width = m_ref.shape[1]

    def gate_step(c, carry):
        sl = pl.ds(pl.multiple_of(c * 32, 32), 32)
        pre = u_scr[sl, :width]
        gate = u_scr[sl, width:]
        dm = dm_scr[sl, :]
        cdf = 0.5 * (1.0 + lax.erf(pre * (0.5**0.5)))
        pdf = jnp.exp(-0.5 * pre * pre) * 0.3989422804014327
        act = pre * cdf
        m_ref[sl, :] = (act * gate).astype(BF16)
        du_ref[sl, :width] = (dm * gate * (cdf + pre * pdf)).astype(BF16)
        du_ref[sl, width:] = (dm * act).astype(BF16)
        return carry

    lax.fori_loop(0, total // 32, gate_step, 0)
    u_scr[:, :dim] = dot_nt(du_ref[...], win_scr[...].reshape(dim, lanes))
    total_gain = jnp.zeros((1, dim), F32)
    for m in range(n_rep):
        sl = spot(j ^ m, rows)
        da = u_scr[sl, :dim]
        refs_da[m][...] = da.astype(BF16)
        total_gain = total_gain + jnp.sum(da * hat_scr[sl, :], axis=0, keepdims=True)
    gain_ref[...] = total_gain
    wait_all(last)


def copy_down(copies, w_rows, ffw_ref, wdown_scr):
    _, pitch, dim = wdown_scr.shape
    _, spots = packed_rows(pitch, dim, ffw_ref.shape[2])
    started = []
    for row, lane, row_in, col_in, n, w in spots:
        source = ffw_ref.at[:, w_rows + row : w_rows + row + n, lane : lane + w]
        started.append(copies.start(source, wdown_scr.at[:, row_in : row_in + n, col_in : col_in + w]))
    return started


def ff_grads_kernel(
    n_rep, at_ref, m_ref, ffw_ref, refs_c, a_ref, du_ref, refs_lo, grad_out,
    down_scr, wdown_scr, c_scr, din_scr, sems,
):
    rows, dim = refs_lo[0].shape
    n_inner, w_rows, lanes = din_scr.shape
    pitch = down_scr.shape[1]
    j = at_ref[0]
    copies = Copies(sems)
    early = [copies.start(refs_c[m], c_scr.at[spot(j ^ m, rows), :]) for m in range(n_rep)]
    late = copy_down(copies, w_rows, ffw_ref, wdown_scr)
    din_scr[...] = dot_tn(a_ref[...], du_ref[...]).astype(BF16).reshape(n_inner, w_rows, lanes)
    sent = [copies.start(din_scr, grad_out.at[:, :w_rows, :])]
    wait_all(early)
    down_scr[...] = dot_tn(m_ref[...], c_scr[...]).astype(BF16).reshape(n_inner, pitch, dim)
    for row, lane, row_in, col_in, n, w in packed_rows(pitch, dim, lanes)[1]:
        source = down_scr.at[:, row_in : row_in + n, col_in : col_in + w]
        sent.append(copies.start(source, grad_out.at[:, w_rows + row : w_rows + row + n, lane : lane + w]))
    wait_all(late)
    down_scr_all = wdown_scr[...].reshape(n_inner * pitch, dim)
    c_scr[...] = dot(m_ref[...], down_scr_all).astype(BF16)
    for m in range(n_rep):
        refs_lo[m][...] = c_scr[spot(j ^ m, rows), :]
    wait_all(sent)


def norm_back(values, gain, grad):
    hat, inv = hat_of(values)
    dhat = grad * gain
    return inv * (
        dhat
        - jnp.mean(dhat, axis=-1, keepdims=True)
        - hat * jnp.mean(dhat * hat, axis=-1, keepdims=True)
    )


def sum_of(refs):
    total = refs[0][...].astype(F32)
    for ref in refs[1:]:
        total = total + ref[...].astype(F32)
    return total


def middle_kernel(n_rep, refs_da, r_ref, c_ref, gains_ref, dr_ref, dz_ref):
    dr = c_ref[...].astype(F32) + norm_back(r_ref[...], gains_ref[1:2, :], sum_of(refs_da))
    dr_ref[...] = dr
    dz_ref[...] = dr.astype(BF16)


def last_kernel(n_rep, at_ref, refs_da, refs_lo, x_ref, dr_ref, r_ref, gains_ref, outs, scr):
    rows = x_ref.shape[0]
    sub = rows // n_rep
    scr[...] = r_ref[...] + sum_of(refs_lo)
    send_back(n_rep, at_ref, scr, outs, sub)
    back = norm_back(x_ref[...].astype(F32), gains_ref[0:1, :], sum_of(refs_da))
    scr[...] = dr_ref[...] + back
    send_back(n_rep, at_ref, scr, outs, 0)


def attend_back_kernel(
    n_rep, n_part, sub_j, refs_dz, wout_ref, o_ref, q_ref, refs_kv, lse_ref, cos_ref, sin_ref,
    dq_ref, dkv_ref, refs_send, dz_ref, do_scr, k_scr, v_scr, kt_scr, delta_scr, dk_scr, dv_scr,
):
    rows, width = q_ref.shape
    keys = refs_kv[0].shape[0]
    part = refs_dz[0].shape[0]
    for m in range(n_rep):
        dz_ref[spot(sub_j[0] ^ m, part), :] = refs_dz[m][...]
    dout = dot_nt(dz_ref[...], wout_ref[...].reshape(width, dz_ref.shape[1])).astype(BF16)
    do_scr[...] = dout
    prod_t = (dout.astype(F32) * o_ref[...].astype(F32)).T
    heads = width // HEAD_DIM
    for h in range(heads):
        delta_scr[h : h + 1, :] = jnp.sum(
            prod_t[h * HEAD_DIM : (h + 1) * HEAD_DIM, :], axis=0, keepdims=True
        )
    for l in range(n_part):
        sl = slice(l * keys, (l + 1) * keys)
        k_scr[sl, :] = refs_kv[l][:, :width]
        v_scr[sl, :] = refs_kv[l][:, width:]
        kt_scr[:, sl] = refs_kv[l][:, :width].astype(F32).T.astype(BF16)
    dk_scr[...] = jnp.zeros_like(dk_scr)
    dv_scr[...] = jnp.zeros_like(dv_scr)
    step = min(256, rows)

    def body(c, carry):
        r0 = pl.multiple_of(c * step, step)
        for h in range(heads):
            pair = h // 2 * 128
            lanes = slice(pair, pair + 128)
            mask = head_mask(h % 2, 128)
            q = q_ref[pl.ds(r0, step), lanes] * mask
            do = do_scr[pl.ds(r0, step), lanes] * mask
            p = jnp.exp(dot_nt(k_scr[:, lanes], q) - lse_ref[h : h + 1, pl.ds(r0, step)])
            dp = dot_nt(v_scr[:, lanes], do)
            ds = (p * (dp - delta_scr[h : h + 1, pl.ds(r0, step)])).astype(BF16)
            dv_scr[:, lanes] += dot(p.astype(BF16), do)
            dk_scr[:, lanes] += dot(ds, q)
            dq_list.append(dot(kt_scr[h * HEAD_DIM : (h + 1) * HEAD_DIM, :], ds))
            if h % 2 == 1:
                dq = jnp.concatenate(dq_list, axis=0).T * HEAD_DIM**-0.5
                dq_list.clear()
                cos = cos_ref[pl.ds(r0, step), :]
                sin = sin_ref[pl.ds(r0, step), :]
                dq_ref[pl.ds(r0, step), lanes] = (dq * cos - partner(dq) * sin).astype(BF16)
        return carry

    dq_list = []
    lax.fori_loop(0, rows // step, body, 0)
    dkv_ref[:, :width] = dk_scr[:keys, :]
    dkv_ref[:, width:] = dv_scr[:keys, :]
    for l in range(1, n_part):
        sl = slice(l * keys, (l + 1) * keys)
        refs_send[l - 1][:, :width] = dk_scr[sl, :].astype(BF16)
        refs_send[l - 1][:, width:] = dv_scr[sl, :].astype(BF16)


def out_grad_kernel(sub_j, o_ref, dz_ref, dout_ref):
    quarter = dout_ref.shape[1]
    cols = dz_ref[:, pl.ds(pl.multiple_of(sub_j[0] * quarter, quarter), quarter)]
    dout_ref[...] = dot_tn(o_ref[...], cols).astype(BF16)


def qkv_back_kernel(
    n_rep, n_part, at_ref, dq_ref, dkv_ref, refs_got, cos_ref, sin_ref, a_ref, w_ref, refs_x, dout_ref,
    gain_two_ref, keep_ref, refs_send, refs_da, dp_scr, da_scr, grad_scr,
):
    width = dq_ref.shape[1]
    rows, dim = refs_x[0].shape
    lanes = 4 * width
    high = keep_ref.shape[0] // n_rep
    w_rows = high - 8
    dkv = dkv_ref[...]
    for got in refs_got:
        dkv = dkv + got[...].astype(F32)
    dk = dkv[:, :width]
    cos = tile_lanes(cos_ref[...], width)
    sin = tile_lanes(sin_ref[...], width)
    dp_scr[:, :width] = dq_ref[...]
    dp_scr[:, width : 2 * width] = (dk * cos - partner(dk) * sin).astype(BF16)
    dp_scr[:, 2 * width :] = dkv[:, width:].astype(BF16)
    grad_scr[:, : 3 * width] = dot_tn(a_ref[...], dp_scr[...]).astype(BF16)
    grad_scr[:, 3 * width :] = dout_ref[...]
    da_scr[...] = dot_nt(dp_scr[...], w_ref[...].reshape(dim, 3 * width))
    gain = jnp.zeros((1, dim), F32)
    for m in range(n_rep):
        da = da_scr[spot(at_ref[0] ^ m, rows), :]
        refs_da[m][...] = da.astype(BF16)
        hat, _ = hat_of(refs_x[m][...].astype(F32))
        gain = gain + jnp.sum(da * hat, axis=0, keepdims=True)
    per = dim // lanes
    strips = [g[:, k * lanes : (k + 1) * lanes] for g in (gain, gain_two_ref[...]) for k in range(per)]
    strips.append(jnp.zeros((8 - len(strips), lanes), F32))
    gains = jnp.concatenate(strips, axis=0).astype(BF16)
    for l in range(n_part):
        ref = keep_ref if l == 0 else refs_send[l - 1]
        for m in range(n_rep):
            shard = m * n_part + (at_ref[2] ^ l)
            ref[m * high : m * high + w_rows, :] = grad_scr[spot(shard, w_rows), :]
            ref[m * high + w_rows : (m + 1) * high, :] = gains


def part_sum_kernel(keep_ref, refs_got, out_ref):
    total = keep_ref[...].astype(F32)
    for got in refs_got:
        total = total + got[...].astype(F32)
    out_ref[...] = total.astype(BF16)


def grads_kernel(n_rep, at_ref, pieces, qkv_ref, out_ref, gains_ref):
    width = pieces[0].shape[1] // 4
    rows, dim = out_ref.shape
    for m in range(n_rep):
        for p in range(3):
            start = pl.multiple_of(p * dim + (at_ref[0] ^ m) * width, width)
            qkv_ref[:, pl.ds(start, width)] = pieces[m][:rows, p * width : (p + 1) * width].astype(F32)
        start = pl.multiple_of((at_ref[0] ^ m) * width, width)
        out_ref[:, pl.ds(start, width)] = pieces[m][:rows, 3 * width :].astype(F32)
    gains = pieces[0][rows:, :].astype(F32)
    for m in range(1, n_rep):
        gains = gains + pieces[m][rows:, :].astype(F32)
    gains_ref[...] = gains


def ff_out_kernel(n_rep, unit, pitch, cuts, at_ref, pieces, in_ref, down_ref, scr, down_scr):
    lanes = pieces[0].shape[1]
    rows = in_ref.shape[0]
    shard, dim = down_ref.shape
    for (m, top), piece in zip(cuts, pieces, strict=True):
        scr[at_ref[0] ^ m, top : top + piece.shape[0], :] = piece[...]
    _, spots = packed_rows(pitch, dim, lanes)
    strips = []
    for jj in range(n_rep):
        size = min(unit, shard - jj * unit)
        for row, lane, row_in, col_in, n, w in spots:
            down_scr[row_in : row_in + n, col_in : col_in + w] = scr[
                jj, rows + row : rows + row + n, lane : lane + w
            ].astype(F32)
        down_ref[jj * unit : jj * unit + size, :] = down_scr[:size, :]
    for p in range(lanes // pitch):
        strips = []
        for jj in range(n_rep):
            size = min(unit, shard - jj * unit)
            strips.append(scr[jj, :rows, p * pitch : p * pitch + size].astype(F32))
        in_ref[:, p * shard : (p + 1) * shard] = jnp.concatenate(strips, axis=1)


def split_refs(counts, refs):
    out, at = [], 0
    for n in counts:
        if n is None:
            out.append(refs[at])
            at += 1
        else:
            out.append(list(refs[at : at + n]))
            at += n
    return out


def grouped(kernel, static, counts):
    def body(*refs):
        kernel(*static, *split_refs(counts, refs))

    return body


def on_device(
    n_rep, n_inner,
    tokens, cotangent, qkv_weight, out_weight, in_weight, down_weight, gain_one, gain_two,
):
    part = n_inner // n_rep
    rows, dim = tokens.shape
    sub = rows // n_rep
    w_rows = qkv_weight.shape[0]
    width = dim // n_rep
    lanes = 4 * width
    high = w_rows + 8
    ff_shard = down_weight.shape[0]
    unit = -(-ff_shard // n_rep)
    pitch = -(-unit // 16) * 16
    ff = pitch * n_inner
    ff_high = w_rows + pitch * dim // (2 * ff)
    total = n_rep * rows
    j = lax.axis_index("rep")
    i = lax.axis_index("inner")
    s = i // part
    t = i % part
    at = jnp.stack([j, s, t]).astype(jnp.int32)

    def rep_swap(x, m):
        return lax.ppermute(x, "rep", [(a, a ^ m) for a in range(n_rep)])

    def plane_swap(x, m):
        pairs = [(a * part + b, (a ^ m) * part + b) for a in range(n_rep) for b in range(part)]
        return lax.ppermute(x, "inner", pairs)

    def part_swap(x, l):
        pairs = [(a * part + b, a * part + (b ^ l)) for a in range(n_rep) for b in range(part)]
        return lax.ppermute(x, "inner", pairs)

    def rep_gather(x):
        return [x] + [rep_swap(x, m) for m in range(1, n_rep)]

    def rep_spread(x):
        if n_rep != 4:
            return [[piece] for piece in rep_gather(x)]
        half = x.shape[0] // 2
        near = [rep_swap(x, 1), rep_swap(x, 2)]
        return [[x], [near[0]], [near[1]], [rep_swap(near[0][:half], 2), rep_swap(near[1][half:], 1)]]

    def rep_trade(pieces):
        return [pieces[0]] + [rep_swap(pieces[m], m) for m in range(1, n_rep)]

    def plane_trade(pieces):
        return [pieces[0]] + [plane_swap(pieces[m], m) for m in range(1, n_rep)]

    def send_home(pieces):
        got = []
        for k in range(n_rep):
            pairs = []
            for a in range(n_rep):
                for z in range(n_rep):
                    for b in range(part):
                        pairs.append((a * n_inner + z * part + b, z * n_inner + (a ^ k) * part + b))
            got.append(lax.ppermute(pieces[k], ("rep", "inner"), pairs))
        return got

    home = [((2 * sub, dim), BF16)] * n_rep
    planes = [[z * part + b for z in range(n_rep)] for b in range(part)]

    (w_pack,) = call(
        functools.partial(weight_kernel, n_inner, part), [((high, lanes), BF16)],
        [at, qkv_weight, out_weight, jnp.stack([gain_one, gain_two])], n_smem=1,
    )
    w_all = lax.all_gather(w_pack, "inner")
    x_first = lax.all_to_all(after(tokens, w_pack), "rep", 0, 0, tiled=True)
    in_late = after(in_weight, x_first)
    x_own = lax.all_to_all(x_first, "inner", 0, 0, axis_index_groups=planes, tiled=True)
    c_first = lax.all_to_all(after(cotangent, x_first), "rep", 0, 0, tiled=True)
    x_own = after(x_own, c_first)
    c_own = lax.all_to_all(after(c_first, x_own), "inner", 0, 0, axis_index_groups=planes, tiled=True)
    xs = rep_gather(x_own)
    (ff_pack,) = call(
        grouped(ff_weight_kernel, (n_rep, unit, pitch), (None,) * 5),
        [((ff_high, 2 * ff), BF16)],
        [at, in_late, down_weight, w_pack],
        [((pitch, dim), BF16)],
        n_smem=1, n_any=1,
    )
    ff_w = lax.all_gather(ff_pack, "inner")

    own = w_all.reshape(n_rep, part, high, lanes)
    own = lax.dynamic_slice_in_dim(own, t, 1, 1)[:, 0, :w_rows, 3 * width :].reshape(n_rep * w_rows, width)
    wo_own = rep_gather(after(own.reshape(n_rep, w_rows, width), xs[-1]))
    wo_other = [part_swap(jnp.stack(wo_own), l) for l in range(1, part)]

    order = jnp.arange(total, dtype=jnp.int32)
    place = ((order // sub % n_rep) * part + t) * rows + (order // rows) * sub + order % sub
    inv_freq = 1.0 / THETA ** (jnp.arange(HEAD_DIM // 2, dtype=F32) * (2.0 / HEAD_DIM))
    angle = place.astype(F32)[:, None] * inv_freq[None, :]
    cos_half, sin_half = jnp.cos(angle), jnp.sin(angle)
    cos = jnp.concatenate([cos_half] * 4, axis=1)
    sin = jnp.concatenate([-sin_half, sin_half] * 2, axis=1)

    q, kv, a_one, w_qkv, gains = call(
        grouped(qkv_kernel, (n_rep,), (None, n_rep) + (None,) * 12),
        [
            ((total, width), BF16), ((total, 2 * width), BF16), ((total, dim), BF16),
            ((n_inner, w_rows, 3 * width), BF16), ((2, dim), F32),
        ],
        [at, *xs, w_all, cos, sin, c_own],
        [((total, dim), BF16), ((n_inner, w_rows, 3 * width), BF16), ((n_inner, 8, lanes), BF16)],
        n_smem=1, n_any=1, far=(1 + n_rep,), far_outs=(2, 3), n_sems=4, whole=True, micros=2,
    )
    kvs = [kv] + [part_swap(kv, l) for l in range(1, part)]
    heads = width // HEAD_DIM
    stat_rows = -(-heads // 8) * 8
    o, lse = call(
        grouped(attend_kernel, (part,), (None, part) + (None,) * 4),
        [((total, width), BF16), ((stat_rows, total), F32)],
        [q, *kvs, *wo_own[1:]],
        [((total * part, width), BF16), ((width, total * part), BF16)],
        n_any=n_rep - 1, micros=6,
    )
    os_ = rep_gather(o)
    cs = rep_gather(after(c_own, xs[-1]))
    n_spots = len(packed_rows(pitch, dim, 2 * ff)[1])
    per = width // (part * w_rows)
    ff_out = call(
        grouped(
            ff_kernel, (n_rep, part),
            (None, n_rep, n_rep, n_rep, part - 1, None, n_rep, None, None, n_rep) + (None,) * 16,
        ),
        [((rows, dim), F32)]
        + [((rows, dim), BF16)] * n_rep
        + [
            ((total, dim), BF16), ((total, ff), BF16), ((total, 2 * ff), BF16),
            ((total, dim), BF16), ((per, part, w_rows, dim), BF16), ((1, dim), F32),
        ],
        [at, *xs, *os_, *wo_own, *wo_other, ff_w, *cs, gains],
        [
            ((total, dim), F32), ((total, 2 * ff), F32), ((total, ff), F32), ((n_inner, w_rows, 2 * ff), BF16),
            ((n_inner, pitch, dim), BF16), ((total, dim), BF16), ((total, dim), BF16), ((total, dim), BF16),
            ((n_rep, part, w_rows, dim), BF16),
        ],
        n_smem=1, far=range(1, 1 + 4 * n_rep + part), far_outs=(4 + n_rep, 5 + n_rep),
        n_sems=n_rep * (part + 3) + 1 + n_spots + 1 + per, whole=True, micros=11,
    )
    r_own, da_two = ff_out[0], ff_out[1 : 1 + n_rep]
    a_two, gated, d_hidden, o_all, w_out, gain_two_part = ff_out[1 + n_rep :]
    das = rep_trade(da_two)
    ff_back = call(
        grouped(ff_grads_kernel, (n_rep,), (None, None, None, n_rep, None, None, n_rep) + (None,) * 6),
        [((rows, dim), BF16)] * n_rep + [((n_inner, ff_high, 2 * ff), BF16)],
        [at, gated, ff_w, *cs, a_two, d_hidden],
        [
            ((n_inner, pitch, dim), BF16), ((n_inner, pitch, dim), BF16), ((total, dim), BF16),
            ((n_inner, w_rows, 2 * ff), BF16),
        ],
        n_smem=1, far=range(2, 3 + n_rep), far_outs=(n_rep,), n_sems=n_rep + 2 * n_spots + 1, whole=True, micros=5,
    )
    lo, ff_grad = ff_back[:-1], ff_back[-1]
    dr, dz = call(
        grouped(middle_kernel, (n_rep,), (n_rep,) + (None,) * 5),
        [((rows, dim), F32), ((rows, dim), BF16)],
        [*das, r_own, c_own, gains, lo[0]],
        n_any=1, micros=2,
    )
    ff_grad = lax.psum_scatter(after(ff_grad, das[1]), "inner", scatter_dimension=0)
    dzs = rep_gather(dz)

    back = call(
        grouped(
            attend_back_kernel,
            (n_rep, part),
            (None, n_rep, None, None, None, part, None, None, None, None, None, part - 1, None) + (None,) * 7,
        ),
        [((total, width), BF16), ((total, 2 * width), F32)]
        + [((total, 2 * width), BF16)] * (part - 1)
        + [((total, dim), BF16)],
        [at, *dzs, w_out, o, q, *kvs, lse, cos, sin],
        [
            ((total, width), BF16), ((total * part, width), BF16), ((total * part, width), BF16),
            ((width, total * part), BF16), ((stat_rows, total), F32),
            ((total * part, width), F32), ((total * part, width), F32),
        ],
        n_smem=1, micros=10,
    )
    dq, dkv, sends, dz_all = back[0], back[1], back[2:-1], back[-1]
    los = rep_trade([after(x, dzs[-1]) for x in lo])
    gots = [part_swap(after(x, *los[1:]), l + 1) for l, x in enumerate(sends)]
    (d_out,) = call(
        out_grad_kernel, [((dim, width), BF16)], [at, o_all, dz_all], n_smem=1, micros=2,
    )
    qkv_out = call(
        grouped(
            qkv_back_kernel, (n_rep, part),
            (None, None, None, part - 1, None, None, None, None, n_rep, None, None, None, part - 1, n_rep) + (None,) * 3,
        ),
        [((n_rep * high, lanes), BF16)] * part + [((rows, dim), BF16)] * n_rep,
        [at, dq, dkv, *gots, cos, sin, a_one, w_qkv, *xs, d_out, gain_two_part],
        [((total, 3 * width), BF16), ((total, dim), F32), ((dim, lanes), BF16)],
        n_smem=1, micros=4,
    )
    keep, sends, da_one = qkv_out[0], qkv_out[1:part], qkv_out[part:]
    gots = [part_swap(x, l + 1) for l, x in enumerate(sends)]
    (summed,) = call(
        grouped(part_sum_kernel, (), (None, part - 1, None)), [((n_rep * high, lanes), BF16)], [keep, *gots]
    )
    das = rep_trade(da_one)
    d_pack = lax.psum_scatter(
        after(summed, ff_grad), "inner", scatter_dimension=0, axis_index_groups=planes, tiled=True
    )
    parts = call(
        grouped(last_kernel, (n_rep,), (None, n_rep, n_rep, None, None, None, None, n_rep, None)),
        home, [at, *das, *los, xs[0], dr, r_own, gains], [((rows, dim), F32)], n_smem=1, whole=True, micros=2,
    )
    ff_grads = rep_spread(after(ff_grad, *das[1:]))
    back_home = send_home(parts)
    quarter = after(d_pack, *back_home)
    input_grad, layer_out = call(
        grouped(place_kernel, (n_rep,), (None, n_rep, None, None)),
        [((rows, dim), BF16)] * 2, [at, *back_home, d_pack], n_smem=1, n_any=1,
    )
    g_qkv, g_out, g_gains = call(
        grouped(grads_kernel, (n_rep,), (None, n_rep, None, None, None)),
        [((w_rows, 3 * dim), F32), ((w_rows, dim), F32), ((8, lanes), F32)],
        [at, *rep_gather(quarter)],
        n_smem=1, micros=2,
    )
    cuts, flat = [], []
    for m, pieces in enumerate(ff_grads):
        top = 0
        for piece in pieces:
            cuts.append((m, top))
            flat.append(piece)
            top += piece.shape[0]
    g_in, g_down = call(
        grouped(ff_out_kernel, (n_rep, unit, pitch, cuts), (None, len(flat)) + (None,) * 4),
        [((w_rows, 2 * n_inner * ff_shard), F32), ((ff_shard, dim), F32)],
        [at, *flat, d_pack],
        [((n_rep, ff_high, 2 * ff), BF16), ((pitch, dim), F32)],
        n_smem=1, n_any=1, micros=4,
    )
    gain_grads = g_gains[: 2 * dim // lanes].reshape(2, dim)
    gain_grads = lax.dynamic_slice_in_dim(gain_grads, i * w_rows, w_rows, 1)
    return (layer_out, input_grad, g_qkv, g_out, g_in, g_down, gain_grads[0], gain_grads[1])


def solution(mesh):
    rows = P(("rep", "inner"), None)
    weight = P("inner", None)
    return jax.shard_map(
        functools.partial(on_device, mesh.shape["rep"], mesh.shape["inner"]),
        mesh=mesh,
        in_specs=(rows, rows, weight, weight, weight, weight, P("inner"), P("inner")),
        out_specs=(rows, rows, weight, weight, weight, weight, P("inner"), P("inner")),
        check_vma=False,
    )
```

```python
import functools
import math

import jax
import jax.numpy as jnp
from jax import lax
from jax.experimental import pallas as pl
from jax.experimental.pallas import tpu as pltpu
from jax.sharding import PartitionSpec as P

HEAD_DIM = 64
EPSILON = 1e-05
THETA = 160000.0
F32 = jnp.float32
BF16 = jnp.bfloat16
NT = (((1,), (1,)), ((), ()))
TN = (((0,), (0,)), ((), ()))
VMEM_SPARE = 8 * 1024 * 1024
VMEM_WHOLE = 60 * 1024 * 1024


def dot(a, b):
    return jnp.dot(a, b, preferred_element_type=F32)


def dot_nt(a, b):
    return lax.dot_general(a, b, NT, preferred_element_type=F32)


def dot_tn(a, b):
    return lax.dot_general(a, b, TN, preferred_element_type=F32)


def call(body, outs, args, scratch=(), n_smem=0, n_any=0, far=(), far_outs=(), n_sems=0, whole=False, micros=1):
    n_passed = len(args) - n_any
    spaces = [pltpu.SMEM] * n_smem + [pltpu.VMEM] * (n_passed - n_smem) + [pltpu.HBM] * n_any
    for k in far:
        spaces[k] = pltpu.HBM
    held = sum(math.prod(s) * jnp.dtype(d).itemsize for s, d in scratch)

    def without_waited(*refs):
        body(*refs[:n_passed], *refs[len(args) :])

    return pl.pallas_call(
        without_waited,
        out_shape=[jax.ShapeDtypeStruct(s, d) for s, d in outs],
        in_specs=[pl.BlockSpec(memory_space=space) for space in spaces],
        out_specs=[pl.BlockSpec(memory_space=pltpu.HBM if k in far_outs else pltpu.VMEM) for k in range(len(outs))],
        scratch_shapes=[pltpu.VMEM(s, d) for s, d in scratch]
        + ([pltpu.SemaphoreType.DMA((n_sems,))] if n_sems else []),
        compiler_params=pltpu.CompilerParams(vmem_limit_bytes=VMEM_WHOLE if whole else held + VMEM_SPARE),
        cost_estimate=pl.CostEstimate(
            flops=int(micros * 1e9), transcendentals=0, bytes_accessed=int(micros * 1e6)
        ),
    )(*args)


class Copies:
    def __init__(self, sems):
        self.sems = sems
        self.used = 0

    def start(self, source, target):
        copy = pltpu.make_async_copy(source, target, self.sems.at[self.used])
        self.used += 1
        copy.start()
        return copy


def wait_all(copies):
    for copy in copies:
        copy.wait()


def after(value, *others):
    return lax.optimization_barrier((value, *others))[0]


def hat_of(values):
    centred = values - jnp.mean(values, axis=-1, keepdims=True)
    inv = lax.rsqrt(jnp.mean(centred * centred, axis=-1, keepdims=True) + EPSILON)
    return centred * inv, inv


def spot(block, size):
    return pl.ds(pl.multiple_of(block * size, size), size)


def partner(x):
    width = x.shape[-1]
    half = HEAD_DIM // 2
    lane = lax.broadcasted_iota(jnp.int32, x.shape, x.ndim - 1)
    ahead = pltpu.roll(x, width - half, 1)
    behind = pltpu.roll(x, half, 1)
    return jnp.where(lane % HEAD_DIM < half, ahead, behind)


def tile_lanes(table, width):
    return jnp.concatenate([table] * (width // table.shape[-1]), axis=-1)


def head_mask(h, width):
    lane = lax.broadcasted_iota(jnp.int32, (1, width), 1)
    return ((lane >= h * HEAD_DIM) & (lane < (h + 1) * HEAD_DIM)).astype(BF16)


def place_kernel(n_rep, at_ref, pieces, first_ref, second_ref):
    sub = pieces[0].shape[0] // 2
    for k in range(n_rep):
        spot = pl.ds(pl.multiple_of((at_ref[1] ^ k) * sub, sub), sub)
        first_ref[spot, :] = pieces[k][:sub, :]
        second_ref[spot, :] = pieces[k][sub:, :]


def send_back(n_rep, at_ref, scr, outs, first):
    sub = outs[0].shape[0] // 2
    for k in range(n_rep):
        block = at_ref[0] ^ k
        outs[k][first : first + sub, :] = scr[pl.ds(pl.multiple_of(block * sub, sub), sub), :].astype(BF16)


def weight_kernel(n_inner, n_part, at_ref, qkv_ref, out_ref, gains_ref, pack_ref):
    rows, dim = out_ref.shape
    lanes = pack_ref.shape[1]
    width = lanes // 4
    for p in range(3):
        start = pl.multiple_of(p * dim + at_ref[0] * width, width)
        pack_ref[:rows, p * width : (p + 1) * width] = qkv_ref[:, pl.ds(start, width)]
    start = pl.multiple_of(at_ref[0] * width, width)
    pack_ref[:rows, 3 * width :] = out_ref[:, pl.ds(start, width)]
    shard = lax.broadcasted_iota(jnp.int32, (2, dim), 1) // rows
    own = jnp.concatenate([gains_ref[...].astype(F32)] * n_inner, axis=1)
    own = jnp.where(shard == at_ref[1] * n_part + at_ref[2], own, 0.0)
    strips = [own[g : g + 1, k * lanes : (k + 1) * lanes] for g in range(2) for k in range(dim // lanes)]
    strips.append(jnp.zeros((8 - len(strips), lanes), F32))
    pack_ref[rows:, :] = jnp.concatenate(strips, axis=0).astype(BF16)


def packed_rows(pitch, dim, lanes):
    extra = pitch * dim // lanes
    spots = [(0, 0, 0, 0, extra, min(dim, lanes))]
    left = lanes - dim
    if left:
        rest = pitch - extra
        for c in range(dim // left):
            spots.append((c * rest, dim, extra, c * left, rest, left))
    return extra, spots


def ff_weight_kernel(n_rep, unit, pitch, at_ref, in_ref, down_ref, pack_ref, down_scr):
    rows = in_ref.shape[0]
    shard, dim = down_ref.shape
    lanes = pack_ref.shape[1]
    for jj in range(n_rep):
        size = min(unit, shard - jj * unit)

        @pl.when(at_ref[0] == jj)
        def _(jj=jj, size=size):
            pieces = []
            for p in range(in_ref.shape[1] // shard):
                first = p * shard + jj * unit
                pieces.append(in_ref[:, first : first + size])
                pieces.append(jnp.zeros((rows, pitch - size), BF16))
            pack_ref[:rows, :] = jnp.concatenate(pieces, axis=1)
            down_scr[:size, :] = down_ref[jj * unit : jj * unit + size, :]
            down_scr[size:, :] = jnp.zeros((pitch - size, dim), BF16)

    _, spots = packed_rows(pitch, dim, lanes)
    for row, lane, row_in, col_in, n, w in spots:
        pack_ref[rows + row : rows + row + n, lane : lane + w] = down_scr[row_in : row_in + n, col_in : col_in + w]


def qkv_kernel(
    n_rep, at_ref, refs_x, pack_ref, cos_ref, sin_ref, q_ref, kv_ref, a_out, w_out, gains_ref,
    a_ref, w_ref, rows_scr, sems,
):
    rows = refs_x[0].shape[0]
    width = q_ref.shape[1]
    dim = a_ref.shape[1]
    lanes = 4 * width
    n_inner, high, _ = pack_ref.shape
    w_rows = high - 8
    copies = Copies(sems)
    gains_in = copies.start(pack_ref.at[:, w_rows:, :], rows_scr)
    weights_in = copies.start(pack_ref.at[:, :w_rows, : 3 * width], w_ref)
    gains_in.wait()
    gains = rows_scr[0].astype(F32)
    for p in range(1, n_inner):
        gains = gains + rows_scr[p].astype(F32)
    per = dim // lanes
    for g in range(2):
        gains_ref[g : g + 1, :] = jnp.concatenate(
            [gains[g * per + k : g * per + k + 1, :] for k in range(per)], axis=1
        )
    for m in range(n_rep):
        hat, _ = hat_of(refs_x[m][...].astype(F32))
        a_ref[spot(at_ref[0] ^ m, rows), :] = (hat * gains_ref[0:1, :]).astype(BF16)
    weights_in.wait()
    done = [copies.start(a_ref, a_out), copies.start(w_ref, w_out)]
    weights = w_ref[...].reshape(dim, 3 * width)
    step = 2 * rows if n_rep % 2 == 0 else rows
    for r0 in range(0, n_rep * rows, step):
        sl = slice(r0, r0 + step)
        proj = dot(a_ref[sl, :], weights)
        cos = tile_lanes(cos_ref[sl, :], width)
        sin = tile_lanes(sin_ref[sl, :], width)
        query = proj[:, :width]
        key = proj[:, width : 2 * width]
        query = (query * cos + partner(query) * sin).astype(BF16).astype(F32)
        q_ref[sl, :] = (query * HEAD_DIM**-0.5).astype(BF16)
        kv_ref[sl, :width] = (key * cos + partner(key) * sin).astype(BF16)
        kv_ref[sl, width:] = proj[:, 2 * width :].astype(BF16)
    wait_all(done)


def attend_kernel(n_part, q_ref, refs_kv, o_ref, lse_ref, k_scr, vt_scr):
    rows, width = q_ref.shape
    keys = refs_kv[0].shape[0]
    for l in range(n_part):
        k_scr[l * keys : (l + 1) * keys, :] = refs_kv[l][:, :width]
        vt_scr[:, l * keys : (l + 1) * keys] = refs_kv[l][:, width:].astype(F32).T.astype(BF16)
    heads = width // HEAD_DIM
    step = min(256, rows)

    def body(c, carry):
        r0 = pl.multiple_of(c * step, step)
        for h in range(heads):
            pair = h // 2 * 128
            q = q_ref[pl.ds(r0, step), pair : pair + 128] * head_mask(h % 2, 128)
            s = dot_nt(k_scr[:, pair : pair + 128], q)
            top = jnp.max(s, axis=0, keepdims=True)
            e = jnp.exp(s - top)
            mass = jnp.sum(e, axis=0, keepdims=True)
            lse_ref[h : h + 1, pl.ds(r0, step)] = top + jnp.log(mass)
            ot = dot(vt_scr[h * HEAD_DIM : (h + 1) * HEAD_DIM, :], e.astype(BF16)) / mass
            ot_list.append(ot)
            if h % 2 == 1:
                both = jnp.concatenate(ot_list, axis=0)
                o_ref[pl.ds(r0, step), pair : pair + 128] = both.T.astype(BF16)
                ot_list.clear()
        return carry

    ot_list = []
    lax.fori_loop(0, rows // step, body, 0)


def ff_kernel(
    n_rep, n_part, at_ref, refs_x, refs_o, refs_wo, refs_wo_other, ffw_ref, refs_c, gains_ref,
    r_ref, refs_da, a_ref, m_ref, du_ref, o_out, wout_out, gain_ref,
    hat_scr, u_scr, dm_scr, win_scr, wdown_scr, x_scr, c_scr, o_scr, wout_scr, sems,
):
    rows, dim = refs_x[0].shape
    total = n_rep * rows
    quarter = refs_o[0].shape[1]
    j, t = at_ref[0], at_ref[2]
    _, w_rows, lanes = win_scr.shape
    copies = Copies(sems)
    first = []
    for m in range(n_rep):
        cols = spot(j ^ m, quarter)
        first.append(copies.start(refs_wo[m], wout_scr.at[:, t, :, cols]))
        for l in range(1, n_part):
            first.append(copies.start(refs_wo_other[l - 1].at[m], wout_scr.at[:, t ^ l, :, cols]))
        first.append(copies.start(refs_o[m], o_scr.at[:, cols]))
        first.append(copies.start(refs_x[m], x_scr.at[spot(j ^ m, rows), :]))
    second = copies.start(ffw_ref.at[:, :w_rows, :], win_scr)
    third = [copies.start(refs_c[m], c_scr.at[spot(j ^ m, rows), :]) for m in range(n_rep)]
    third += copy_down(copies, w_rows, ffw_ref, wdown_scr)
    wait_all(first)
    weights = wout_scr[...].reshape(dim, dim)
    last = [copies.start(o_scr, o_out)]
    hat_scr[...] = x_scr[...].astype(F32) + dot(o_scr[...], weights)
    r_ref[...] = hat_scr[spot(j, rows), :]
    per = quarter // w_rows // n_part
    for k in range(per):
        block = wout_scr.at[pl.ds(j * per + k, 1)]
        last.append(copies.start(block, wout_out.at[pl.ds(k, 1)]))
    gain = gains_ref[1:2, :]

    def norm_step(c, carry):
        r0 = pl.multiple_of(c * 64, 64)
        hat, _ = hat_of(hat_scr[pl.ds(r0, 64), :])
        hat_scr[pl.ds(r0, 64), :] = hat
        a_ref[pl.ds(r0, 64), :] = (hat * gain).astype(BF16)
        return carry

    lax.fori_loop(0, total // 64, norm_step, 0)
    second.wait()
    weights = win_scr[...].reshape(dim, lanes)
    u_scr[...] = dot(a_ref[...], weights)
    wait_all(third)
    dm_scr[...] = dot_nt(c_scr[...], wdown_scr[...].reshape(m_ref.shape[1], dim))
    width = m_ref.shape[1]

    def gate_step(c, carry):
        sl = pl.ds(pl.multiple_of(c * 32, 32), 32)
        pre = u_scr[sl, :width]
        gate = u_scr[sl, width:]
        dm = dm_scr[sl, :]
        cdf = 0.5 * (1.0 + lax.erf(pre * (0.5**0.5)))
        pdf = jnp.exp(-0.5 * pre * pre) * 0.3989422804014327
        act = pre * cdf
        m_ref[sl, :] = (act * gate).astype(BF16)
        du_ref[sl, :width] = (dm * gate * (cdf + pre * pdf)).astype(BF16)
        du_ref[sl, width:] = (dm * act).astype(BF16)
        return carry

    lax.fori_loop(0, total // 32, gate_step, 0)
    u_scr[:, :dim] = dot_nt(du_ref[...], win_scr[...].reshape(dim, lanes))
    total_gain = jnp.zeros((1, dim), F32)
    for m in range(n_rep):
        sl = spot(j ^ m, rows)
        da = u_scr[sl, :dim]
        refs_da[m][...] = da.astype(BF16)
        total_gain = total_gain + jnp.sum(da * hat_scr[sl, :], axis=0, keepdims=True)
    gain_ref[...] = total_gain
    wait_all(last)


def copy_down(copies, w_rows, ffw_ref, wdown_scr):
    _, pitch, dim = wdown_scr.shape
    _, spots = packed_rows(pitch, dim, ffw_ref.shape[2])
    started = []
    for row, lane, row_in, col_in, n, w in spots:
        source = ffw_ref.at[:, w_rows + row : w_rows + row + n, lane : lane + w]
        started.append(copies.start(source, wdown_scr.at[:, row_in : row_in + n, col_in : col_in + w]))
    return started


def ff_grads_kernel(
    n_rep, at_ref, m_ref, ffw_ref, refs_c, a_ref, du_ref, refs_lo, grad_out,
    down_scr, wdown_scr, c_scr, din_scr, sems,
):
    rows, dim = refs_lo[0].shape
    n_inner, w_rows, lanes = din_scr.shape
    pitch = down_scr.shape[1]
    j = at_ref[0]
    copies = Copies(sems)
    early = [copies.start(refs_c[m], c_scr.at[spot(j ^ m, rows), :]) for m in range(n_rep)]
    late = copy_down(copies, w_rows, ffw_ref, wdown_scr)
    din_scr[...] = dot_tn(a_ref[...], du_ref[...]).astype(BF16).reshape(n_inner, w_rows, lanes)
    sent = [copies.start(din_scr, grad_out.at[:, :w_rows, :])]
    wait_all(early)
    down_scr[...] = dot_tn(m_ref[...], c_scr[...]).astype(BF16).reshape(n_inner, pitch, dim)
    for row, lane, row_in, col_in, n, w in packed_rows(pitch, dim, lanes)[1]:
        source = down_scr.at[:, row_in : row_in + n, col_in : col_in + w]
        sent.append(copies.start(source, grad_out.at[:, w_rows + row : w_rows + row + n, lane : lane + w]))
    wait_all(late)
    down_scr_all = wdown_scr[...].reshape(n_inner * pitch, dim)
    c_scr[...] = dot(m_ref[...], down_scr_all).astype(BF16)
    for m in range(n_rep):
        refs_lo[m][...] = c_scr[spot(j ^ m, rows), :]
    wait_all(sent)


def norm_back(values, gain, grad):
    hat, inv = hat_of(values)
    dhat = grad * gain
    return inv * (
        dhat
        - jnp.mean(dhat, axis=-1, keepdims=True)
        - hat * jnp.mean(dhat * hat, axis=-1, keepdims=True)
    )


def sum_of(refs):
    total = refs[0][...].astype(F32)
    for ref in refs[1:]:
        total = total + ref[...].astype(F32)
    return total


def middle_kernel(n_rep, refs_da, r_ref, c_ref, gains_ref, dr_ref, dz_ref):
    dr = c_ref[...].astype(F32) + norm_back(r_ref[...], gains_ref[1:2, :], sum_of(refs_da))
    dr_ref[...] = dr
    dz_ref[...] = dr.astype(BF16)


def last_kernel(n_rep, at_ref, refs_da, refs_lo, x_ref, dr_ref, r_ref, gains_ref, outs, scr):
    rows = x_ref.shape[0]
    sub = rows // n_rep
    scr[...] = r_ref[...] + sum_of(refs_lo)
    send_back(n_rep, at_ref, scr, outs, sub)
    back = norm_back(x_ref[...].astype(F32), gains_ref[0:1, :], sum_of(refs_da))
    scr[...] = dr_ref[...] + back
    send_back(n_rep, at_ref, scr, outs, 0)


def attend_back_kernel(
    n_rep, n_part, sub_j, refs_dz, wout_ref, o_ref, q_ref, refs_kv, lse_ref, cos_ref, sin_ref,
    dq_ref, dkv_ref, refs_send, dz_ref, do_scr, k_scr, v_scr, kt_scr, delta_scr, dk_scr, dv_scr,
):
    rows, width = q_ref.shape
    keys = refs_kv[0].shape[0]
    part = refs_dz[0].shape[0]
    for m in range(n_rep):
        dz_ref[spot(sub_j[0] ^ m, part), :] = refs_dz[m][...]
    dout = dot_nt(dz_ref[...], wout_ref[...].reshape(width, dz_ref.shape[1])).astype(BF16)
    do_scr[...] = dout
    prod_t = (dout.astype(F32) * o_ref[...].astype(F32)).T
    heads = width // HEAD_DIM
    for h in range(heads):
        delta_scr[h : h + 1, :] = jnp.sum(
            prod_t[h * HEAD_DIM : (h + 1) * HEAD_DIM, :], axis=0, keepdims=True
        )
    for l in range(n_part):
        sl = slice(l * keys, (l + 1) * keys)
        k_scr[sl, :] = refs_kv[l][:, :width]
        v_scr[sl, :] = refs_kv[l][:, width:]
        kt_scr[:, sl] = refs_kv[l][:, :width].astype(F32).T.astype(BF16)
    dk_scr[...] = jnp.zeros_like(dk_scr)
    dv_scr[...] = jnp.zeros_like(dv_scr)
    step = min(256, rows)

    def body(c, carry):
        r0 = pl.multiple_of(c * step, step)
        for h in range(heads):
            pair = h // 2 * 128
            lanes = slice(pair, pair + 128)
            mask = head_mask(h % 2, 128)
            q = q_ref[pl.ds(r0, step), lanes] * mask
            do = do_scr[pl.ds(r0, step), lanes] * mask
            p = jnp.exp(dot_nt(k_scr[:, lanes], q) - lse_ref[h : h + 1, pl.ds(r0, step)])
            dp = dot_nt(v_scr[:, lanes], do)
            ds = (p * (dp - delta_scr[h : h + 1, pl.ds(r0, step)])).astype(BF16)
            dv_scr[:, lanes] += dot(p.astype(BF16), do)
            dk_scr[:, lanes] += dot(ds, q)
            dq_list.append(dot(kt_scr[h * HEAD_DIM : (h + 1) * HEAD_DIM, :], ds))
            if h % 2 == 1:
                dq = jnp.concatenate(dq_list, axis=0).T * HEAD_DIM**-0.5
                dq_list.clear()
                cos = cos_ref[pl.ds(r0, step), :]
                sin = sin_ref[pl.ds(r0, step), :]
                dq_ref[pl.ds(r0, step), lanes] = (dq * cos - partner(dq) * sin).astype(BF16)
        return carry

    dq_list = []
    lax.fori_loop(0, rows // step, body, 0)
    dkv_ref[:, :width] = dk_scr[:keys, :]
    dkv_ref[:, width:] = dv_scr[:keys, :]
    for l in range(1, n_part):
        sl = slice(l * keys, (l + 1) * keys)
        refs_send[l - 1][:, :width] = dk_scr[sl, :].astype(BF16)
        refs_send[l - 1][:, width:] = dv_scr[sl, :].astype(BF16)


def out_grad_kernel(sub_j, o_ref, dz_ref, dout_ref):
    quarter = dout_ref.shape[1]
    cols = dz_ref[:, pl.ds(pl.multiple_of(sub_j[0] * quarter, quarter), quarter)]
    dout_ref[...] = dot_tn(o_ref[...], cols).astype(BF16)


def qkv_back_kernel(
    n_rep, n_part, at_ref, dq_ref, dkv_ref, refs_got, cos_ref, sin_ref, a_ref, w_ref, refs_x, dout_ref,
    gain_two_ref, keep_ref, refs_send, refs_da, dp_scr, da_scr, grad_scr,
):
    width = dq_ref.shape[1]
    rows, dim = refs_x[0].shape
    lanes = 4 * width
    high = keep_ref.shape[0] // n_rep
    w_rows = high - 8
    dkv = dkv_ref[...]
    for got in refs_got:
        dkv = dkv + got[...].astype(F32)
    dk = dkv[:, :width]
    cos = tile_lanes(cos_ref[...], width)
    sin = tile_lanes(sin_ref[...], width)
    dp_scr[:, :width] = dq_ref[...]
    dp_scr[:, width : 2 * width] = (dk * cos - partner(dk) * sin).astype(BF16)
    dp_scr[:, 2 * width :] = dkv[:, width:].astype(BF16)
    grad_scr[:, : 3 * width] = dot_tn(a_ref[...], dp_scr[...]).astype(BF16)
    grad_scr[:, 3 * width :] = dout_ref[...]
    da_scr[...] = dot_nt(dp_scr[...], w_ref[...].reshape(dim, 3 * width))
    gain = jnp.zeros((1, dim), F32)
    for m in range(n_rep):
        da = da_scr[spot(at_ref[0] ^ m, rows), :]
        refs_da[m][...] = da.astype(BF16)
        hat, _ = hat_of(refs_x[m][...].astype(F32))
        gain = gain + jnp.sum(da * hat, axis=0, keepdims=True)
    per = dim // lanes
    strips = [g[:, k * lanes : (k + 1) * lanes] for g in (gain, gain_two_ref[...]) for k in range(per)]
    strips.append(jnp.zeros((8 - len(strips), lanes), F32))
    gains = jnp.concatenate(strips, axis=0).astype(BF16)
    for l in range(n_part):
        ref = keep_ref if l == 0 else refs_send[l - 1]
        for m in range(n_rep):
            shard = m * n_part + (at_ref[2] ^ l)
            ref[m * high : m * high + w_rows, :] = grad_scr[spot(shard, w_rows), :]
            ref[m * high + w_rows : (m + 1) * high, :] = gains


def part_sum_kernel(keep_ref, refs_got, out_ref):
    total = keep_ref[...].astype(F32)
    for got in refs_got:
        total = total + got[...].astype(F32)
    out_ref[...] = total.astype(BF16)


def grads_kernel(n_rep, at_ref, pieces, qkv_ref, out_ref, gains_ref):
    width = pieces[0].shape[1] // 4
    rows, dim = out_ref.shape
    for m in range(n_rep):
        for p in range(3):
            start = pl.multiple_of(p * dim + (at_ref[0] ^ m) * width, width)
            qkv_ref[:, pl.ds(start, width)] = pieces[m][:rows, p * width : (p + 1) * width].astype(F32)
        start = pl.multiple_of((at_ref[0] ^ m) * width, width)
        out_ref[:, pl.ds(start, width)] = pieces[m][:rows, 3 * width :].astype(F32)
    gains = pieces[0][rows:, :].astype(F32)
    for m in range(1, n_rep):
        gains = gains + pieces[m][rows:, :].astype(F32)
    gains_ref[...] = gains


def ff_out_kernel(n_rep, unit, pitch, cuts, at_ref, pieces, in_ref, down_ref, scr, down_scr):
    lanes = pieces[0].shape[1]
    rows = in_ref.shape[0]
    shard, dim = down_ref.shape
    for (m, top), piece in zip(cuts, pieces, strict=True):
        scr[at_ref[0] ^ m, top : top + piece.shape[0], :] = piece[...]
    _, spots = packed_rows(pitch, dim, lanes)
    strips = []
    for jj in range(n_rep):
        size = min(unit, shard - jj * unit)
        for row, lane, row_in, col_in, n, w in spots:
            down_scr[row_in : row_in + n, col_in : col_in + w] = scr[
                jj, rows + row : rows + row + n, lane : lane + w
            ].astype(F32)
        down_ref[jj * unit : jj * unit + size, :] = down_scr[:size, :]
    for p in range(lanes // pitch):
        strips = []
        for jj in range(n_rep):
            size = min(unit, shard - jj * unit)
            strips.append(scr[jj, :rows, p * pitch : p * pitch + size].astype(F32))
        in_ref[:, p * shard : (p + 1) * shard] = jnp.concatenate(strips, axis=1)


def split_refs(counts, refs):
    out, at = [], 0
    for n in counts:
        if n is None:
            out.append(refs[at])
            at += 1
        else:
            out.append(list(refs[at : at + n]))
            at += n
    return out


def grouped(kernel, static, counts):
    def body(*refs):
        kernel(*static, *split_refs(counts, refs))

    return body


def on_device(
    n_rep, n_inner,
    tokens, cotangent, qkv_weight, out_weight, in_weight, down_weight, gain_one, gain_two,
):
    part = n_inner // n_rep
    rows, dim = tokens.shape
    sub = rows // n_rep
    w_rows = qkv_weight.shape[0]
    width = dim // n_rep
    lanes = 4 * width
    high = w_rows + 8
    ff_shard = down_weight.shape[0]
    unit = -(-ff_shard // n_rep)
    pitch = -(-unit // 16) * 16
    ff = pitch * n_inner
    ff_high = w_rows + pitch * dim // (2 * ff)
    total = n_rep * rows
    j = lax.axis_index("rep")
    i = lax.axis_index("inner")
    s = i // part
    t = i % part
    at = jnp.stack([j, s, t]).astype(jnp.int32)

    def rep_swap(x, m):
        return lax.ppermute(x, "rep", [(a, a ^ m) for a in range(n_rep)])

    def plane_swap(x, m):
        pairs = [(a * part + b, (a ^ m) * part + b) for a in range(n_rep) for b in range(part)]
        return lax.ppermute(x, "inner", pairs)

    def part_swap(x, l):
        pairs = [(a * part + b, a * part + (b ^ l)) for a in range(n_rep) for b in range(part)]
        return lax.ppermute(x, "inner", pairs)

    def rep_gather(x):
        return [x] + [rep_swap(x, m) for m in range(1, n_rep)]

    def rep_spread(x):
        if n_rep != 4:
            return [[piece] for piece in rep_gather(x)]
        half = x.shape[0] // 2
        near = [rep_swap(x, 1), rep_swap(x, 2)]
        return [[x], [near[0]], [near[1]], [rep_swap(near[0][:half], 2), rep_swap(near[1][half:], 1)]]

    def rep_trade(pieces):
        return [pieces[0]] + [rep_swap(pieces[m], m) for m in range(1, n_rep)]

    def plane_trade(pieces):
        return [pieces[0]] + [plane_swap(pieces[m], m) for m in range(1, n_rep)]

    def send_home(pieces):
        got = []
        for k in range(n_rep):
            pairs = []
            for a in range(n_rep):
                for z in range(n_rep):
                    for b in range(part):
                        pairs.append((a * n_inner + z * part + b, z * n_inner + (a ^ k) * part + b))
            got.append(lax.ppermute(pieces[k], ("rep", "inner"), pairs))
        return got

    home = [((2 * sub, dim), BF16)] * n_rep
    planes = [[z * part + b for z in range(n_rep)] for b in range(part)]

    (w_pack,) = call(
        functools.partial(weight_kernel, n_inner, part), [((high, lanes), BF16)],
        [at, qkv_weight, out_weight, jnp.stack([gain_one, gain_two])], n_smem=1,
    )
    w_all = lax.all_gather(w_pack, "inner")
    x_first = lax.all_to_all(after(tokens, w_pack), "rep", 0, 0, tiled=True)
    in_late = after(in_weight, x_first)
    x_own = lax.all_to_all(x_first, "inner", 0, 0, axis_index_groups=planes, tiled=True)
    c_first = lax.all_to_all(after(cotangent, x_first), "rep", 0, 0, tiled=True)
    x_own = after(x_own, c_first)
    c_own = lax.all_to_all(after(c_first, x_own), "inner", 0, 0, axis_index_groups=planes, tiled=True)
    xs = rep_gather(x_own)
    (ff_pack,) = call(
        grouped(ff_weight_kernel, (n_rep, unit, pitch), (None,) * 5),
        [((ff_high, 2 * ff), BF16)],
        [at, in_late, down_weight, w_pack],
        [((pitch, dim), BF16)],
        n_smem=1, n_any=1,
    )
    ff_w = lax.all_gather(ff_pack, "inner")

    own = w_all.reshape(n_rep, part, high, lanes)
    own = lax.dynamic_slice_in_dim(own, t, 1, 1)[:, 0, :w_rows, 3 * width :].reshape(n_rep * w_rows, width)
    wo_own = rep_gather(after(own.reshape(n_rep, w_rows, width), xs[-1]))
    wo_other = [part_swap(jnp.stack(wo_own), l) for l in range(1, part)]

    order = jnp.arange(total, dtype=jnp.int32)
    place = ((order // sub % n_rep) * part + t) * rows + (order // rows) * sub + order % sub
    inv_freq = 1.0 / THETA ** (jnp.arange(HEAD_DIM // 2, dtype=F32) * (2.0 / HEAD_DIM))
    angle = place.astype(F32)[:, None] * inv_freq[None, :]
    cos_half, sin_half = jnp.cos(angle), jnp.sin(angle)
    cos = jnp.concatenate([cos_half] * 4, axis=1)
    sin = jnp.concatenate([-sin_half, sin_half] * 2, axis=1)

    q, kv, a_one, w_qkv, gains = call(
        grouped(qkv_kernel, (n_rep,), (None, n_rep) + (None,) * 12),
        [
            ((total, width), BF16), ((total, 2 * width), BF16), ((total, dim), BF16),
            ((n_inner, w_rows, 3 * width), BF16), ((2, dim), F32),
        ],
        [at, *xs, w_all, cos, sin, c_own],
        [((total, dim), BF16), ((n_inner, w_rows, 3 * width), BF16), ((n_inner, 8, lanes), BF16)],
        n_smem=1, n_any=1, far=(1 + n_rep,), far_outs=(2, 3), n_sems=4, whole=True, micros=2,
    )
    kvs = [kv] + [part_swap(kv, l) for l in range(1, part)]
    heads = width // HEAD_DIM
    stat_rows = -(-heads // 8) * 8
    o, lse = call(
        grouped(attend_kernel, (part,), (None, part) + (None,) * 4),
        [((total, width), BF16), ((stat_rows, total), F32)],
        [q, *kvs, *wo_own[1:]],
        [((total * part, width), BF16), ((width, total * part), BF16)],
        n_any=n_rep - 1, micros=6,
    )
    os_ = rep_gather(o)
    cs = rep_gather(after(c_own, xs[-1]))
    n_spots = len(packed_rows(pitch, dim, 2 * ff)[1])
    per = width // (part * w_rows)
    ff_out = call(
        grouped(
            ff_kernel, (n_rep, part),
            (None, n_rep, n_rep, n_rep, part - 1, None, n_rep, None, None, n_rep) + (None,) * 16,
        ),
        [((rows, dim), F32)]
        + [((rows, dim), BF16)] * n_rep
        + [
            ((total, dim), BF16), ((total, ff), BF16), ((total, 2 * ff), BF16),
            ((total, dim), BF16), ((per, part, w_rows, dim), BF16), ((1, dim), F32),
        ],
        [at, *xs, *os_, *wo_own, *wo_other, ff_w, *cs, gains],
        [
            ((total, dim), F32), ((total, 2 * ff), F32), ((total, ff), F32), ((n_inner, w_rows, 2 * ff), BF16),
            ((n_inner, pitch, dim), BF16), ((total, dim), BF16), ((total, dim), BF16), ((total, dim), BF16),
            ((n_rep, part, w_rows, dim), BF16),
        ],
        n_smem=1, far=range(1, 1 + 4 * n_rep + part), far_outs=(4 + n_rep, 5 + n_rep),
        n_sems=n_rep * (part + 3) + 1 + n_spots + 1 + per, whole=True, micros=11,
    )
    r_own, da_two = ff_out[0], ff_out[1 : 1 + n_rep]
    a_two, gated, d_hidden, o_all, w_out, gain_two_part = ff_out[1 + n_rep :]
    das = rep_trade(da_two)
    ff_back = call(
        grouped(ff_grads_kernel, (n_rep,), (None, None, None, n_rep, None, None, n_rep) + (None,) * 6),
        [((rows, dim), BF16)] * n_rep + [((n_inner, ff_high, 2 * ff), BF16)],
        [at, gated, ff_w, *cs, a_two, d_hidden],
        [
            ((n_inner, pitch, dim), BF16), ((n_inner, pitch, dim), BF16), ((total, dim), BF16),
            ((n_inner, w_rows, 2 * ff), BF16),
        ],
        n_smem=1, far=range(2, 3 + n_rep), far_outs=(n_rep,), n_sems=n_rep + 2 * n_spots + 1, whole=True, micros=5,
    )
    lo, ff_grad = ff_back[:-1], ff_back[-1]
    dr, dz = call(
        grouped(middle_kernel, (n_rep,), (n_rep,) + (None,) * 5),
        [((rows, dim), F32), ((rows, dim), BF16)],
        [*das, r_own, c_own, gains, lo[0]],
        n_any=1, micros=2,
    )
    ff_grad = lax.psum_scatter(after(ff_grad, das[1]), "inner", scatter_dimension=0)
    dzs = rep_gather(dz)

    back = call(
        grouped(
            attend_back_kernel,
            (n_rep, part),
            (None, n_rep, None, None, None, part, None, None, None, None, None, part - 1, None) + (None,) * 7,
        ),
        [((total, width), BF16), ((total, 2 * width), F32)]
        + [((total, 2 * width), BF16)] * (part - 1)
        + [((total, dim), BF16)],
        [at, *dzs, w_out, o, q, *kvs, lse, cos, sin],
        [
            ((total, width), BF16), ((total * part, width), BF16), ((total * part, width), BF16),
            ((width, total * part), BF16), ((stat_rows, total), F32),
            ((total * part, width), F32), ((total * part, width), F32),
        ],
        n_smem=1, micros=10,
    )
    dq, dkv, sends, dz_all = back[0], back[1], back[2:-1], back[-1]
    los = rep_trade([after(x, dzs[-1]) for x in lo])
    gots = [part_swap(after(x, *los[1:]), l + 1) for l, x in enumerate(sends)]
    (d_out,) = call(
        out_grad_kernel, [((dim, width), BF16)], [at, o_all, dz_all], n_smem=1, micros=2,
    )
    qkv_out = call(
        grouped(
            qkv_back_kernel, (n_rep, part),
            (None, None, None, part - 1, None, None, None, None, n_rep, None, None, None, part - 1, n_rep) + (None,) * 3,
        ),
        [((n_rep * high, lanes), BF16)] * part + [((rows, dim), BF16)] * n_rep,
        [at, dq, dkv, *gots, cos, sin, a_one, w_qkv, *xs, d_out, gain_two_part],
        [((total, 3 * width), BF16), ((total, dim), F32), ((dim, lanes), BF16)],
        n_smem=1, micros=4,
    )
    keep, sends, da_one = qkv_out[0], qkv_out[1:part], qkv_out[part:]
    gots = [part_swap(x, l + 1) for l, x in enumerate(sends)]
    (summed,) = call(
        grouped(part_sum_kernel, (), (None, part - 1, None)), [((n_rep * high, lanes), BF16)], [keep, *gots]
    )
    das = rep_trade(da_one)
    d_pack = lax.psum_scatter(
        after(summed, ff_grad), "inner", scatter_dimension=0, axis_index_groups=planes, tiled=True
    )
    parts = call(
        grouped(last_kernel, (n_rep,), (None, n_rep, n_rep, None, None, None, None, n_rep, None)),
        home, [at, *das, *los, xs[0], dr, r_own, gains], [((rows, dim), F32)], n_smem=1, whole=True, micros=2,
    )
    ff_grads = rep_spread(after(ff_grad, *das[1:]))
    back_home = send_home(parts)
    quarter = after(d_pack, back_home[1])
    input_grad, layer_out = call(
        grouped(place_kernel, (n_rep,), (None, n_rep, None, None)),
        [((rows, dim), BF16)] * 2, [at, *back_home, d_pack], n_smem=1, n_any=1,
    )
    g_qkv, g_out, g_gains = call(
        grouped(grads_kernel, (n_rep,), (None, n_rep, None, None, None)),
        [((w_rows, 3 * dim), F32), ((w_rows, dim), F32), ((8, lanes), F32)],
        [at, *rep_gather(quarter)],
        n_smem=1, micros=2,
    )
    cuts, flat = [], []
    for m, pieces in enumerate(ff_grads):
        top = 0
        for piece in pieces:
            cuts.append((m, top))
            flat.append(piece)
            top += piece.shape[0]
    g_in, g_down = call(
        grouped(ff_out_kernel, (n_rep, unit, pitch, cuts), (None, len(flat)) + (None,) * 4),
        [((w_rows, 2 * n_inner * ff_shard), F32), ((ff_shard, dim), F32)],
        [at, *flat, d_pack],
        [((n_rep, ff_high, 2 * ff), BF16), ((pitch, dim), F32)],
        n_smem=1, n_any=1, micros=4,
    )
    gain_grads = g_gains[: 2 * dim // lanes].reshape(2, dim)
    gain_grads = lax.dynamic_slice_in_dim(gain_grads, i * w_rows, w_rows, 1)
    return (layer_out, input_grad, g_qkv, g_out, g_in, g_down, gain_grads[0], gain_grads[1])


def solution(mesh):
    rows = P(("rep", "inner"), None)
    weight = P("inner", None)
    return jax.shard_map(
        functools.partial(on_device, mesh.shape["rep"], mesh.shape["inner"]),
        mesh=mesh,
        in_specs=(rows, rows, weight, weight, weight, weight, P("inner"), P("inner")),
        out_specs=(rows, rows, weight, weight, weight, weight, P("inner"), P("inner")),
        check_vma=False,
    )
```

```python
import functools
import math

import jax
import jax.numpy as jnp
from jax import lax
from jax.experimental import pallas as pl
from jax.experimental.pallas import tpu as pltpu
from jax.sharding import PartitionSpec as P

HEAD_DIM = 64
EPSILON = 1e-05
THETA = 160000.0
F32 = jnp.float32
BF16 = jnp.bfloat16
NT = (((1,), (1,)), ((), ()))
TN = (((0,), (0,)), ((), ()))
VMEM_SPARE = 8 * 1024 * 1024
VMEM_WHOLE = 60 * 1024 * 1024


def dot(a, b):
    return jnp.dot(a, b, preferred_element_type=F32)


def dot_nt(a, b):
    return lax.dot_general(a, b, NT, preferred_element_type=F32)


def dot_tn(a, b):
    return lax.dot_general(a, b, TN, preferred_element_type=F32)


def call(body, outs, args, scratch=(), n_smem=0, n_any=0, far=(), far_outs=(), n_sems=0, whole=False, micros=1):
    n_passed = len(args) - n_any
    spaces = [pltpu.SMEM] * n_smem + [pltpu.VMEM] * (n_passed - n_smem) + [pltpu.HBM] * n_any
    for k in far:
        spaces[k] = pltpu.HBM
    held = sum(math.prod(s) * jnp.dtype(d).itemsize for s, d in scratch)

    def without_waited(*refs):
        body(*refs[:n_passed], *refs[len(args) :])

    return pl.pallas_call(
        without_waited,
        out_shape=[jax.ShapeDtypeStruct(s, d) for s, d in outs],
        in_specs=[pl.BlockSpec(memory_space=space) for space in spaces],
        out_specs=[pl.BlockSpec(memory_space=pltpu.HBM if k in far_outs else pltpu.VMEM) for k in range(len(outs))],
        scratch_shapes=[pltpu.VMEM(s, d) for s, d in scratch]
        + ([pltpu.SemaphoreType.DMA((n_sems,))] if n_sems else []),
        compiler_params=pltpu.CompilerParams(vmem_limit_bytes=VMEM_WHOLE if whole else held + VMEM_SPARE),
        cost_estimate=pl.CostEstimate(
            flops=int(micros * 1e9), transcendentals=0, bytes_accessed=int(micros * 1e6)
        ),
    )(*args)


class Copies:
    def __init__(self, sems):
        self.sems = sems
        self.used = 0

    def start(self, source, target):
        copy = pltpu.make_async_copy(source, target, self.sems.at[self.used])
        self.used += 1
        copy.start()
        return copy


def wait_all(copies):
    for copy in copies:
        copy.wait()


def after(value, *others):
    return lax.optimization_barrier((value, *others))[0]


def hat_of(values):
    centred = values - jnp.mean(values, axis=-1, keepdims=True)
    inv = lax.rsqrt(jnp.mean(centred * centred, axis=-1, keepdims=True) + EPSILON)
    return centred * inv, inv


def spot(block, size):
    return pl.ds(pl.multiple_of(block * size, size), size)


def partner(x):
    width = x.shape[-1]
    half = HEAD_DIM // 2
    lane = lax.broadcasted_iota(jnp.int32, x.shape, x.ndim - 1)
    ahead = pltpu.roll(x, width - half, 1)
    behind = pltpu.roll(x, half, 1)
    return jnp.where(lane % HEAD_DIM < half, ahead, behind)


def tile_lanes(table, width):
    return jnp.concatenate([table] * (width // table.shape[-1]), axis=-1)


def head_mask(h, width):
    lane = lax.broadcasted_iota(jnp.int32, (1, width), 1)
    return ((lane >= h * HEAD_DIM) & (lane < (h + 1) * HEAD_DIM)).astype(BF16)


def place_kernel(n_rep, at_ref, pieces, first_ref, second_ref):
    sub = pieces[0].shape[0] // 2
    for k in range(n_rep):
        spot = pl.ds(pl.multiple_of((at_ref[1] ^ k) * sub, sub), sub)
        first_ref[spot, :] = pieces[k][:sub, :]
        second_ref[spot, :] = pieces[k][sub:, :]


def send_back(n_rep, at_ref, scr, outs, first):
    sub = outs[0].shape[0] // 2
    for k in range(n_rep):
        block = at_ref[0] ^ k
        outs[k][first : first + sub, :] = scr[pl.ds(pl.multiple_of(block * sub, sub), sub), :].astype(BF16)


def weight_kernel(n_inner, n_part, at_ref, qkv_ref, out_ref, gains_ref, pack_ref):
    rows, dim = out_ref.shape
    lanes = pack_ref.shape[1]
    width = lanes // 4
    for p in range(3):
        start = pl.multiple_of(p * dim + at_ref[0] * width, width)
        pack_ref[:rows, p * width : (p + 1) * width] = qkv_ref[:, pl.ds(start, width)]
    start = pl.multiple_of(at_ref[0] * width, width)
    pack_ref[:rows, 3 * width :] = out_ref[:, pl.ds(start, width)]
    shard = lax.broadcasted_iota(jnp.int32, (2, dim), 1) // rows
    own = jnp.concatenate([gains_ref[...].astype(F32)] * n_inner, axis=1)
    own = jnp.where(shard == at_ref[1] * n_part + at_ref[2], own, 0.0)
    strips = [own[g : g + 1, k * lanes : (k + 1) * lanes] for g in range(2) for k in range(dim // lanes)]
    strips.append(jnp.zeros((8 - len(strips), lanes), F32))
    pack_ref[rows:, :] = jnp.concatenate(strips, axis=0).astype(BF16)


def packed_rows(pitch, dim, lanes):
    extra = pitch * dim // lanes
    spots = [(0, 0, 0, 0, extra, min(dim, lanes))]
    left = lanes - dim
    if left:
        rest = pitch - extra
        for c in range(dim // left):
            spots.append((c * rest, dim, extra, c * left, rest, left))
    return extra, spots


def ff_weight_kernel(n_rep, unit, pitch, at_ref, in_ref, down_ref, pack_ref, down_scr):
    rows = in_ref.shape[0]
    shard, dim = down_ref.shape
    lanes = pack_ref.shape[1]
    for jj in range(n_rep):
        size = min(unit, shard - jj * unit)

        @pl.when(at_ref[0] == jj)
        def _(jj=jj, size=size):
            pieces = []
            for p in range(in_ref.shape[1] // shard):
                first = p * shard + jj * unit
                pieces.append(in_ref[:, first : first + size])
                pieces.append(jnp.zeros((rows, pitch - size), BF16))
            pack_ref[:rows, :] = jnp.concatenate(pieces, axis=1)
            down_scr[:size, :] = down_ref[jj * unit : jj * unit + size, :]
            down_scr[size:, :] = jnp.zeros((pitch - size, dim), BF16)

    _, spots = packed_rows(pitch, dim, lanes)
    for row, lane, row_in, col_in, n, w in spots:
        pack_ref[rows + row : rows + row + n, lane : lane + w] = down_scr[row_in : row_in + n, col_in : col_in + w]


def qkv_kernel(
    n_rep, at_ref, refs_x, pack_ref, cos_ref, sin_ref, q_ref, kv_ref, a_out, w_out, gains_ref,
    a_ref, w_ref, rows_scr, sems,
):
    rows = refs_x[0].shape[0]
    width = q_ref.shape[1]
    dim = a_ref.shape[1]
    lanes = 4 * width
    n_inner, high, _ = pack_ref.shape
    w_rows = high - 8
    copies = Copies(sems)
    gains_in = copies.start(pack_ref.at[:, w_rows:, :], rows_scr)
    weights_in = copies.start(pack_ref.at[:, :w_rows, : 3 * width], w_ref)
    gains_in.wait()
    gains = rows_scr[0].astype(F32)
    for p in range(1, n_inner):
        gains = gains + rows_scr[p].astype(F32)
    per = dim // lanes
    for g in range(2):
        gains_ref[g : g + 1, :] = jnp.concatenate(
            [gains[g * per + k : g * per + k + 1, :] for k in range(per)], axis=1
        )
    for m in range(n_rep):
        hat, _ = hat_of(refs_x[m][...].astype(F32))
        a_ref[spot(at_ref[0] ^ m, rows), :] = (hat * gains_ref[0:1, :]).astype(BF16)
    weights_in.wait()
    done = [copies.start(a_ref, a_out), copies.start(w_ref, w_out)]
    weights = w_ref[...].reshape(dim, 3 * width)
    step = 2 * rows if n_rep % 2 == 0 else rows
    for r0 in range(0, n_rep * rows, step):
        sl = slice(r0, r0 + step)
        proj = dot(a_ref[sl, :], weights)
        cos = tile_lanes(cos_ref[sl, :], width)
        sin = tile_lanes(sin_ref[sl, :], width)
        query = proj[:, :width]
        key = proj[:, width : 2 * width]
        query = (query * cos + partner(query) * sin).astype(BF16).astype(F32)
        q_ref[sl, :] = (query * HEAD_DIM**-0.5).astype(BF16)
        kv_ref[sl, :width] = (key * cos + partner(key) * sin).astype(BF16)
        kv_ref[sl, width:] = proj[:, 2 * width :].astype(BF16)
    wait_all(done)


def attend_kernel(n_part, q_ref, refs_kv, o_ref, lse_ref, k_scr, vt_scr):
    rows, width = q_ref.shape
    keys = refs_kv[0].shape[0]
    for l in range(n_part):
        k_scr[l * keys : (l + 1) * keys, :] = refs_kv[l][:, :width]
        vt_scr[:, l * keys : (l + 1) * keys] = refs_kv[l][:, width:].astype(F32).T.astype(BF16)
    heads = width // HEAD_DIM
    step = min(256, rows)

    def body(c, carry):
        r0 = pl.multiple_of(c * step, step)
        for h in range(heads):
            pair = h // 2 * 128
            q = q_ref[pl.ds(r0, step), pair : pair + 128] * head_mask(h % 2, 128)
            s = dot_nt(k_scr[:, pair : pair + 128], q)
            top = jnp.max(s, axis=0, keepdims=True)
            e = jnp.exp(s - top)
            mass = jnp.sum(e, axis=0, keepdims=True)
            lse_ref[h : h + 1, pl.ds(r0, step)] = top + jnp.log(mass)
            ot = dot(vt_scr[h * HEAD_DIM : (h + 1) * HEAD_DIM, :], e.astype(BF16)) / mass
            ot_list.append(ot)
            if h % 2 == 1:
                both = jnp.concatenate(ot_list, axis=0)
                o_ref[pl.ds(r0, step), pair : pair + 128] = both.T.astype(BF16)
                ot_list.clear()
        return carry

    ot_list = []
    lax.fori_loop(0, rows // step, body, 0)


def ff_kernel(
    n_rep, n_part, at_ref, refs_x, refs_o, refs_wo, refs_wo_other, ffw_ref, refs_c, gains_ref,
    r_ref, refs_da, a_ref, m_ref, du_ref, o_out, wout_out, gain_ref,
    hat_scr, u_scr, dm_scr, win_scr, wdown_scr, x_scr, c_scr, o_scr, wout_scr, sems,
):
    rows, dim = refs_x[0].shape
    total = n_rep * rows
    quarter = refs_o[0].shape[1]
    j, t = at_ref[0], at_ref[2]
    _, w_rows, lanes = win_scr.shape
    copies = Copies(sems)
    first = []
    for m in range(n_rep):
        cols = spot(j ^ m, quarter)
        first.append(copies.start(refs_wo[m], wout_scr.at[:, t, :, cols]))
        for l in range(1, n_part):
            first.append(copies.start(refs_wo_other[l - 1].at[m], wout_scr.at[:, t ^ l, :, cols]))
        first.append(copies.start(refs_o[m], o_scr.at[:, cols]))
        first.append(copies.start(refs_x[m], x_scr.at[spot(j ^ m, rows), :]))
    second = copies.start(ffw_ref.at[:, :w_rows, :], win_scr)
    third = [copies.start(refs_c[m], c_scr.at[spot(j ^ m, rows), :]) for m in range(n_rep)]
    third += copy_down(copies, w_rows, ffw_ref, wdown_scr)
    wait_all(first)
    weights = wout_scr[...].reshape(dim, dim)
    last = [copies.start(o_scr, o_out)]
    hat_scr[...] = x_scr[...].astype(F32) + dot(o_scr[...], weights)
    r_ref[...] = hat_scr[spot(j, rows), :]
    per = quarter // w_rows // n_part
    for k in range(per):
        block = wout_scr.at[pl.ds(j * per + k, 1)]
        last.append(copies.start(block, wout_out.at[pl.ds(k, 1)]))
    gain = gains_ref[1:2, :]

    def norm_step(c, carry):
        r0 = pl.multiple_of(c * 64, 64)
        hat, _ = hat_of(hat_scr[pl.ds(r0, 64), :])
        hat_scr[pl.ds(r0, 64), :] = hat
        a_ref[pl.ds(r0, 64), :] = (hat * gain).astype(BF16)
        return carry

    lax.fori_loop(0, total // 64, norm_step, 0)
    second.wait()
    weights = win_scr[...].reshape(dim, lanes)
    u_scr[...] = dot(a_ref[...], weights)
    wait_all(third)
    dm_scr[...] = dot_nt(c_scr[...], wdown_scr[...].reshape(m_ref.shape[1], dim))
    width = m_ref.shape[1]

    def gate_step(c, carry):
        sl = pl.ds(pl.multiple_of(c * 32, 32), 32)
        pre = u_scr[sl, :width]
        gate = u_scr[sl, width:]
        dm = dm_scr[sl, :]
        cdf = 0.5 * (1.0 + lax.erf(pre * (0.5**0.5)))
        pdf = jnp.exp(-0.5 * pre * pre) * 0.3989422804014327
        act = pre * cdf
        m_ref[sl, :] = (act * gate).astype(BF16)
        du_ref[sl, :width] = (dm * gate * (cdf + pre * pdf)).astype(BF16)
        du_ref[sl, width:] = (dm * act).astype(BF16)
        return carry

    lax.fori_loop(0, total // 32, gate_step, 0)
    u_scr[:, :dim] = dot_nt(du_ref[...], win_scr[...].reshape(dim, lanes))
    total_gain = jnp.zeros((1, dim), F32)
    for m in range(n_rep):
        sl = spot(j ^ m, rows)
        da = u_scr[sl, :dim]
        refs_da[m][...] = da.astype(BF16)
        total_gain = total_gain + jnp.sum(da * hat_scr[sl, :], axis=0, keepdims=True)
    gain_ref[...] = total_gain
    wait_all(last)


def copy_down(copies, w_rows, ffw_ref, wdown_scr):
    _, pitch, dim = wdown_scr.shape
    _, spots = packed_rows(pitch, dim, ffw_ref.shape[2])
    started = []
    for row, lane, row_in, col_in, n, w in spots:
        source = ffw_ref.at[:, w_rows + row : w_rows + row + n, lane : lane + w]
        started.append(copies.start(source, wdown_scr.at[:, row_in : row_in + n, col_in : col_in + w]))
    return started


def ff_grads_kernel(
    n_rep, at_ref, m_ref, ffw_ref, refs_c, a_ref, du_ref, refs_lo, grad_out,
    down_scr, wdown_scr, c_scr, din_scr, sems,
):
    rows, dim = refs_lo[0].shape
    n_inner, w_rows, lanes = din_scr.shape
    pitch = down_scr.shape[1]
    j = at_ref[0]
    copies = Copies(sems)
    early = [copies.start(refs_c[m], c_scr.at[spot(j ^ m, rows), :]) for m in range(n_rep)]
    late = copy_down(copies, w_rows, ffw_ref, wdown_scr)
    din_scr[...] = dot_tn(a_ref[...], du_ref[...]).astype(BF16).reshape(n_inner, w_rows, lanes)
    sent = [copies.start(din_scr, grad_out.at[:, :w_rows, :])]
    wait_all(early)
    down_scr[...] = dot_tn(m_ref[...], c_scr[...]).astype(BF16).reshape(n_inner, pitch, dim)
    for row, lane, row_in, col_in, n, w in packed_rows(pitch, dim, lanes)[1]:
        source = down_scr.at[:, row_in : row_in + n, col_in : col_in + w]
        sent.append(copies.start(source, grad_out.at[:, w_rows + row : w_rows + row + n, lane : lane + w]))
    wait_all(late)
    down_scr_all = wdown_scr[...].reshape(n_inner * pitch, dim)
    c_scr[...] = dot(m_ref[...], down_scr_all).astype(BF16)
    for m in range(n_rep):
        refs_lo[m][...] = c_scr[spot(j ^ m, rows), :]
    wait_all(sent)


def norm_back(values, gain, grad):
    hat, inv = hat_of(values)
    dhat = grad * gain
    return inv * (
        dhat
        - jnp.mean(dhat, axis=-1, keepdims=True)
        - hat * jnp.mean(dhat * hat, axis=-1, keepdims=True)
    )


def sum_of(refs):
    total = refs[0][...].astype(F32)
    for ref in refs[1:]:
        total = total + ref[...].astype(F32)
    return total


def middle_kernel(n_rep, refs_da, r_ref, c_ref, gains_ref, dr_ref, dz_ref):
    dr = c_ref[...].astype(F32) + norm_back(r_ref[...], gains_ref[1:2, :], sum_of(refs_da))
    dr_ref[...] = dr
    dz_ref[...] = dr.astype(BF16)


def last_kernel(n_rep, at_ref, refs_da, refs_lo, x_ref, dr_ref, r_ref, gains_ref, outs, scr):
    rows = x_ref.shape[0]
    sub = rows // n_rep
    scr[...] = r_ref[...] + sum_of(refs_lo)
    send_back(n_rep, at_ref, scr, outs, sub)
    back = norm_back(x_ref[...].astype(F32), gains_ref[0:1, :], sum_of(refs_da))
    scr[...] = dr_ref[...] + back
    send_back(n_rep, at_ref, scr, outs, 0)


def attend_back_kernel(
    n_rep, n_part, sub_j, refs_dz, wout_ref, o_ref, q_ref, refs_kv, lse_ref, cos_ref, sin_ref,
    dq_ref, dkv_ref, refs_send, dz_ref, do_scr, k_scr, v_scr, kt_scr, delta_scr, dk_scr, dv_scr,
):
    rows, width = q_ref.shape
    keys = refs_kv[0].shape[0]
    part = refs_dz[0].shape[0]
    for m in range(n_rep):
        dz_ref[spot(sub_j[0] ^ m, part), :] = refs_dz[m][...]
    dout = dot_nt(dz_ref[...], wout_ref[...].reshape(width, dz_ref.shape[1])).astype(BF16)
    do_scr[...] = dout
    prod_t = (dout.astype(F32) * o_ref[...].astype(F32)).T
    heads = width // HEAD_DIM
    for h in range(heads):
        delta_scr[h : h + 1, :] = jnp.sum(
            prod_t[h * HEAD_DIM : (h + 1) * HEAD_DIM, :], axis=0, keepdims=True
        )
    for l in range(n_part):
        sl = slice(l * keys, (l + 1) * keys)
        k_scr[sl, :] = refs_kv[l][:, :width]
        v_scr[sl, :] = refs_kv[l][:, width:]
        kt_scr[:, sl] = refs_kv[l][:, :width].astype(F32).T.astype(BF16)
    dk_scr[...] = jnp.zeros_like(dk_scr)
    dv_scr[...] = jnp.zeros_like(dv_scr)
    step = min(256, rows)

    def body(c, carry):
        r0 = pl.multiple_of(c * step, step)
        for h in range(heads):
            pair = h // 2 * 128
            lanes = slice(pair, pair + 128)
            mask = head_mask(h % 2, 128)
            q = q_ref[pl.ds(r0, step), lanes] * mask
            do = do_scr[pl.ds(r0, step), lanes] * mask
            p = jnp.exp(dot_nt(k_scr[:, lanes], q) - lse_ref[h : h + 1, pl.ds(r0, step)])
            dp = dot_nt(v_scr[:, lanes], do)
            ds = (p * (dp - delta_scr[h : h + 1, pl.ds(r0, step)])).astype(BF16)
            dv_scr[:, lanes] += dot(p.astype(BF16), do)
            dk_scr[:, lanes] += dot(ds, q)
            dq_list.append(dot(kt_scr[h * HEAD_DIM : (h + 1) * HEAD_DIM, :], ds))
            if h % 2 == 1:
                dq = jnp.concatenate(dq_list, axis=0).T * HEAD_DIM**-0.5
                dq_list.clear()
                cos = cos_ref[pl.ds(r0, step), :]
                sin = sin_ref[pl.ds(r0, step), :]
                dq_ref[pl.ds(r0, step), lanes] = (dq * cos - partner(dq) * sin).astype(BF16)
        return carry

    dq_list = []
    lax.fori_loop(0, rows // step, body, 0)
    dkv_ref[:, :width] = dk_scr[:keys, :]
    dkv_ref[:, width:] = dv_scr[:keys, :]
    for l in range(1, n_part):
        sl = slice(l * keys, (l + 1) * keys)
        refs_send[l - 1][:, :width] = dk_scr[sl, :].astype(BF16)
        refs_send[l - 1][:, width:] = dv_scr[sl, :].astype(BF16)


def out_grad_kernel(sub_j, o_ref, dz_ref, dout_ref):
    quarter = dout_ref.shape[1]
    cols = dz_ref[:, pl.ds(pl.multiple_of(sub_j[0] * quarter, quarter), quarter)]
    dout_ref[...] = dot_tn(o_ref[...], cols).astype(BF16)


def qkv_back_kernel(
    n_rep, n_part, at_ref, dq_ref, dkv_ref, refs_got, cos_ref, sin_ref, a_ref, w_ref, refs_x, dout_ref,
    gain_two_ref, keep_ref, refs_send, refs_da, dp_scr, da_scr, grad_scr,
):
    width = dq_ref.shape[1]
    rows, dim = refs_x[0].shape
    lanes = 4 * width
    high = keep_ref.shape[0] // n_rep
    w_rows = high - 8
    dkv = dkv_ref[...]
    for got in refs_got:
        dkv = dkv + got[...].astype(F32)
    dk = dkv[:, :width]
    cos = tile_lanes(cos_ref[...], width)
    sin = tile_lanes(sin_ref[...], width)
    dp_scr[:, :width] = dq_ref[...]
    dp_scr[:, width : 2 * width] = (dk * cos - partner(dk) * sin).astype(BF16)
    dp_scr[:, 2 * width :] = dkv[:, width:].astype(BF16)
    grad_scr[:, : 3 * width] = dot_tn(a_ref[...], dp_scr[...]).astype(BF16)
    grad_scr[:, 3 * width :] = dout_ref[...]
    da_scr[...] = dot_nt(dp_scr[...], w_ref[...].reshape(dim, 3 * width))
    gain = jnp.zeros((1, dim), F32)
    for m in range(n_rep):
        da = da_scr[spot(at_ref[0] ^ m, rows), :]
        refs_da[m][...] = da.astype(BF16)
        hat, _ = hat_of(refs_x[m][...].astype(F32))
        gain = gain + jnp.sum(da * hat, axis=0, keepdims=True)
    per = dim // lanes
    strips = [g[:, k * lanes : (k + 1) * lanes] for g in (gain, gain_two_ref[...]) for k in range(per)]
    strips.append(jnp.zeros((8 - len(strips), lanes), F32))
    gains = jnp.concatenate(strips, axis=0).astype(BF16)
    for l in range(n_part):
        ref = keep_ref if l == 0 else refs_send[l - 1]
        for m in range(n_rep):
            shard = m * n_part + (at_ref[2] ^ l)
            ref[m * high : m * high + w_rows, :] = grad_scr[spot(shard, w_rows), :]
            ref[m * high + w_rows : (m + 1) * high, :] = gains


def part_sum_kernel(keep_ref, refs_got, out_ref):
    total = keep_ref[...].astype(F32)
    for got in refs_got:
        total = total + got[...].astype(F32)
    out_ref[...] = total.astype(BF16)


def grads_kernel(n_rep, at_ref, pieces, qkv_ref, out_ref, gains_ref):
    width = pieces[0].shape[1] // 4
    rows, dim = out_ref.shape
    for m in range(n_rep):
        for p in range(3):
            start = pl.multiple_of(p * dim + (at_ref[0] ^ m) * width, width)
            qkv_ref[:, pl.ds(start, width)] = pieces[m][:rows, p * width : (p + 1) * width].astype(F32)
        start = pl.multiple_of((at_ref[0] ^ m) * width, width)
        out_ref[:, pl.ds(start, width)] = pieces[m][:rows, 3 * width :].astype(F32)
    gains = pieces[0][rows:, :].astype(F32)
    for m in range(1, n_rep):
        gains = gains + pieces[m][rows:, :].astype(F32)
    gains_ref[...] = gains


def ff_out_kernel(n_rep, unit, pitch, cuts, at_ref, pieces, in_ref, down_ref, scr, down_scr):
    lanes = pieces[0].shape[1]
    rows = in_ref.shape[0]
    shard, dim = down_ref.shape
    for (m, top), piece in zip(cuts, pieces, strict=True):
        scr[at_ref[0] ^ m, top : top + piece.shape[0], :] = piece[...]
    _, spots = packed_rows(pitch, dim, lanes)
    strips = []
    for jj in range(n_rep):
        size = min(unit, shard - jj * unit)
        for row, lane, row_in, col_in, n, w in spots:
            down_scr[row_in : row_in + n, col_in : col_in + w] = scr[
                jj, rows + row : rows + row + n, lane : lane + w
            ].astype(F32)
        down_ref[jj * unit : jj * unit + size, :] = down_scr[:size, :]
    for p in range(lanes // pitch):
        strips = []
        for jj in range(n_rep):
            size = min(unit, shard - jj * unit)
            strips.append(scr[jj, :rows, p * pitch : p * pitch + size].astype(F32))
        in_ref[:, p * shard : (p + 1) * shard] = jnp.concatenate(strips, axis=1)


def split_refs(counts, refs):
    out, at = [], 0
    for n in counts:
        if n is None:
            out.append(refs[at])
            at += 1
        else:
            out.append(list(refs[at : at + n]))
            at += n
    return out


def grouped(kernel, static, counts):
    def body(*refs):
        kernel(*static, *split_refs(counts, refs))

    return body


def on_device(
    n_rep, n_inner,
    tokens, cotangent, qkv_weight, out_weight, in_weight, down_weight, gain_one, gain_two,
):
    part = n_inner // n_rep
    rows, dim = tokens.shape
    sub = rows // n_rep
    w_rows = qkv_weight.shape[0]
    width = dim // n_rep
    lanes = 4 * width
    high = w_rows + 8
    ff_shard = down_weight.shape[0]
    unit = -(-ff_shard // n_rep)
    pitch = -(-unit // 16) * 16
    ff = pitch * n_inner
    ff_high = w_rows + pitch * dim // (2 * ff)
    total = n_rep * rows
    j = lax.axis_index("rep")
    i = lax.axis_index("inner")
    s = i // part
    t = i % part
    at = jnp.stack([j, s, t]).astype(jnp.int32)

    def rep_swap(x, m):
        return lax.ppermute(x, "rep", [(a, a ^ m) for a in range(n_rep)])

    def plane_swap(x, m):
        pairs = [(a * part + b, (a ^ m) * part + b) for a in range(n_rep) for b in range(part)]
        return lax.ppermute(x, "inner", pairs)

    def part_swap(x, l):
        pairs = [(a * part + b, a * part + (b ^ l)) for a in range(n_rep) for b in range(part)]
        return lax.ppermute(x, "inner", pairs)

    def rep_gather(x):
        return [x] + [rep_swap(x, m) for m in range(1, n_rep)]

    def rep_spread(x):
        if n_rep != 4:
            return [[piece] for piece in rep_gather(x)]
        half = x.shape[0] // 2
        near = [rep_swap(x, 1), rep_swap(x, 2)]
        return [[x], [near[0]], [near[1]], [rep_swap(near[0][:half], 2), rep_swap(near[1][half:], 1)]]

    def rep_trade(pieces):
        return [pieces[0]] + [rep_swap(pieces[m], m) for m in range(1, n_rep)]

    def plane_trade(pieces):
        return [pieces[0]] + [plane_swap(pieces[m], m) for m in range(1, n_rep)]

    def send_home(pieces):
        got = []
        for k in range(n_rep):
            pairs = []
            for a in range(n_rep):
                for z in range(n_rep):
                    for b in range(part):
                        pairs.append((a * n_inner + z * part + b, z * n_inner + (a ^ k) * part + b))
            got.append(lax.ppermute(pieces[k], ("rep", "inner"), pairs))
        return got

    home = [((2 * sub, dim), BF16)] * n_rep
    planes = [[z * part + b for z in range(n_rep)] for b in range(part)]

    (w_pack,) = call(
        functools.partial(weight_kernel, n_inner, part), [((high, lanes), BF16)],
        [at, qkv_weight, out_weight, jnp.stack([gain_one, gain_two])], n_smem=1, whole=True,
    )
    w_all = lax.all_gather(w_pack, "inner")
    x_first = lax.all_to_all(after(tokens, w_pack), "rep", 0, 0, tiled=True)
    in_late = after(in_weight, x_first)
    x_own = lax.all_to_all(x_first, "inner", 0, 0, axis_index_groups=planes, tiled=True)
    c_first = lax.all_to_all(after(cotangent, x_first), "rep", 0, 0, tiled=True)
    x_own = after(x_own, c_first)
    c_own = lax.all_to_all(after(c_first, x_own), "inner", 0, 0, axis_index_groups=planes, tiled=True)
    xs = rep_gather(x_own)
    (ff_pack,) = call(
        grouped(ff_weight_kernel, (n_rep, unit, pitch), (None,) * 5),
        [((ff_high, 2 * ff), BF16)],
        [at, in_late, down_weight, w_pack],
        [((pitch, dim), BF16)],
        n_smem=1, n_any=1,
    )
    ff_w = lax.all_gather(ff_pack, "inner")

    own = w_all.reshape(n_rep, part, high, lanes)
    own = lax.dynamic_slice_in_dim(own, t, 1, 1)[:, 0, :w_rows, 3 * width :].reshape(n_rep * w_rows, width)
    wo_own = rep_gather(after(own.reshape(n_rep, w_rows, width), xs[-1]))
    wo_other = [part_swap(jnp.stack(wo_own), l) for l in range(1, part)]

    order = jnp.arange(total, dtype=jnp.int32)
    place = ((order // sub % n_rep) * part + t) * rows + (order // rows) * sub + order % sub
    inv_freq = 1.0 / THETA ** (jnp.arange(HEAD_DIM // 2, dtype=F32) * (2.0 / HEAD_DIM))
    angle = place.astype(F32)[:, None] * inv_freq[None, :]
    cos_half, sin_half = jnp.cos(angle), jnp.sin(angle)
    cos = jnp.concatenate([cos_half] * 4, axis=1)
    sin = jnp.concatenate([-sin_half, sin_half] * 2, axis=1)

    q, kv, a_one, w_qkv, gains = call(
        grouped(qkv_kernel, (n_rep,), (None, n_rep) + (None,) * 12),
        [
            ((total, width), BF16), ((total, 2 * width), BF16), ((total, dim), BF16),
            ((n_inner, w_rows, 3 * width), BF16), ((2, dim), F32),
        ],
        [at, *xs, w_all, cos, sin, c_own],
        [((total, dim), BF16), ((n_inner, w_rows, 3 * width), BF16), ((n_inner, 8, lanes), BF16)],
        n_smem=1, n_any=1, far=(1 + n_rep,), far_outs=(2, 3), n_sems=4, whole=True, micros=2,
    )
    kvs = [kv] + [part_swap(kv, l) for l in range(1, part)]
    heads = width // HEAD_DIM
    stat_rows = -(-heads // 8) * 8
    o, lse = call(
        grouped(attend_kernel, (part,), (None, part) + (None,) * 4),
        [((total, width), BF16), ((stat_rows, total), F32)],
        [after(q, *wo_own[1:]), *kvs],
        [((total * part, width), BF16), ((width, total * part), BF16)],
        micros=6,
    )
    os_ = rep_gather(o)
    cs = rep_gather(after(c_own, xs[-1]))
    n_spots = len(packed_rows(pitch, dim, 2 * ff)[1])
    per = width // (part * w_rows)
    ff_out = call(
        grouped(
            ff_kernel, (n_rep, part),
            (None, n_rep, n_rep, n_rep, part - 1, None, n_rep, None, None, n_rep) + (None,) * 16,
        ),
        [((rows, dim), F32)]
        + [((rows, dim), BF16)] * n_rep
        + [
            ((total, dim), BF16), ((total, ff), BF16), ((total, 2 * ff), BF16),
            ((total, dim), BF16), ((per, part, w_rows, dim), BF16), ((1, dim), F32),
        ],
        [at, *xs, *os_, *wo_own, *wo_other, ff_w, *cs, gains],
        [
            ((total, dim), F32), ((total, 2 * ff), F32), ((total, ff), F32), ((n_inner, w_rows, 2 * ff), BF16),
            ((n_inner, pitch, dim), BF16), ((total, dim), BF16), ((total, dim), BF16), ((total, dim), BF16),
            ((n_rep, part, w_rows, dim), BF16),
        ],
        n_smem=1, far=range(1, 1 + 4 * n_rep + part), far_outs=(4 + n_rep, 5 + n_rep),
        n_sems=n_rep * (part + 3) + 1 + n_spots + 1 + per, whole=True, micros=11,
    )
    r_own, da_two = ff_out[0], ff_out[1 : 1 + n_rep]
    a_two, gated, d_hidden, o_all, w_out, gain_two_part = ff_out[1 + n_rep :]
    das = rep_trade(da_two)
    ff_back = call(
        grouped(ff_grads_kernel, (n_rep,), (None, None, None, n_rep, None, None, n_rep) + (None,) * 6),
        [((rows, dim), BF16)] * n_rep + [((n_inner, ff_high, 2 * ff), BF16)],
        [at, gated, ff_w, *cs, a_two, d_hidden],
        [
            ((n_inner, pitch, dim), BF16), ((n_inner, pitch, dim), BF16), ((total, dim), BF16),
            ((n_inner, w_rows, 2 * ff), BF16),
        ],
        n_smem=1, far=range(2, 3 + n_rep), far_outs=(n_rep,), n_sems=n_rep + 2 * n_spots + 1, whole=True, micros=5,
    )
    lo, ff_grad = ff_back[:-1], ff_back[-1]
    dr, dz = call(
        grouped(middle_kernel, (n_rep,), (n_rep,) + (None,) * 5),
        [((rows, dim), F32), ((rows, dim), BF16)],
        [*das, r_own, c_own, gains, lo[0]],
        n_any=1, micros=2,
    )
    ff_grad = lax.psum_scatter(after(ff_grad, das[1]), "inner", scatter_dimension=0)
    dzs = rep_gather(dz)

    back = call(
        grouped(
            attend_back_kernel,
            (n_rep, part),
            (None, n_rep, None, None, None, part, None, None, None, None, None, part - 1, None) + (None,) * 7,
        ),
        [((total, width), BF16), ((total, 2 * width), F32)]
        + [((total, 2 * width), BF16)] * (part - 1)
        + [((total, dim), BF16)],
        [at, *dzs, w_out, o, q, *kvs, lse, cos, sin],
        [
            ((total, width), BF16), ((total * part, width), BF16), ((total * part, width), BF16),
            ((width, total * part), BF16), ((stat_rows, total), F32),
            ((total * part, width), F32), ((total * part, width), F32),
        ],
        n_smem=1, micros=10,
    )
    dq, dkv, sends, dz_all = back[0], back[1], back[2:-1], back[-1]
    los = rep_trade([after(x, dzs[-1]) for x in lo])
    gots = [part_swap(after(x, *los[1:]), l + 1) for l, x in enumerate(sends)]
    (d_out,) = call(
        out_grad_kernel, [((dim, width), BF16)], [at, o_all, dz_all], n_smem=1, micros=2,
    )
    qkv_out = call(
        grouped(
            qkv_back_kernel, (n_rep, part),
            (None, None, None, part - 1, None, None, None, None, n_rep, None, None, None, part - 1, n_rep) + (None,) * 3,
        ),
        [((n_rep * high, lanes), BF16)] * part + [((rows, dim), BF16)] * n_rep,
        [at, dq, dkv, *gots, cos, sin, a_one, w_qkv, *xs, d_out, gain_two_part],
        [((total, 3 * width), BF16), ((total, dim), F32), ((dim, lanes), BF16)],
        n_smem=1, micros=4,
    )
    keep, sends, da_one = qkv_out[0], qkv_out[1:part], qkv_out[part:]
    gots = [part_swap(x, l + 1) for l, x in enumerate(sends)]
    (summed,) = call(
        grouped(part_sum_kernel, (), (None, part - 1, None)), [((n_rep * high, lanes), BF16)], [keep, *gots]
    )
    das = rep_trade(da_one)
    d_pack = lax.psum_scatter(
        after(summed, ff_grad), "inner", scatter_dimension=0, axis_index_groups=planes, tiled=True
    )
    parts = call(
        grouped(last_kernel, (n_rep,), (None, n_rep, n_rep, None, None, None, None, n_rep, None)),
        home, [at, *das, *los, xs[0], dr, r_own, gains], [((rows, dim), F32)], n_smem=1, whole=True, micros=2,
    )
    ff_grads = rep_spread(after(ff_grad, *das[1:]))
    back_home = send_home(parts)
    quarter = after(d_pack, back_home[1])
    input_grad, layer_out = call(
        grouped(place_kernel, (n_rep,), (None, n_rep, None, None)),
        [((rows, dim), BF16)] * 2, [at, *back_home, d_pack], n_smem=1, n_any=1,
    )
    g_qkv, g_out, g_gains = call(
        grouped(grads_kernel, (n_rep,), (None, n_rep, None, None, None)),
        [((w_rows, 3 * dim), F32), ((w_rows, dim), F32), ((8, lanes), F32)],
        [at, *rep_gather(quarter)],
        n_smem=1, micros=2,
    )
    cuts, flat = [], []
    for m, pieces in enumerate(ff_grads):
        top = 0
        for piece in pieces:
            cuts.append((m, top))
            flat.append(piece)
            top += piece.shape[0]
    g_in, g_down = call(
        grouped(ff_out_kernel, (n_rep, unit, pitch, cuts), (None, len(flat)) + (None,) * 4),
        [((w_rows, 2 * n_inner * ff_shard), F32), ((ff_shard, dim), F32)],
        [at, *flat, d_pack],
        [((n_rep, ff_high, 2 * ff), BF16), ((pitch, dim), F32)],
        n_smem=1, n_any=1, micros=4,
    )
    gain_grads = g_gains[: 2 * dim // lanes].reshape(2, dim)
    gain_grads = lax.dynamic_slice_in_dim(gain_grads, i * w_rows, w_rows, 1)
    return (layer_out, input_grad, g_qkv, g_out, g_in, g_down, gain_grads[0], gain_grads[1])


def solution(mesh):
    rows = P(("rep", "inner"), None)
    weight = P("inner", None)
    return jax.shard_map(
        functools.partial(on_device, mesh.shape["rep"], mesh.shape["inner"]),
        mesh=mesh,
        in_specs=(rows, rows, weight, weight, weight, weight, P("inner"), P("inner")),
        out_specs=(rows, rows, weight, weight, weight, weight, P("inner"), P("inner")),
        check_vma=False,
    )
```
